32 devices in a mesh: shard: 2 (over y), context: 4 (over z), tensor: 4 (over x, core).
Axes of the slice: x: 2, y: 2, z: 4, core: 2. Of those that a mesh axis runs over, the one named last changes fastest.
Arguments:
- hidden_in: bfloat16 [8192, 1024], P(('shard', 'context')), may hold values from -6 to 6
- segment_ids: int32 [2, 4096], P('shard', 'context'), may hold values from 0 to 15, never falling along the last dimension, each value on 1 to 2048 neighbouring positions
- cotangent: bfloat16 [8192, 1024], P(('shard', 'context')), may hold values from -6 to 6
- qkv_weight: bfloat16 [2, 1024, 3, 1024], P(None, 'shard', None, 'tensor'), may hold values from -0.1875 to 0.1875
- merge_weight: bfloat16 [2, 1024, 1024], P(None, 'tensor', 'shard'), may hold values from -0.75 to 0.75
- up_weight: bfloat16 [2, 1024, 4096], P(None, 'shard', 'tensor'), may hold values from -0.1875 to 0.1875
- down_weight: bfloat16 [2, 4096, 1024], P(None, 'tensor', 'shard'), may hold values from -0.1875 to 0.1875
- row_gains: bfloat16 [2, 2, 1024], P(None, None, 'shard'), may hold values from 0.5 to 1.5
- row_bias: bfloat16 [2, 4, 1024], P(None, None, 'shard'), may hold values from -4 to 4
- head_bias: bfloat16 [2, 2, 1024], P(None, None, 'tensor'), may hold values from -4 to 4
- up_bias: bfloat16 [2, 4096], P(None, 'tensor'), may hold values from -6 to 6
Outputs:
- hidden_out: bfloat16 [8192, 1024], P(('shard', 'context'))
- input_grad: float32 [8192, 1024], P(('shard', 'context'))
- grad_qkv: float32 [2, 1024, 3, 1024], P(None, 'shard', None, 'tensor')
- grad_merge: float32 [2, 1024, 1024], P(None, 'tensor', 'shard')
- grad_up: float32 [2, 1024, 4096], P(None, 'shard', 'tensor')
- grad_down: float32 [2, 4096, 1024], P(None, 'tensor', 'shard')
- grad_gains: float32 [2, 2, 1024], P(None, None, 'shard')
- grad_shifts: float32 [2, 4, 1024], P(None, None, 'shard')
- grad_heads: float32 [2, 2, 1024], P(None, None, 'tensor')
- grad_hidden: float32 [2, 4096], P(None, 'tensor')
The draws below stay inside these ranges and needn't reach their ends.
Inputs may be any that keep to these rules, and one draw needn't show every extreme that they name: `segment_ids`: in each sequence the document numbers never fall and take every value of 0 to 15; each document has 1 to 2048 tokens, and one has exactly 2048.
All inputs are finite; a program needn't handle non-finite values.
Results may differ from the reference program's by a relative error of at most 0.035.
Values may be sent and summed in bfloat16 or wider, within the bound.
No kernel may reach another device: no remote copies, remote signals or barrier semaphores. Data moves between devices by JAX's collectives and lax.ppermute only.
A program may use at most 320 MiB of HBM per device.

```python
import math
import jax
import jax.numpy as jnp
import numpy as np
from jax import lax

D = 1024
HEADS = 16
HEAD_DIM = 64
FF = 4096
LAYERS = 2
SEQ = 4096
DOCS = 16
DOC_MOST = 2048
SEQS = 2
TOKENS = 8192


def level_of(key, dims, shards, smallest, top_value):
    factor_of = 1.0
    for dim, shards_of in shards:
        heights = jax.random.uniform(jax.random.fold_in(jax.random.fold_in(key, 6), dim), (shards_of,), jnp.float32, smallest / len(shards), top_value / len(shards))
        factor_of = factor_of * jnp.repeat(jnp.exp(heights), dims[dim] // shards_of).reshape((-1,) + (1,) * (len(dims) - 1 - dim))
    return factor_of


def profile(number_of, total, reach, lean):
    weights = [(1 << 20) // math.isqrt(rank ** lean) + 1 for rank in range(2, number_of + 1)]
    spare, counts = total - reach - (number_of - 1), [1] * (number_of - 1)
    while spare > 0:
        movable = [i for i in range(number_of - 1) if counts[i] < reach]
        pool, budget = sum([weights[i] for i in movable]), spare
        for i in movable:
            more = min(reach - counts[i], max(1, budget * weights[i] // pool), spare)
            counts[i] = counts[i] + more
            spare = spare - more
    return np.array([reach] + counts)


def uneven(stream_key, number_of, total, reach, slope):
    if number_of == 2:
        one = jax.random.randint(stream_key, (), max(1, total - reach), min(reach, total - 1) + 1)
        return jnp.stack([one, total - one])
    tallies = jnp.asarray(profile(number_of, total, reach, slope), jnp.int32)
    twos = (number_of - 1) // 2
    giver, sink = tallies[1:1 + 2 * twos:2], tallies[2:2 + 2 * twos:2]
    room = jnp.minimum(giver - 1, reach - sink)
    passed = jax.random.randint(jax.random.fold_in(stream_key, 1), (twos,), 0, 1 << 20) % (room + 1)
    tallies = tallies.at[1:1 + 2 * twos:2].set(giver - passed).at[2:2 + 2 * twos:2].set(sink + passed)
    return tallies[jax.random.permutation(jax.random.fold_in(stream_key, 2), number_of)]


def centred(rng, dims, width, most, shards=(), held_as=jnp.bfloat16):
    array = jax.random.normal(rng, dims, jnp.float32) * width
    if len(shards) > 0:
        array = level_of(rng, dims, shards, -0.22, 0.18) * array
    return jnp.clip(array, min=-most, max=most).astype(held_as)


def setup_inputs(seed: int = 0) -> dict:
    arg_keys = jax.random.split(jax.random.key(seed), 12)
    return {
        "hidden_in": centred(arg_keys[0], (TOKENS, D), 1.0, 6.0, ((0, 8),)),
        "segment_ids": jax.vmap(lambda own: jnp.searchsorted(jnp.cumsum(uneven(own, DOCS, SEQ, DOC_MOST, 2)), jnp.arange(SEQ), side="right"))(jax.random.split(arg_keys[1], SEQS)).reshape((SEQS, SEQ)).astype(jnp.int32),
        "cotangent": centred(arg_keys[2], (TOKENS, D), 1.0, 6.0, ((0, 8),)),
        "qkv_weight": centred(arg_keys[3], (LAYERS, D, 3, D), D ** -0.5, 0.1875, ((1, 2), (3, 4))),
        "merge_weight": centred(arg_keys[4], (LAYERS, D, D), (D // 16) ** -0.5, 0.75, ((1, 4), (2, 2))),
        "up_weight": centred(arg_keys[5], (LAYERS, D, FF), D ** -0.5, 0.1875, ((1, 2), (2, 4))),
        "down_weight": centred(arg_keys[6], (LAYERS, FF, D), (FF // 4) ** -0.5, 0.1875, ((1, 4), (2, 2))),
        "row_gains": jnp.clip(1.0 + 0.1 * jax.random.normal(arg_keys[7], (LAYERS, 2, D), jnp.float32), 0.5, 1.5).astype(jnp.bfloat16),
        "row_bias": centred(arg_keys[8], (LAYERS, 4, D), 0.3, 4.0, ((2, 2),)),
        "head_bias": centred(arg_keys[9], (LAYERS, 2, D), 0.3, 4.0, ((2, 4),)),
        "up_bias": centred(arg_keys[10], (LAYERS, FF), 0.5, 6.0, ((1, 4),)),
    }


@jax.custom_vjp
def low(v):
    return lax.optimization_barrier(v.astype(jnp.bfloat16)).astype(jnp.float32)

@jax.custom_vjp
def low_back(v):
    return v

def low_keep(v):
    return (low(v), None)

def low_pass(kept, grad):
    return (grad,)

def back_keep(v):
    return (v, None)

def back_low(kept, grad):
    return (low(grad),)
low.defvjp(low_keep, low_pass)
low_back.defvjp(back_keep, back_low)

def layer_norm(value, gain, shift):
    center = value - lax.optimization_barrier(jnp.mean(value, axis=-1, keepdims=True))
    spread = lax.optimization_barrier(jnp.mean(center * center, axis=-1, keepdims=True))
    return center * lax.rsqrt(spread + 1e-05) * gain + shift

def attention(query, key, value, segment_ids):
    highest = lax.Precision.HIGHEST
    shape = (segment_ids.shape[0], segment_ids.shape[1], HEADS, HEAD_DIM)
    queries = query.reshape(shape)
    keys = key.reshape(shape)
    values = value.reshape(shape)

    def one_sequence(args):
        seq_query, seq_key, seq_value, seq_ids = args
        block = min(512, seq_query.shape[0])
        count = seq_query.shape[0] // block

        def one_block(block_args):
            block_query, block_ids = block_args
            scores = low_back(jnp.einsum('qhd,khd->hqk', block_query, seq_key, precision=highest))
            same = block_ids[:, None] == seq_ids[None, :]
            scores = jnp.where(same[None], scores, -1e+30)
            probs = low(jax.nn.softmax(scores, axis=-1))
            return jnp.einsum('hqk,khd->qhd', probs, seq_value, precision=highest)
        out = lax.map(jax.checkpoint(one_block), (seq_query.reshape(count, block, HEADS, HEAD_DIM), seq_ids.reshape(count, block)))
        return out.reshape(seq_query.shape)
    result = lax.map(one_sequence, (queries, keys, values, segment_ids))
    return result.reshape(query.shape)

def encoder_layer(x, w_qkv, w_merge, w_up, w_down, gains, biases, bias_heads, bias_up, segment_ids):
    highest = lax.Precision.HIGHEST
    scale = HEAD_DIM ** (-0.5)
    x_low = low(x)
    projected = jnp.einsum('td,dcj->tcj', x_low, w_qkv, precision=highest)
    query = low_back(low((projected[:, 0] + bias_heads[0]) * scale))
    key = low_back(low(projected[:, 1]))
    value = low_back(low(projected[:, 2] + bias_heads[1]))
    context = low_back(low(attention(query, key, value, segment_ids)))
    branch = low_back(jnp.dot(context, w_merge, precision=highest))
    mixed = x + branch + biases[0]
    normed = layer_norm(mixed, gains[0], biases[1])
    normed_low = low(normed)
    pre = low_back(jnp.dot(normed_low, w_up, precision=highest) + bias_up)
    act = low(jax.nn.gelu(pre, approximate=False))
    down = low_back(jnp.dot(act, w_down, precision=highest))
    summed = normed + down + biases[2]
    return layer_norm(summed, gains[1], biases[3])

def reference(hidden_in, segment_ids, cotangent, qkv_weight, merge_weight, up_weight, down_weight, row_gains, row_bias, head_bias, up_bias):
    params = (qkv_weight.astype(jnp.float32), merge_weight.astype(jnp.float32), up_weight.astype(jnp.float32), down_weight.astype(jnp.float32), row_gains.astype(jnp.float32), row_bias.astype(jnp.float32), head_bias.astype(jnp.float32), up_bias.astype(jnp.float32))

    def forward(x, weights):
        for layer in range(LAYERS):
            x = encoder_layer(x, weights[0][layer], weights[1][layer], weights[2][layer], weights[3][layer], weights[4][layer], weights[5][layer], weights[6][layer], weights[7][layer], segment_ids)
        return x
    output, backward = jax.vjp(forward, hidden_in.astype(jnp.float32), params)
    d_input, d_params = backward(cotangent.astype(jnp.float32))
    return (output.astype(jnp.bfloat16), d_input, d_params[0], d_params[1], d_params[2], d_params[3], d_params[4], d_params[5], d_params[6], d_params[7])
```

```python
import functools
import math

import jax
import jax.numpy as jnp
from jax import lax
from jax.experimental import pallas as pl
from jax.experimental.pallas import tpu as pltpu
from jax.sharding import PartitionSpec as P

HEAD_DIM = 64
DOCS = 16
NEG = -1e30
EPSILON = 1e-05
CALM = 75.0
FAR = 1 << 24
F32 = jnp.float32
BF16 = jnp.bfloat16
SHARD = "shard"
CONTEXT = "context"
VMEM = pl.BlockSpec(memory_space=pltpu.VMEM)


def dot(a, b, ca, cb):
    return lax.dot_general(a, b, (((ca,), (cb,)), ((), ())), preferred_element_type=F32)


def params(mib=56):
    return pltpu.CompilerParams(vmem_limit_bytes=mib << 20)


def cost(flops, nbytes, trans=0):
    return pl.CostEstimate(flops=1, bytes_accessed=1, transcendentals=0)


def qkv_kernel(perm, cols, *refs, n_x, n_w):
    xs, bias_ref = refs[:n_x], refs[n_x]
    w_refs = refs[n_x + 1 : n_x + 1 + n_w]
    out_ref = refs[n_x + 1 + n_w]
    x_ref = xs[0]
    if n_x > 1:
        x_ref = refs[n_x + 2 + n_w]
        for i in range(n_x):

            @pl.when(pl.program_id(0) == i)
            def _():
                x_ref[...] = xs[i][...]

    scale = HEAD_DIM ** (-0.5)
    width = w_refs[0].shape[-1]
    for c in range(3):
        acc = None
        k = 0
        for w_ref in w_refs:
            deep = w_ref.shape[2]
            for i in range(w_ref.shape[0]):
                off = pl.multiple_of(cols[k] * deep, 128)
                part = dot(x_ref[:, pl.ds(off, deep)], w_ref[i, c], 1, 0)
                acc = part if acc is None else acc + part
                k += 1
        if c == 0:
            acc = (acc + bias_ref[0:1, :].astype(F32)) * scale
        if c == 2:
            acc = acc + bias_ref[1:2, :].astype(F32)
        turned = acc.T.astype(BF16)
        for h in range(width // HEAD_DIM):
            out_ref[h, c] = turned[h * HEAD_DIM : (h + 1) * HEAD_DIM]


def project(xs, weights, cols, bias, perm, piece):
    width = xs[0].shape[1]
    rows = sum(x.shape[0] for x in xs)
    hw = weights[0].shape[-1]
    heads = hw // HEAD_DIM
    out_shape = [jax.ShapeDtypeStruct((heads, 3, HEAD_DIM, rows), BF16)]
    out_specs = [pl.BlockSpec((heads, 3, HEAD_DIM, piece), lambda r, p, c: (0, 0, 0, p[r]))]
    x_specs = [pl.BlockSpec((piece, width), lambda r, p, c: (r, 0))]
    if len(xs) > 1:
        x_specs = [pl.BlockSpec((piece, width), lambda r, p, c: (0, 0))] * len(xs)
        out_shape.append(jax.ShapeDtypeStruct((rows, width), BF16))
        out_specs.append(pl.BlockSpec((piece, width), lambda r, p, c: (p[r], 0)))
    return pl.pallas_call(
        functools.partial(qkv_kernel, n_x=len(xs), n_w=len(weights)),
        grid_spec=pltpu.PrefetchScalarGridSpec(
            num_scalar_prefetch=2,
            grid=(rows // piece,),
            in_specs=x_specs
            + [pl.BlockSpec(bias.shape, lambda r, p, c: (0, 0))]
            + [pl.BlockSpec(w.shape, lambda r, p, c: (0, 0, 0, 0)) for w in weights],
            out_specs=out_specs,
        ),
        out_shape=out_shape,
        compiler_params=params(),
        cost_estimate=cost(2 * rows * width * 3 * hw, 2 * rows * width * 2 + 6 * width * hw),
        name="project",
    )(perm, cols, *xs, bias, *weights)


def back_kernel(perm, cols, *refs, n_w):
    d_ref = refs[0]
    w_refs = refs[1 : 1 + n_w]
    out_refs = refs[1 + n_w : -2]
    proj_ref, sum_ref = refs[-2:]
    heads = d_ref.shape[0]
    r = pl.program_id(0)
    first = r == 0

    @pl.when(first)
    def _():
        sum_ref[...] = jnp.zeros_like(sum_ref)

    parts = []
    for c in range(3):
        flat = jnp.concatenate([d_ref[h, c] for h in range(heads)], axis=0)
        turned = flat.astype(F32).T
        if c != 1:
            row = c // 2
            sum_ref[row : row + 1, :] += jnp.sum(turned, axis=0, keepdims=True)
        turned = turned.astype(BF16)
        proj_ref[c] = turned
        parts.append(turned)
    k = 0
    for w_ref in w_refs:
        deep = w_ref.shape[2]
        for i in range(w_ref.shape[0]):
            acc = dot(parts[0], w_ref[i, 0], 1, 1)
            acc = acc + dot(parts[1], w_ref[i, 1], 1, 1)
            acc = acc + dot(parts[2], w_ref[i, 2], 1, 1)
            off = pl.multiple_of(cols[k] * deep, 128)
            low = acc.astype(BF16)
            for n, out_ref in enumerate(out_refs):

                @pl.when(r == n)
                def _():
                    out_ref[:, pl.ds(off, deep)] = low

            k += 1


def project_back(d_heads, weights, cols, perm, piece, width):
    heads, _, _, rows = d_heads.shape
    blocks = rows // piece
    hw = heads * HEAD_DIM
    return pl.pallas_call(
        functools.partial(back_kernel, n_w=len(weights)),
        grid_spec=pltpu.PrefetchScalarGridSpec(
            num_scalar_prefetch=2,
            grid=(blocks,),
            in_specs=[pl.BlockSpec((heads, 3, HEAD_DIM, piece), lambda r, p, c: (0, 0, 0, p[r]))]
            + [pl.BlockSpec(w.shape, lambda r, p, c: (0, 0, 0, 0)) for w in weights],
            out_specs=[pl.BlockSpec((piece, width), lambda r, p, c: (0, 0))] * blocks
            + [
                pl.BlockSpec((3, piece, hw), lambda r, p, c: (0, p[r], 0)),
                pl.BlockSpec((2, hw), lambda r, p, c: (0, 0)),
            ],
        ),
        out_shape=[jax.ShapeDtypeStruct((piece, width), BF16)] * blocks
        + [
            jax.ShapeDtypeStruct((3, rows, hw), BF16),
            jax.ShapeDtypeStruct((2, hw), F32),
        ],
        compiler_params=params(),
        cost_estimate=cost(2 * rows * width * 3 * hw, 2 * rows * width * 2 + 6 * width * hw),
        name="project_back",
    )(perm, cols, d_heads, *weights)


def tile_kernel_index(tiles, t, size, bq, bk, chunk):
    q0 = pl.multiple_of(tiles[1 + t] * bq, bq)
    k0 = pl.multiple_of(tiles[1 + size + t] * bk, bk)
    cj, kj = q0 // chunk, k0 // chunk
    off = pl.multiple_of(q0 - cj * chunk, bq)
    ko = pl.multiple_of(k0 - kj * chunk, bk)
    return q0, k0, cj, off, kj, ko, tiles[1 + 2 * size + t]


def inside(spot, pos, start, length):
    place = (spot + (pos - start)).astype(jnp.uint32)
    return place < length.astype(jnp.uint32)


def attend_kernel(
    tiles,
    qkv,
    start,
    length,
    low,
    high,
    lse,
    keys,
    acc,
    total,
    top,
    *,
    bq,
    bk,
    seq,
    chunk,
    piece,
    unroll,
    size,
):
    n_chunks = seq // chunk
    q_most = jnp.zeros((1, chunk), F32)
    k_most = jnp.zeros((1, chunk), F32)
    for j in range(n_chunks):
        q = qkv[j, 0].astype(F32)
        k = qkv[j, 1].astype(F32)
        q_most = jnp.maximum(q_most, jnp.sum(q * q, axis=0, keepdims=True))
        k_most = jnp.maximum(k_most, jnp.sum(k * k, axis=0, keepdims=True))
        keys[j * chunk : (j + 1) * chunk, :] = k.T.astype(BF16)
    calm = jnp.max(q_most) * jnp.max(k_most) < CALM * CALM
    acc[...] = jnp.zeros_like(acc)
    total[...] = jnp.zeros_like(total)
    spot = lax.broadcasted_iota(jnp.int32, (bk, bq), 0)

    def tile(t):
        q0, k0, cj, off, kj, ko, pos = tile_kernel_index(tiles, t, size, bq, bk, chunk)
        s = dot(keys[pl.ds(k0, bk), :], qkv[cj, 0, :, pl.ds(off, bq)], 1, 0)
        ok = inside(spot, pos, start[:, pl.ds(q0, bq)], length[:, pl.ds(q0, bq)])
        return q0, kj, ko, s, ok

    @pl.when(calm)
    def _():
        top[...] = jnp.zeros_like(top)

        def step(i, _):
            group = [tile(i * unroll + u) for u in range(unroll)]
            for q0, kj, ko, s, ok in group:
                p = jnp.where(ok, jnp.exp(s), 0.0)
                total[:, pl.ds(q0, bq)] += jnp.sum(p, axis=0, keepdims=True)
                value = qkv[kj, 2, :, pl.ds(ko, bk)]
                acc[:, pl.ds(q0, bq)] += dot(value, p.astype(BF16), 1, 0)
            return 0

        lax.fori_loop(0, tiles[0], step, 0)

    @pl.when(jnp.logical_not(calm))
    def _():
        top[...] = jnp.full_like(top, NEG)

        def step(i, _):
            q0, kj, ko, s, ok = tile(i)
            s = jnp.where(ok, s, NEG)
            here = pl.ds(q0, bq)
            new = jnp.maximum(top[:, here], jnp.max(s, axis=0, keepdims=True))
            p = jnp.where(ok, jnp.exp(s - new), 0.0)
            fade = jnp.exp(top[:, here] - new)
            total[:, here] = total[:, here] * fade + jnp.sum(p, axis=0, keepdims=True)
            value = qkv[kj, 2, :, pl.ds(ko, bk)]
            acc[:, here] = acc[:, here] * fade + dot(value, p.astype(BF16), 1, 0)
            top[:, here] = new
            return 0

        lax.fori_loop(0, tiles[0] * unroll, step, 0)

    lse[...] = top[...] + jnp.log(total[...])
    for z in range(n_chunks):
        for t in range(chunk // piece):
            base = z * chunk + t * piece
            out = acc[:, base : base + piece] / total[:, base : base + piece]
            low[t * n_chunks + z] = out.astype(BF16)
            high[t * n_chunks + z] = out


def attend(qkv, doc, tiles, piece, bq, bk, unroll):
    n_chunks, _, hd, chunk = qkv.shape
    seq = n_chunks * chunk
    start, end = doc
    pieces = seq // piece
    return pl.pallas_call(
        functools.partial(
            attend_kernel,
            bq=bq,
            bk=bk,
            seq=seq,
            chunk=chunk,
            piece=piece,
            unroll=unroll,
            size=(tiles.shape[0] - 1) // 3,
        ),
        grid_spec=pltpu.PrefetchScalarGridSpec(
            num_scalar_prefetch=1,
            grid=(),
            in_specs=[VMEM] * 3,
            out_specs=[VMEM] * 3,
            scratch_shapes=[
                pltpu.VMEM((seq, hd), BF16),
                pltpu.VMEM((hd, seq), F32),
                pltpu.VMEM((1, seq), F32),
                pltpu.VMEM((1, seq), F32),
            ],
        ),
        out_shape=[
            jax.ShapeDtypeStruct((pieces, hd, piece), BF16),
            jax.ShapeDtypeStruct((pieces, hd, piece), F32),
            jax.ShapeDtypeStruct((1, seq), F32),
        ],
        compiler_params=params(40),
        cost_estimate=cost(2 * seq * seq * hd, 8 * seq * hd, seq * seq // 4),
        name="attend",
    )(tiles, qkv, start[None], (end - start)[None])


def attend_back_kernel(
    tiles,
    qkv,
    start,
    length,
    lse,
    ctx,
    d_ctx,
    out,
    keys,
    values,
    queries,
    grads,
    d_keys,
    d_values,
    d_queries,
    delta,
    d_turned,
    *,
    bq,
    bk,
    seq,
    chunk,
    piece,
    unroll,
    size,
):
    n_chunks = seq // chunk
    for j in range(n_chunks):
        sl = slice(j * chunk, (j + 1) * chunk)
        queries[sl, :] = qkv[j, 0].astype(F32).T.astype(BF16)
        keys[sl, :] = qkv[j, 1].astype(F32).T.astype(BF16)
        values[sl, :] = qkv[j, 2].astype(F32).T.astype(BF16)
    for at in range(seq // piece):
        t, z = at // n_chunks, at % n_chunks
        base = z * chunk + t * piece
        part = d_ctx[at].astype(F32)
        d_turned[:, base : base + piece] = d_ctx[at]
        grads[base : base + piece, :] = part.T.astype(BF16)
        delta[:, base : base + piece] = jnp.sum(part * ctx[at], axis=0, keepdims=True)
    d_queries[...] = jnp.zeros_like(d_queries)
    d_keys[...] = jnp.zeros_like(d_keys)
    d_values[...] = jnp.zeros_like(d_values)
    spot = lax.broadcasted_iota(jnp.int32, (bk, bq), 0)

    def tile(t):
        q0, k0, cj, off, kj, ko, pos = tile_kernel_index(tiles, t, size, bq, bk, chunk)
        s = dot(keys[pl.ds(k0, bk), :], qkv[cj, 0, :, pl.ds(off, bq)], 1, 0)
        dp = dot(values[pl.ds(k0, bk), :], d_turned[:, pl.ds(q0, bq)], 1, 0)
        ok = inside(spot, pos, start[:, pl.ds(q0, bq)], length[:, pl.ds(q0, bq)])
        return q0, k0, kj, ko, s, dp, ok

    def step(i, _):
        group = [tile(i * unroll + u) for u in range(unroll)]
        for q0, k0, kj, ko, s, dp, ok in group:
            here = pl.ds(q0, bq)
            there = pl.ds(k0, bk)
            p = jnp.where(ok, jnp.exp(s - lse[:, here]), 0.0)
            ds = (p * (dp - delta[:, here])).astype(BF16)
            d_values[there, :] += dot(p.astype(BF16), grads[here, :], 1, 0)
            d_keys[there, :] += dot(ds, queries[here, :], 1, 0)
            d_queries[:, here] += dot(qkv[kj, 1, :, pl.ds(ko, bk)], ds, 1, 0)
        return 0

    lax.fori_loop(0, tiles[0], step, 0)
    scale = HEAD_DIM ** (-0.5)
    for j in range(n_chunks):
        sl = slice(j * chunk, (j + 1) * chunk)
        out[j, 0] = (d_queries[:, sl].astype(BF16).astype(F32) * scale).astype(BF16)
        out[j, 1] = d_keys[sl, :].T.astype(BF16)
        out[j, 2] = d_values[sl, :].T.astype(BF16)


def attend_back(qkv, doc, tiles, lse, ctx, d_ctx, piece, bq, bk, unroll):
    n_chunks, _, hd, chunk = qkv.shape
    seq = n_chunks * chunk
    start, end = doc
    return pl.pallas_call(
        functools.partial(
            attend_back_kernel,
            bq=bq,
            bk=bk,
            seq=seq,
            chunk=chunk,
            piece=piece,
            unroll=unroll,
            size=(tiles.shape[0] - 1) // 3,
        ),
        grid_spec=pltpu.PrefetchScalarGridSpec(
            num_scalar_prefetch=1,
            grid=(),
            in_specs=[VMEM] * 6,
            out_specs=VMEM,
            scratch_shapes=[pltpu.VMEM((seq, hd), BF16)] * 4
            + [pltpu.VMEM((seq, hd), F32)] * 2
            + [
                pltpu.VMEM((hd, seq), F32),
                pltpu.VMEM((1, seq), F32),
                pltpu.VMEM((hd, seq), BF16),
            ],
        ),
        out_shape=jax.ShapeDtypeStruct((n_chunks, 3, hd, chunk), BF16),
        compiler_params=params(48),
        cost_estimate=cost(4 * seq * seq * hd, 16 * seq * hd, seq * seq // 4),
        name="attend_back",
    )(tiles, qkv, start[None], (end - start)[None], lse, ctx, d_ctx)


def document_bounds(seg):
    ids = jnp.arange(DOCS, dtype=jnp.int32)[:, None]
    below = jnp.sum((seg[None] < ids).astype(jnp.int32), axis=1, keepdims=True)
    upto = jnp.sum((seg[None] <= ids).astype(jnp.int32), axis=1, keepdims=True)
    mine = seg[None] == ids
    start = jnp.sum(jnp.where(mine, below, 0), axis=0)
    end = jnp.sum(jnp.where(mine, upto, 0), axis=0)
    return start, end


def tile_list(start, end, bq, bk, unroll):
    n, m = start.shape[0] // bq, start.shape[0] // bk
    low = start.reshape(n, bq)[:, 0] // bk
    high = (end.reshape(n, bq)[:, -1] + bk - 1) // bk
    count = high - low
    order = jnp.arange(n)
    upto = jnp.sum(jnp.where(order[:, None] <= order[None], count[:, None], 0), axis=0)
    total = upto[-1]
    t = jnp.arange(n * m + unroll, dtype=jnp.int32)
    mine = jnp.minimum(jnp.sum((t[:, None] >= upto[None]).astype(jnp.int32), axis=1), n - 1)
    base = jnp.sum(jnp.where(mine[:, None] == order[None], (high - upto)[None], 0), axis=1)
    real = t < total
    key = jnp.where(real, base + t, 0)
    pos = jnp.where(real, key * bk, FAR)
    steps = (total + unroll - 1) // unroll
    return jnp.concatenate([steps[None], mine, key, pos]).astype(jnp.int32)


def norm_stats(value):
    center = value - jnp.mean(value, axis=-1, keepdims=True)
    rstd = lax.rsqrt(jnp.mean(center * center, axis=-1, keepdims=True) + EPSILON)
    return center * rstd, rstd


def norm_back(xhat, rstd, d_out, gain):
    scaled = d_out * gain
    m1 = jnp.mean(scaled, axis=-1, keepdims=True)
    m2 = jnp.mean(scaled * xhat, axis=-1, keepdims=True)
    return (scaled - m1 - xhat * m2) * rstd


def column(value):
    return jnp.sum(value, axis=0, keepdims=True)


def merge_kernel(perm, cols, ctx, x, vec, *refs):
    ws = refs[:-3]
    mixed_ref, normed_ref, low_ref = refs[-3:]
    halves, deep, wide = ws[0].shape
    parts = []
    for r in range(len(ws)):
        rows = pl.ds(pl.multiple_of(perm[r] * deep, deep), deep)
        parts.append(ctx[rows, :].astype(F32).T.astype(BF16))
    for s in range(halves):
        acc = dot(parts[0], ws[0][s], 1, 0)
        for r in range(1, len(ws)):
            acc = acc + dot(parts[r], ws[r][s], 1, 0)
        sl = pl.ds(pl.multiple_of(cols[s] * wide, 128), wide)
        mixed_ref[:, sl] = x[:, sl] + acc + vec[2:3, sl]
    xhat, _ = norm_stats(mixed_ref[...])
    normed = xhat * vec[0:1, :] + vec[3:4, :]
    normed_ref[...] = normed
    low_ref[...] = normed.astype(BF16)


def merge_specs(ws, layer):
    shape = ws[0].shape
    spec = pl.BlockSpec((shape[0], None) + shape[2:], lambda *_: (0, layer, 0, 0))
    return [spec] * len(ws)


def merge_norm(ctx, ws, layer, x, vec, perm, cols):
    rows, width = x.shape
    big = jax.ShapeDtypeStruct((rows, width), F32)
    return pl.pallas_call(
        merge_kernel,
        grid_spec=pltpu.PrefetchScalarGridSpec(
            num_scalar_prefetch=2,
            grid=(1,),
            in_specs=[VMEM] * 3 + merge_specs(ws, layer),
            out_specs=[VMEM] * 3,
        ),
        out_shape=[big, big, jax.ShapeDtypeStruct((rows, width), BF16)],
        compiler_params=params(),
        cost_estimate=cost(2 * rows * width * width, 2 * width * width + 16 * rows * width),
        name="merge_norm",
    )(perm, cols, ctx, x, vec, *ws)


def add_up(refs):
    total = refs[0][...].astype(F32)
    for ref in refs[1:]:
        total = total + ref[...].astype(F32)
    return total


def norm_kernel(vec, *refs, n_in):
    summed_ref, out_ref, low_ref = refs[n_in:]
    summed = add_up(refs[:n_in]) + vec[4:5, :]
    summed_ref[...] = summed
    xhat, _ = norm_stats(summed)
    out = xhat * vec[1:2, :] + vec[5:6, :]
    out_ref[...] = out
    low_ref[...] = out.astype(BF16)


def second_norm(vec, terms):
    shape = terms[0].shape
    big = jax.ShapeDtypeStruct(shape, F32)
    return pl.pallas_call(
        functools.partial(norm_kernel, n_in=len(terms)),
        in_specs=[VMEM] * (1 + len(terms)),
        out_specs=[VMEM] * 3,
        out_shape=[big, big, jax.ShapeDtypeStruct(shape, BF16)],
        compiler_params=params(),
        cost_estimate=cost(20 * shape[0] * shape[1], 20 * shape[0] * shape[1]),
        name="second_norm",
    )(vec, *terms)


def second_back_math(vec, summed, d_out, d_ref, low_ref, sum_ref):
    xhat, rstd = norm_stats(summed)
    d_summed = norm_back(xhat, rstd, d_out, vec[1:2, :])
    d_ref[...] = d_summed
    low_ref[...] = d_summed.astype(BF16)
    sum_ref[0:1, :] = column(d_out * xhat)
    sum_ref[1:2, :] = column(d_out)
    sum_ref[2:3, :] = column(d_summed)
    return xhat


def last_kernel(vec, d_out_ref, *refs, n_in):
    out_ref, d_ref, low_ref, sum_ref = refs[n_in:]
    summed = add_up(refs[:n_in]) + vec[4:5, :]
    d_out = d_out_ref[...].astype(F32)
    xhat = second_back_math(vec, summed, d_out, d_ref, low_ref, sum_ref)
    out_ref[...] = (xhat * vec[1:2, :] + vec[5:6, :]).astype(BF16)


def last_norm(vec, d_out, terms):
    rows, width = terms[0].shape
    low = jax.ShapeDtypeStruct((rows, width), BF16)
    return pl.pallas_call(
        functools.partial(last_kernel, n_in=len(terms)),
        in_specs=[VMEM] * (2 + len(terms)),
        out_specs=[VMEM] * 4,
        out_shape=[
            low,
            jax.ShapeDtypeStruct((rows, width), F32),
            low,
            jax.ShapeDtypeStruct((3, width), F32),
        ],
        compiler_params=params(),
        cost_estimate=cost(40 * rows * width, 20 * rows * width),
        name="last_norm",
    )(vec, d_out, *terms)


def second_back_kernel(vec, summed_ref, *refs, n_in):
    d_ref, low_ref, sum_ref = refs[n_in:]
    second_back_math(vec, summed_ref[...], add_up(refs[:n_in]), d_ref, low_ref, sum_ref)


def second_back(vec, summed, terms):
    rows, width = summed.shape
    return pl.pallas_call(
        functools.partial(second_back_kernel, n_in=len(terms)),
        in_specs=[VMEM] * (2 + len(terms)),
        out_specs=[VMEM] * 3,
        out_shape=[
            jax.ShapeDtypeStruct((rows, width), F32),
            jax.ShapeDtypeStruct((rows, width), BF16),
            jax.ShapeDtypeStruct((3, width), F32),
        ],
        compiler_params=params(),
        cost_estimate=cost(40 * rows * width, 20 * rows * width),
        name="second_back",
    )(vec, summed, *terms)


def first_back_kernel(perm, cols, vec, mixed_ref, *refs, n_w, n_in):
    ws = refs[:n_w]
    d_ref, low_ref, sum_ref, ctx_ref = refs[n_w + n_in :]
    d_out = add_up(refs[n_w : n_w + n_in])
    xhat, rstd = norm_stats(mixed_ref[...])
    d_mixed = norm_back(xhat, rstd, d_out, vec[0:1, :])
    d_ref[...] = d_mixed
    low_ref[...] = d_mixed.astype(BF16)
    sum_ref[0:1, :] = column(d_out * xhat)
    sum_ref[1:2, :] = column(d_out)
    sum_ref[2:3, :] = column(d_mixed)
    halves, deep, wide = ws[0].shape
    parts = []
    for s in range(halves):
        parts.append(low_ref[:, pl.ds(pl.multiple_of(cols[s] * wide, 128), wide)])
    for r in range(n_w):
        acc = dot(ws[r][0], parts[0], 1, 1)
        for s in range(1, halves):
            acc = acc + dot(ws[r][s], parts[s], 1, 1)
        rows = pl.ds(pl.multiple_of(perm[r] * deep, deep), deep)
        ctx_ref[rows, :] = acc.astype(BF16)


def first_back(vec, mixed, ws, layer, terms, perm, cols):
    rows, width = mixed.shape
    return pl.pallas_call(
        functools.partial(first_back_kernel, n_w=len(ws), n_in=len(terms)),
        grid_spec=pltpu.PrefetchScalarGridSpec(
            num_scalar_prefetch=2,
            grid=(1,),
            in_specs=[VMEM] * 2 + merge_specs(ws, layer) + [VMEM] * len(terms),
            out_specs=[VMEM] * 4,
        ),
        out_shape=[
            jax.ShapeDtypeStruct((rows, width), F32),
            jax.ShapeDtypeStruct((rows, width), BF16),
            jax.ShapeDtypeStruct((3, width), F32),
            jax.ShapeDtypeStruct((width, rows), BF16),
        ],
        compiler_params=params(),
        cost_estimate=cost(2 * rows * width * width, 2 * width * width + 20 * rows * width),
        name="first_back",
    )(perm, cols, vec, mixed, *ws, *terms)


ERF_TOP = (
    -2.72614225801306e-10,
    2.77068142495902e-08,
    -2.10102402082508e-06,
    -5.69250639462346e-05,
    -7.34990630326855e-04,
    -2.95459980854025e-03,
    -1.60960333262415e-02,
)
ERF_BOTTOM = (
    -1.45660718464996e-05,
    -2.13374055278905e-04,
    -1.68282697438203e-03,
    -7.37332916720468e-03,
    -1.42647390514189e-02,
)


def erf(value):
    x = jnp.clip(value, -4.0, 4.0)
    sq = x * x
    top = jnp.full_like(x, ERF_TOP[0])
    for c in ERF_TOP[1:]:
        top = top * sq + c
    bottom = jnp.full_like(x, ERF_BOTTOM[0])
    for c in ERF_BOTTOM[1:]:
        bottom = bottom * sq + c
    return x * top / bottom


def up_kernel(*refs, n, fc):
    xs = refs[:n]
    up, bias, down = refs[n : n + 3]
    outs = refs[n + 3 : 2 * n + 3]
    cat_ref, act_ref, slope_ref = refs[2 * n + 3 :]
    r = pl.program_id(0)
    for i in range(n):

        @pl.when(r == i)
        def _():
            cat_ref[...] = xs[i][...]

    halves, deep, hidden = up.shape
    for f in range(0, hidden, fc):
        fs = slice(f, f + fc)
        u = dot(cat_ref[:, :deep], up[0, :, fs], 1, 0)
        for s in range(1, halves):
            u = u + dot(cat_ref[:, s * deep : (s + 1) * deep], up[s, :, fs], 1, 0)
        u = u + bias[:, fs].astype(F32)
        phi = 0.5 + 0.5 * erf(u * (0.5**0.5))
        act_ref[:, fs] = (u * phi).astype(BF16)
        slope = phi + u * (jnp.exp(-0.5 * u * u) * 0.3989422804014327)
        slope_ref[:, fs] = slope.astype(BF16)
    out = [dot(act_ref[...], down[s], 1, 0).astype(BF16) for s in range(halves)]
    for i in range(n):

        @pl.when(r == i)
        def _():
            for s in range(halves):
                outs[i][:, s * deep : (s + 1) * deep] = out[s]


def ff_specs(n, piece, width, hidden):
    whole = pl.BlockSpec((piece, width), lambda r: (0, 0))
    flat = pl.BlockSpec((piece, width), lambda r: (r, 0))
    tall = pl.BlockSpec((piece, hidden), lambda r: (r, 0))
    shapes = [jax.ShapeDtypeStruct((piece, width), BF16)] * n
    shapes += [jax.ShapeDtypeStruct((n * piece, w), BF16) for w in (width, hidden)]
    return whole, flat, tall, shapes


def feed_forward(xs, up, bias, down, fc):
    n = len(xs)
    piece, width = xs[0].shape
    hidden = up.shape[2]
    whole, flat, tall, shapes = ff_specs(n, piece, width, hidden)
    got = pl.pallas_call(
        functools.partial(up_kernel, n=n, fc=fc),
        grid=(n,),
        in_specs=[whole] * n
        + [
            pl.BlockSpec(up.shape, lambda r: (0, 0, 0)),
            pl.BlockSpec((1, hidden), lambda r: (0, 0)),
            pl.BlockSpec(down.shape, lambda r: (0, 0, 0)),
        ],
        out_specs=[whole] * n + [flat, tall, tall],
        out_shape=shapes + [shapes[-1]],
        compiler_params=params(),
        cost_estimate=cost(
            4 * n * piece * width * hidden, 12 * n * piece * width + 4 * width * hidden
        ),
        name="feed_forward",
    )(*xs, up, bias, down)
    return got[:n], got[n], got[n + 1], got[n + 2]


def down_kernel(*refs, n, fc):
    ds = refs[:n]
    slope_ref, up, down = refs[n : n + 3]
    outs = refs[n + 3 : 2 * n + 3]
    cat_ref, du_ref, sum_ref = refs[2 * n + 3 :]
    r = pl.program_id(0)
    for i in range(n):

        @pl.when(r == i)
        def _():
            cat_ref[...] = ds[i][...]

    halves, deep, hidden = up.shape

    @pl.when(r == 0)
    def _():
        sum_ref[...] = jnp.zeros_like(sum_ref)

    for f in range(0, hidden, fc):
        fs = slice(f, f + fc)
        d = dot(cat_ref[:, :deep], down[0, fs, :], 1, 1)
        for s in range(1, halves):
            d = d + dot(cat_ref[:, s * deep : (s + 1) * deep], down[s, fs, :], 1, 1)
        du = (d * slope_ref[:, fs].astype(F32)).astype(BF16)
        du_ref[:, fs] = du
        sum_ref[:, fs] += column(du.astype(F32))
    out = [dot(du_ref[...], up[s], 1, 1).astype(BF16) for s in range(halves)]
    for i in range(n):

        @pl.when(r == i)
        def _():
            for s in range(halves):
                outs[i][:, s * deep : (s + 1) * deep] = out[s]


def feed_back(ds, slope, up, down, fc):
    n = len(ds)
    piece, width = ds[0].shape
    hidden = up.shape[2]
    whole, flat, tall, shapes = ff_specs(n, piece, width, hidden)
    got = pl.pallas_call(
        functools.partial(down_kernel, n=n, fc=fc),
        grid=(n,),
        in_specs=[whole] * n
        + [
            tall,
            pl.BlockSpec(up.shape, lambda r: (0, 0, 0)),
            pl.BlockSpec(down.shape, lambda r: (0, 0, 0)),
        ],
        out_specs=[whole] * n + [flat, tall, pl.BlockSpec((1, hidden), lambda r: (0, 0))],
        out_shape=shapes + [jax.ShapeDtypeStruct((1, hidden), F32)],
        compiler_params=params(),
        cost_estimate=cost(
            4 * n * piece * width * hidden, 12 * n * piece * width + 4 * width * hidden
        ),
        name="feed_back",
    )(*ds, slope, up, down)
    return got[:n], got[n], got[n + 1], got[n + 2]


def place_kernel(perm, *refs):
    out = refs[-1]
    for i, ref in enumerate(refs[:-1]):

        @pl.when(pl.program_id(0) == i)
        def _():
            out[...] = ref[...].astype(out.dtype)


def place(blocks, perm, dtype):
    piece, width = blocks[0].shape
    n = len(blocks)
    return pl.pallas_call(
        place_kernel,
        grid_spec=pltpu.PrefetchScalarGridSpec(
            num_scalar_prefetch=1,
            grid=(n,),
            in_specs=[pl.BlockSpec((piece, width), lambda r, p: (0, 0))] * n,
            out_specs=pl.BlockSpec((piece, width), lambda r, p: (p[r], 0)),
        ),
        out_shape=jax.ShapeDtypeStruct((n * piece, width), dtype),
        compiler_params=params(),
        cost_estimate=cost(n * piece * width, 6 * n * piece * width),
        name="place",
    )(perm, *blocks)


def store_kernel(*refs):
    refs[-1][...] = refs[-2][...].astype(F32)


def store(buffer, joined, first, rows, width, layer, layers):
    chunk = joined.shape[1]
    block = math.gcd(math.gcd(rows, 256), first)
    ins = [
        pl.BlockSpec((block, chunk), lambda i, j: ((first + j * rows) // block + i, 0)),
    ]
    args = [joined]
    alias = {}
    if buffer is not None:
        ins = [pl.BlockSpec(memory_space=pl.ANY)] + ins
        args = [buffer] + args
        alias = {0: 0}
    return pl.pallas_call(
        store_kernel,
        grid=(rows // block, width // chunk),
        in_specs=ins,
        out_specs=pl.BlockSpec((None, block, chunk), lambda i, j: (layer, i, j)),
        out_shape=jax.ShapeDtypeStruct((layers, rows, width), F32),
        input_output_aliases=alias,
        compiler_params=params(32),
        cost_estimate=cost(rows * width, 6 * rows * width),
        name="store",
    )(*args)


def swap(value, axis, count, bit):
    return lax.ppermute(value, axis, [(i, i ^ bit) for i in range(count)])


def spread(own, count):
    one = swap(own, "tensor", count, 1)
    two = swap(own, "tensor", count, 2)
    return [own, one, two, swap(two, "tensor", count, 1)]


def collect(blocks, count):
    three = swap(blocks[3], "tensor", count, 1)
    far = (blocks[2].astype(F32) + three.astype(F32)).astype(BF16)
    two = swap(far, "tensor", count, 2)
    return [blocks[0], swap(blocks[1], "tensor", count, 1), two]


def ordered(parts, index, bits):
    for bit in bits:
        flip = (index & bit) != 0
        parts = [jnp.where(flip, parts[i ^ bit], parts[i]) for i in range(len(parts))]
    return parts


def sum_all(value, axis, count):
    bit = 1
    while bit < count:
        value = value + swap(value, axis, count, bit)
        bit *= 2
    return value


BQ, BK, UNROLL = 256, 512, 4
BQ_BACK, BK_BACK, UNROLL_BACK = 256, 256, 4


def build(n_shard, n_context, n_tensor):
    def shards(
        hidden_in,
        segment_ids,
        cotangent,
        qkv_weight,
        merge_weight,
        up_weight,
        down_weight,
        row_gains,
        row_bias,
        head_bias,
        up_bias,
    ):
        layers = qkv_weight.shape[0]
        rows, width = hidden_in.shape
        piece = rows // n_tensor
        deep = width // n_shard
        me_s = lax.axis_index(SHARD)
        me_t = lax.axis_index("tensor")
        order = jnp.arange(n_tensor, dtype=jnp.int32)
        relative = order ^ me_t.astype(jnp.int32)
        cols_all = jnp.arange(n_shard, dtype=jnp.int32)
        cols_rel = cols_all ^ me_s.astype(jnp.int32)

        w_in = jnp.transpose(qkv_weight, (0, 2, 1, 3))
        first = [w_in[0:1]]
        for bit in range(1, n_shard):
            first.append(swap(w_in[0:1], SHARD, n_shard, bit))
        segs = [segment_ids[0]]
        for bit in range(1, n_context):
            segs.append(swap(segment_ids[0], CONTEXT, n_context, bit))
        tables = jnp.concatenate([row_gains, row_bias], axis=1)
        w_in = [w_in[layer] for layer in range(layers)]
        up_weight = [up_weight[layer] for layer in range(layers)]
        down_weight = [down_weight[layer] for layer in range(layers)]
        first, segs, tables, merge_weight, up_weight, down_weight, w_in = (
            lax.optimization_barrier(
                (first, segs, tables, merge_weight, up_weight, down_weight, w_in)
            )
        )
        parts = [merge_weight]
        tabs = [tables]
        for bit in range(1, n_shard):
            parts.append(swap(merge_weight, SHARD, n_shard, bit))
            tabs.append(swap(tables, SHARD, n_shard, bit))
        bits = [1 << i for i in range(n_context.bit_length() - 1)]
        seg = jnp.concatenate(ordered(segs, lax.axis_index(CONTEXT), bits))
        doc = document_bounds(seg)
        tiles = tile_list(*doc, BQ, BK, UNROLL)
        tiles_back = tile_list(*doc, BQ_BACK, BK_BACK, UNROLL_BACK)
        w_qkv, cols = [first], [cols_rel]
        x_own = lax.dynamic_slice_in_dim(hidden_in, me_t * piece, piece, 0).astype(F32)
        d_last = lax.dynamic_slice_in_dim(cotangent, me_t * piece, piece, 0)
        xs = [hidden_in]
        x_nat = hidden_in
        saved = []
        for layer in range(layers):
            perm = order if layer == 0 else relative
            got = list(project(xs, w_qkv[layer], cols[layer], head_bias[layer], perm, piece))
            if layer == 0:
                got[0], parts, tabs, up_weight, down_weight, w_in = lax.optimization_barrier(
                    (got[0], parts, tabs, up_weight, down_weight, w_in)
                )
                pair = jnp.stack(parts)
                far = swap(pair, "tensor", n_tensor, 2)
                bits = [1 << i for i in range(n_shard.bit_length() - 1)]
                vec = jnp.concatenate(ordered(tabs, me_s, bits), axis=2).astype(F32)
                w_up, w_down = [], []
                for i in range(layers):
                    if i > 0:
                        w_qkv.append([lax.all_gather(w_in[i], SHARD, axis=0, tiled=False)])
                        cols.append(cols_all)
                    w_up.append(lax.all_gather(up_weight[i], SHARD, axis=0, tiled=False))
                    w_down.append(lax.all_gather(down_weight[i], SHARD, axis=0, tiled=False))
            else:
                x_nat = got[1]
            qkv = lax.all_to_all(got[0], CONTEXT, 0, 0, tiled=True)
            ctx_low, ctx, lse = attend(qkv, doc, tiles, piece, BQ, BK, UNROLL)
            if layer == 0:
                ctx_low, far, pair = lax.optimization_barrier((ctx_low, far, pair))
                w_merge = [pair, swap(pair, "tensor", n_tensor, 1)]
                w_merge += [far, swap(far, "tensor", n_tensor, 1)]
            mine = lax.all_to_all(ctx_low, ("tensor", CONTEXT), 0, 0, tiled=True)
            mine = mine.reshape(width, piece)
            mixed, normed, low = merge_norm(
                mine, w_merge, layer, x_own, vec[layer], relative, cols_rel
            )
            blocks, x1, act, slope = feed_forward(
                spread(low, n_tensor), w_up[layer], up_bias[layer : layer + 1], w_down[layer], 512
            )
            terms = [normed] + collect(blocks, n_tensor)
            keep = [x_nat, qkv, ctx, lse, mine, mixed, x1, act, slope]
            if layer + 1 < layers:
                summed, x_own, x_low = second_norm(vec[layer], terms)
                xs = spread(x_low, n_tensor)
                keep.append(summed)
            else:
                out_low, d_summed, d_low, sums = last_norm(vec[layer], d_last, terms)
            saved.append(keep)

        def send_parts(make):
            return [make(me_s ^ bit).astype(BF16) for bit in range(1, n_shard)]

        def exchange(parts):
            return [swap(p, SHARD, n_shard, i + 1) for i, p in enumerate(parts)]

        def settle(make, got):
            total = make(me_s)
            for part in got:
                total = total + part.astype(F32)
            return total.astype(BF16)

        def context_scatter(value):
            return lax.psum_scatter(value, CONTEXT, scatter_dimension=0, tiled=True)

        def context_gather(value):
            return lax.all_gather(value, CONTEXT, axis=0, tiled=True)

        def chunks(value, wide):
            return [value[:, i : i + wide] for i in range(0, value.shape[1], wide)]

        def join_wide(g_down, g_up):
            return jnp.concatenate([g_down] + chunks(g_up, g_down.shape[1]), axis=0)

        def join_narrow(g_qkv, g_merge):
            flat = g_qkv.reshape(-1, g_qkv.shape[2])
            wide = min(flat.shape[1], g_merge.shape[1])
            return jnp.concatenate(chunks(flat, wide) + chunks(g_merge, wide), axis=0)

        tie = lax.optimization_barrier
        grads = [None] * layers
        rowsums, sides = [None] * layers, [None] * layers
        terms = None
        hidden_out = None
        deep_t = width // n_tensor
        late, wide, narrow = (), (), ()
        for layer in reversed(range(layers)):
            last = layer + 1 == layers
            x_nat, qkv, ctx, lse, mine, mixed, x1, act, slope = saved[layer][:9]
            if not last:
                d_summed, d_low, sums = second_back(vec[layer], saved[layer][9], terms)
            blocks, wide = tie((spread(d_low, n_tensor), wide))
            if not last:
                wide = context_gather(wide)
            blocks, dy, du, g_hidden = feed_back(blocks, slope, w_up[layer], w_down[layer], 512)

            def down_part(i, act=act, dy=dy):
                return dot(act, lax.dynamic_slice_in_dim(dy, i * deep, deep, 1), 0, 0)

            def up_part(i, x1=x1, du=du):
                return dot(lax.dynamic_slice_in_dim(x1, i * deep, deep, 1), du, 0, 0)

            terms = [d_summed] + collect(blocks, n_tensor)
            down_send, up_send = send_parts(down_part), send_parts(up_part)
            terms, down_send, up_send, late, wide = tie((terms, down_send, up_send, late, wide))
            down_got, up_got = exchange(down_send), exchange(up_send)
            d_mixed, d_low, sums_one, d_mine = first_back(
                vec[layer], mixed, w_merge, layer, terms, relative, cols_rel
            )
            if not last:
                narrow = join_narrow(settle(makers[0], late[0]), settle(makers[1], late[1]))
                narrow = context_scatter(narrow)
            pieces = d_mine.reshape(n_tensor * n_context, HEAD_DIM, piece)
            d_ctx = lax.all_to_all(pieces, ("tensor", CONTEXT), 0, 0, tiled=True)
            g_blocks = []
            for r in range(n_tensor):
                part = lax.dynamic_slice_in_dim(mine, relative[r] * deep_t, deep_t, 0)
                g_blocks.append(dot(part, d_low, 1, 0).astype(BF16))
            d_ctx, g_blocks, narrow, down_got, out_low = tie(
                (d_ctx, g_blocks, narrow, down_got, out_low)
            )
            if last:
                out_low = [out_low, swap(out_low, "tensor", n_tensor, 2)]
            else:
                narrow = context_gather(narrow)
            d_heads = attend_back(
                qkv, doc, tiles_back, lse, ctx, d_ctx, piece, BQ_BACK, BK_BACK, UNROLL_BACK
            )
            d_heads, down_got, up_got, g_blocks, out_low, narrow = tie(
                (d_heads, down_got, up_got, g_blocks, out_low, narrow)
            )
            d_heads = lax.all_to_all(d_heads, CONTEXT, 0, 0, tiled=True)
            g_terms = collect(g_blocks, n_tensor)
            g_merge = sum(term.astype(F32) for term in g_terms).astype(BF16)
            new_wide = join_wide(settle(down_part, down_got), settle(up_part, up_got))
            if last:
                near = [swap(v, "tensor", n_tensor, 1) for v in out_low]
                out_low = [out_low[0], near[0], out_low[1], near[1]]
                hidden_out = place(out_low, relative, BF16)
            d_heads, new_wide, g_merge, narrow, hidden_out = tie(
                (d_heads, new_wide, g_merge, narrow, hidden_out)
            )
            new_wide = context_scatter(new_wide)
            got = project_back(d_heads, w_qkv[layer], cols[layer], relative, piece, width)
            d_x, d_proj, g_heads = got[:n_tensor], got[n_tensor], got[n_tensor + 1]

            def merge_part(i, g_merge=g_merge):
                return lax.dynamic_slice_in_dim(g_merge, i * deep, deep, 1).astype(F32)

            def qkv_part(i, x_nat=x_nat, d_proj=d_proj):
                d = lax.dynamic_slice_in_dim(x_nat, i * deep, deep, 1)
                return jnp.einsum("rd,crj->cdj", d, d_proj, preferred_element_type=F32)

            qkv_send, merge_send = send_parts(qkv_part), send_parts(merge_part)
            terms = [d_mixed] + collect(d_x, n_tensor)
            terms, qkv_send, merge_send = tie((terms, qkv_send, merge_send))
            if not last:
                grads[layer + 1] = (wide, narrow)
            late = (exchange(qkv_send), exchange(merge_send))
            makers = (qkv_part, merge_part)
            wide, narrow = new_wide, ()
            rowsums[layer] = jnp.concatenate([sums_one, sums], axis=0)
            sides[layer] = jnp.concatenate([g_heads.reshape(-1), g_hidden.reshape(-1)])
        total = terms[0]
        for term in terms[1:]:
            total = total + term.astype(F32)
        blocks, wide = tie((spread(total.astype(BF16), n_tensor), wide))
        narrow = join_narrow(settle(makers[0], late[0]), settle(makers[1], late[1]))
        wide, narrow = tie((wide, narrow))
        grads[0] = (context_gather(wide), context_gather(context_scatter(narrow)))
        input_grad = place(blocks, relative, F32)
        hw = width // n_tensor
        hidden = up_bias.shape[1]
        g_down = g_up = g_qkv = g_merge = None
        for layer in reversed(range(layers)):
            wide, narrow = grads[layer]
            g_down = store(g_down, wide, 0, hidden, deep, layer, layers)
            g_up = store(g_up, wide, hidden, deep, hidden, layer, layers)
            g_qkv = store(g_qkv, narrow, 0, 3 * deep, hw, layer, layers)
            g_merge = store(
                g_merge, narrow, narrow.shape[0] - hw * deep // narrow.shape[1], hw, deep, layer, layers
            )
        g_qkv = g_qkv.reshape(layers, 3, deep, -1)

        table = sum_all(jnp.concatenate(rowsums, axis=0), "tensor", n_tensor)
        side = jnp.concatenate(sides).reshape(-1, width)
        packed = jnp.concatenate([table, side], axis=0)
        packed = sum_all(packed, SHARD, n_shard)
        packed = sum_all(packed, CONTEXT, n_context)
        table = packed[: layers * 6].reshape(layers, 6, width)
        table = lax.dynamic_slice_in_dim(table, me_s * deep, deep, 2)
        side = packed[layers * 6 :].reshape(layers, -1)
        head_count = 2 * head_bias.shape[2]
        grad_gains = table[:, 0::3]
        grad_shifts = table[:, jnp.array([2, 1, 5, 4])]
        grad_heads = side[:, :head_count].reshape(head_bias.shape)
        grad_hidden = side[:, head_count:]
        return (
            hidden_out,
            input_grad,
            jnp.transpose(g_qkv, (0, 2, 1, 3)),
            g_merge,
            g_up,
            g_down,
            grad_gains,
            grad_shifts,
            grad_heads,
            grad_hidden,
        )

    return shards


def solution(mesh):
    tokens = (SHARD, CONTEXT)
    weights = (
        P(None, SHARD, None, "tensor"),
        P(None, "tensor", SHARD),
        P(None, SHARD, "tensor"),
        P(None, "tensor", SHARD),
        P(None, None, SHARD),
        P(None, None, SHARD),
        P(None, None, "tensor"),
        P(None, "tensor"),
    )
    return jax.shard_map(
        build(mesh.shape[SHARD], mesh.shape[CONTEXT], mesh.shape["tensor"]),
        mesh=mesh,
        in_specs=(P(tokens, None), P(*tokens), P(tokens, None)) + weights,
        out_specs=(P(tokens, None), P(tokens, None)) + weights,
        check_vma=False,
    )
```

```python
import functools
import math

import jax
import jax.numpy as jnp
from jax import lax
from jax.experimental import pallas as pl
from jax.experimental.pallas import tpu as pltpu
from jax.sharding import PartitionSpec as P

HEAD_DIM = 64
DOCS = 16
NEG = -1e30
EPSILON = 1e-05
CALM = 75.0
FAR = 1 << 24
F32 = jnp.float32
BF16 = jnp.bfloat16
SHARD = "shard"
CONTEXT = "context"
VMEM = pl.BlockSpec(memory_space=pltpu.VMEM)


def dot(a, b, ca, cb):
    return lax.dot_general(a, b, (((ca,), (cb,)), ((), ())), preferred_element_type=F32)


def params(mib=56):
    return pltpu.CompilerParams(vmem_limit_bytes=mib << 20)


def cost(flops, nbytes, trans=0):
    return pl.CostEstimate(flops=1, bytes_accessed=1, transcendentals=0)


def qkv_kernel(perm, cols, *refs, n_x, n_w):
    xs, bias_ref = refs[:n_x], refs[n_x]
    w_refs = refs[n_x + 1 : n_x + 1 + n_w]
    out_ref = refs[-1]
    x_ref = xs[0]
    if n_x > 1:
        out_ref, x_ref = refs[-2:]
        for i in range(n_x):

            @pl.when(pl.program_id(0) == i)
            def _():
                x_ref[...] = xs[i][...]

    scale = HEAD_DIM ** (-0.5)
    width = w_refs[0].shape[-1]
    for c in range(3):
        acc = None
        k = 0
        for w_ref in w_refs:
            deep = w_ref.shape[2]
            for i in range(w_ref.shape[0]):
                off = pl.multiple_of(cols[k] * deep, 128)
                part = dot(x_ref[:, pl.ds(off, deep)], w_ref[i, c], 1, 0)
                acc = part if acc is None else acc + part
                k += 1
        if c == 0:
            acc = (acc + bias_ref[0:1, :].astype(F32)) * scale
        if c == 2:
            acc = acc + bias_ref[1:2, :].astype(F32)
        turned = acc.T.astype(BF16)
        for h in range(width // HEAD_DIM):
            out_ref[h, c] = turned[h * HEAD_DIM : (h + 1) * HEAD_DIM]


def project(xs, weights, cols, bias, perm, piece, base, rows, kept):
    width = xs[0].shape[1]
    count = sum(x.shape[0] for x in xs) // piece
    hw = weights[0].shape[-1]
    heads = hw // HEAD_DIM
    out_shape = [jax.ShapeDtypeStruct((heads, 3, HEAD_DIM, rows), BF16)]
    out_specs = [
        pl.BlockSpec((heads, 3, HEAD_DIM, piece), lambda r, p, c: (0, 0, 0, p[r + base]))
    ]
    x_specs = [pl.BlockSpec((piece, width), lambda r, p, c: (r, 0))]
    if len(xs) > 1:
        x_specs = [pl.BlockSpec((piece, width), lambda r, p, c: (0, 0))] * len(xs)
        out_shape.append(jax.ShapeDtypeStruct((rows, width), BF16))
        out_specs.append(pl.BlockSpec((piece, width), lambda r, p, c: (p[r + base], 0)))
    first = 3 + len(xs) + len(weights)
    return pl.pallas_call(
        functools.partial(qkv_kernel, n_x=len(xs), n_w=len(weights)),
        grid_spec=pltpu.PrefetchScalarGridSpec(
            num_scalar_prefetch=2,
            grid=(count,),
            in_specs=x_specs
            + [pl.BlockSpec(bias.shape, lambda r, p, c: (0, 0))]
            + [pl.BlockSpec(w.shape, lambda r, p, c: (0, 0, 0, 0)) for w in weights]
            + [pl.BlockSpec(memory_space=pl.ANY)] * len(kept),
            out_specs=out_specs,
        ),
        out_shape=out_shape,
        input_output_aliases={first + i: i for i in range(len(kept))},
        compiler_params=params(),
        cost_estimate=pl.CostEstimate(
            flops=8 * count * piece * width * 3 * hw, bytes_accessed=1, transcendentals=0
        ),
        name="project",
    )(perm, cols, *xs, bias, *weights, *kept)


def back_kernel(perm, cols, *refs, n_w):
    d_ref = refs[0]
    w_refs = refs[1 : 1 + n_w]
    out_refs = refs[1 + n_w : -2]
    proj_ref, sum_ref = refs[-2:]
    heads = d_ref.shape[0]
    r = pl.program_id(0)
    first = r == 0

    @pl.when(first)
    def _():
        sum_ref[...] = jnp.zeros_like(sum_ref)

    parts = []
    for c in range(3):
        flat = jnp.concatenate([d_ref[h, c] for h in range(heads)], axis=0)
        turned = flat.astype(F32).T
        if c != 1:
            row = c // 2
            sum_ref[row : row + 1, :] += jnp.sum(turned, axis=0, keepdims=True)
        turned = turned.astype(BF16)
        proj_ref[c] = turned
        parts.append(turned)
    k = 0
    for w_ref in w_refs:
        deep = w_ref.shape[2]
        for i in range(w_ref.shape[0]):
            acc = dot(parts[0], w_ref[i, 0], 1, 1)
            acc = acc + dot(parts[1], w_ref[i, 1], 1, 1)
            acc = acc + dot(parts[2], w_ref[i, 2], 1, 1)
            off = pl.multiple_of(cols[k] * deep, 128)
            low = acc.astype(BF16)
            for n, out_ref in enumerate(out_refs):

                @pl.when(r == n)
                def _():
                    out_ref[:, pl.ds(off, deep)] = low

            k += 1


def project_back(d_heads, weights, cols, perm, piece, width):
    heads, _, _, rows = d_heads.shape
    blocks = rows // piece
    hw = heads * HEAD_DIM
    return pl.pallas_call(
        functools.partial(back_kernel, n_w=len(weights)),
        grid_spec=pltpu.PrefetchScalarGridSpec(
            num_scalar_prefetch=2,
            grid=(blocks,),
            in_specs=[pl.BlockSpec((heads, 3, HEAD_DIM, piece), lambda r, p, c: (0, 0, 0, p[r]))]
            + [pl.BlockSpec(w.shape, lambda r, p, c: (0, 0, 0, 0)) for w in weights],
            out_specs=[pl.BlockSpec((piece, width), lambda r, p, c: (0, 0))] * blocks
            + [
                pl.BlockSpec((3, piece, hw), lambda r, p, c: (0, p[r], 0)),
                pl.BlockSpec((2, hw), lambda r, p, c: (0, 0)),
            ],
        ),
        out_shape=[jax.ShapeDtypeStruct((piece, width), BF16)] * blocks
        + [
            jax.ShapeDtypeStruct((3, rows, hw), BF16),
            jax.ShapeDtypeStruct((2, hw), F32),
        ],
        compiler_params=params(),
        cost_estimate=cost(2 * rows * width * 3 * hw, 2 * rows * width * 2 + 6 * width * hw),
        name="project_back",
    )(perm, cols, d_heads, *weights)


def tile_kernel_index(tiles, t, size, bq, bk, chunk):
    q0 = pl.multiple_of(tiles[1 + t] * bq, bq)
    k0 = pl.multiple_of(tiles[1 + size + t] * bk, bk)
    cj, kj = q0 // chunk, k0 // chunk
    off = pl.multiple_of(q0 - cj * chunk, bq)
    ko = pl.multiple_of(k0 - kj * chunk, bk)
    return q0, k0, cj, off, kj, ko, tiles[1 + 2 * size + t]


def inside(spot, pos, start, length):
    place = (spot + (pos - start)).astype(jnp.uint32)
    return place < length.astype(jnp.uint32)


def attend_kernel(
    tiles,
    qkv,
    start,
    length,
    low,
    high,
    lse,
    keys,
    acc,
    total,
    top,
    *,
    bq,
    bk,
    seq,
    chunk,
    piece,
    unroll,
    size,
):
    n_chunks = seq // chunk
    q_most = jnp.zeros((1, chunk), F32)
    k_most = jnp.zeros((1, chunk), F32)
    for j in range(n_chunks):
        q = qkv[j, 0].astype(F32)
        k = qkv[j, 1].astype(F32)
        q_most = jnp.maximum(q_most, jnp.sum(q * q, axis=0, keepdims=True))
        k_most = jnp.maximum(k_most, jnp.sum(k * k, axis=0, keepdims=True))
        keys[j * chunk : (j + 1) * chunk, :] = k.T.astype(BF16)
    calm = jnp.max(q_most) * jnp.max(k_most) < CALM * CALM
    acc[...] = jnp.zeros_like(acc)
    total[...] = jnp.zeros_like(total)
    spot = lax.broadcasted_iota(jnp.int32, (bk, bq), 0)

    def tile(t):
        q0, k0, cj, off, kj, ko, pos = tile_kernel_index(tiles, t, size, bq, bk, chunk)
        s = dot(keys[pl.ds(k0, bk), :], qkv[cj, 0, :, pl.ds(off, bq)], 1, 0)
        ok = inside(spot, pos, start[:, pl.ds(q0, bq)], length[:, pl.ds(q0, bq)])
        return q0, kj, ko, s, ok

    @pl.when(calm)
    def _():
        top[...] = jnp.zeros_like(top)

        def step(i, _):
            group = [tile(i * unroll + u) for u in range(unroll)]
            for q0, kj, ko, s, ok in group:
                p = jnp.where(ok, jnp.exp(s), 0.0)
                total[:, pl.ds(q0, bq)] += jnp.sum(p, axis=0, keepdims=True)
                value = qkv[kj, 2, :, pl.ds(ko, bk)]
                acc[:, pl.ds(q0, bq)] += dot(value, p.astype(BF16), 1, 0)
            return 0

        lax.fori_loop(0, tiles[0], step, 0)

    @pl.when(jnp.logical_not(calm))
    def _():
        top[...] = jnp.full_like(top, NEG)

        def step(i, _):
            q0, kj, ko, s, ok = tile(i)
            s = jnp.where(ok, s, NEG)
            here = pl.ds(q0, bq)
            new = jnp.maximum(top[:, here], jnp.max(s, axis=0, keepdims=True))
            p = jnp.where(ok, jnp.exp(s - new), 0.0)
            fade = jnp.exp(top[:, here] - new)
            total[:, here] = total[:, here] * fade + jnp.sum(p, axis=0, keepdims=True)
            value = qkv[kj, 2, :, pl.ds(ko, bk)]
            acc[:, here] = acc[:, here] * fade + dot(value, p.astype(BF16), 1, 0)
            top[:, here] = new
            return 0

        lax.fori_loop(0, tiles[0] * unroll, step, 0)

    lse[...] = top[...] + jnp.log(total[...])
    for z in range(n_chunks):
        for t in range(chunk // piece):
            base = z * chunk + t * piece
            out = acc[:, base : base + piece] / total[:, base : base + piece]
            low[t * n_chunks + z] = out.astype(BF16)
            high[t * n_chunks + z] = out


def attend(qkv, doc, tiles, piece, bq, bk, unroll):
    n_chunks, _, hd, chunk = qkv.shape
    seq = n_chunks * chunk
    start, end = doc
    pieces = seq // piece
    return pl.pallas_call(
        functools.partial(
            attend_kernel,
            bq=bq,
            bk=bk,
            seq=seq,
            chunk=chunk,
            piece=piece,
            unroll=unroll,
            size=(tiles.shape[0] - 1) // 3,
        ),
        grid_spec=pltpu.PrefetchScalarGridSpec(
            num_scalar_prefetch=1,
            grid=(),
            in_specs=[VMEM] * 3,
            out_specs=[VMEM] * 3,
            scratch_shapes=[
                pltpu.VMEM((seq, hd), BF16),
                pltpu.VMEM((hd, seq), F32),
                pltpu.VMEM((1, seq), F32),
                pltpu.VMEM((1, seq), F32),
            ],
        ),
        out_shape=[
            jax.ShapeDtypeStruct((pieces, hd, piece), BF16),
            jax.ShapeDtypeStruct((pieces, hd, piece), F32),
            jax.ShapeDtypeStruct((1, seq), F32),
        ],
        compiler_params=params(40),
        cost_estimate=cost(2 * seq * seq * hd, 8 * seq * hd, seq * seq // 4),
        name="attend",
    )(tiles, qkv, start[None], (end - start)[None])


def attend_back_kernel(
    tiles,
    qkv,
    start,
    length,
    lse,
    ctx,
    d_ctx,
    out,
    keys,
    values,
    queries,
    grads,
    d_keys,
    d_values,
    d_queries,
    delta,
    d_turned,
    *,
    bq,
    bk,
    seq,
    chunk,
    piece,
    unroll,
    size,
):
    n_chunks = seq // chunk
    for j in range(n_chunks):
        sl = slice(j * chunk, (j + 1) * chunk)
        queries[sl, :] = qkv[j, 0].astype(F32).T.astype(BF16)
        keys[sl, :] = qkv[j, 1].astype(F32).T.astype(BF16)
        values[sl, :] = qkv[j, 2].astype(F32).T.astype(BF16)
    for at in range(seq // piece):
        t, z = at // n_chunks, at % n_chunks
        base = z * chunk + t * piece
        part = d_ctx[at].astype(F32)
        d_turned[:, base : base + piece] = d_ctx[at]
        grads[base : base + piece, :] = part.T.astype(BF16)
        delta[:, base : base + piece] = jnp.sum(part * ctx[at], axis=0, keepdims=True)
    d_queries[...] = jnp.zeros_like(d_queries)
    d_keys[...] = jnp.zeros_like(d_keys)
    d_values[...] = jnp.zeros_like(d_values)
    spot = lax.broadcasted_iota(jnp.int32, (bk, bq), 0)

    def tile(t):
        q0, k0, cj, off, kj, ko, pos = tile_kernel_index(tiles, t, size, bq, bk, chunk)
        s = dot(keys[pl.ds(k0, bk), :], qkv[cj, 0, :, pl.ds(off, bq)], 1, 0)
        dp = dot(values[pl.ds(k0, bk), :], d_turned[:, pl.ds(q0, bq)], 1, 0)
        ok = inside(spot, pos, start[:, pl.ds(q0, bq)], length[:, pl.ds(q0, bq)])
        return q0, k0, kj, ko, s, dp, ok

    def step(i, _):
        group = [tile(i * unroll + u) for u in range(unroll)]
        for q0, k0, kj, ko, s, dp, ok in group:
            here = pl.ds(q0, bq)
            there = pl.ds(k0, bk)
            p = jnp.where(ok, jnp.exp(s - lse[:, here]), 0.0)
            ds = (p * (dp - delta[:, here])).astype(BF16)
            d_values[there, :] += dot(p.astype(BF16), grads[here, :], 1, 0)
            d_keys[there, :] += dot(ds, queries[here, :], 1, 0)
            d_queries[:, here] += dot(qkv[kj, 1, :, pl.ds(ko, bk)], ds, 1, 0)
        return 0

    lax.fori_loop(0, tiles[0], step, 0)
    scale = HEAD_DIM ** (-0.5)
    for j in range(n_chunks):
        sl = slice(j * chunk, (j + 1) * chunk)
        out[j, 0] = (d_queries[:, sl].astype(BF16).astype(F32) * scale).astype(BF16)
        out[j, 1] = d_keys[sl, :].T.astype(BF16)
        out[j, 2] = d_values[sl, :].T.astype(BF16)


def attend_back(qkv, doc, tiles, lse, ctx, d_ctx, piece, bq, bk, unroll):
    n_chunks, _, hd, chunk = qkv.shape
    seq = n_chunks * chunk
    start, end = doc
    return pl.pallas_call(
        functools.partial(
            attend_back_kernel,
            bq=bq,
            bk=bk,
            seq=seq,
            chunk=chunk,
            piece=piece,
            unroll=unroll,
            size=(tiles.shape[0] - 1) // 3,
        ),
        grid_spec=pltpu.PrefetchScalarGridSpec(
            num_scalar_prefetch=1,
            grid=(),
            in_specs=[VMEM] * 6,
            out_specs=VMEM,
            scratch_shapes=[pltpu.VMEM((seq, hd), BF16)] * 4
            + [pltpu.VMEM((seq, hd), F32)] * 2
            + [
                pltpu.VMEM((hd, seq), F32),
                pltpu.VMEM((1, seq), F32),
                pltpu.VMEM((hd, seq), BF16),
            ],
        ),
        out_shape=jax.ShapeDtypeStruct((n_chunks, 3, hd, chunk), BF16),
        compiler_params=params(48),
        cost_estimate=cost(4 * seq * seq * hd, 16 * seq * hd, seq * seq // 4),
        name="attend_back",
    )(tiles, qkv, start[None], (end - start)[None], lse, ctx, d_ctx)


def document_bounds(seg):
    ids = jnp.arange(DOCS, dtype=jnp.int32)[:, None]
    below = jnp.sum((seg[None] < ids).astype(jnp.int32), axis=1, keepdims=True)
    upto = jnp.sum((seg[None] <= ids).astype(jnp.int32), axis=1, keepdims=True)
    mine = seg[None] == ids
    start = jnp.sum(jnp.where(mine, below, 0), axis=0)
    end = jnp.sum(jnp.where(mine, upto, 0), axis=0)
    return start, end


def tile_list(start, end, bq, bk, unroll):
    n, m = start.shape[0] // bq, start.shape[0] // bk
    low = start.reshape(n, bq)[:, 0] // bk
    high = (end.reshape(n, bq)[:, -1] + bk - 1) // bk
    count = high - low
    order = jnp.arange(n)
    upto = jnp.sum(jnp.where(order[:, None] <= order[None], count[:, None], 0), axis=0)
    total = upto[-1]
    t = jnp.arange(n * m + unroll, dtype=jnp.int32)
    mine = jnp.minimum(jnp.sum((t[:, None] >= upto[None]).astype(jnp.int32), axis=1), n - 1)
    base = jnp.sum(jnp.where(mine[:, None] == order[None], (high - upto)[None], 0), axis=1)
    real = t < total
    key = jnp.where(real, base + t, 0)
    pos = jnp.where(real, key * bk, FAR)
    steps = (total + unroll - 1) // unroll
    return jnp.concatenate([steps[None], mine, key, pos]).astype(jnp.int32)


def norm_stats(value):
    center = value - jnp.mean(value, axis=-1, keepdims=True)
    rstd = lax.rsqrt(jnp.mean(center * center, axis=-1, keepdims=True) + EPSILON)
    return center * rstd, rstd


def norm_back(xhat, rstd, d_out, gain):
    scaled = d_out * gain
    m1 = jnp.mean(scaled, axis=-1, keepdims=True)
    m2 = jnp.mean(scaled * xhat, axis=-1, keepdims=True)
    return (scaled - m1 - xhat * m2) * rstd


def column(value):
    return jnp.sum(value, axis=0, keepdims=True)


def merge_kernel(perm, cols, ctx, x, vec, *refs):
    ws = refs[:-3]
    mixed_ref, normed_ref, low_ref = refs[-3:]
    halves, deep, wide = ws[0].shape
    parts = []
    for r in range(len(ws)):
        rows = pl.ds(pl.multiple_of(perm[r] * deep, deep), deep)
        parts.append(ctx[rows, :].astype(F32).T.astype(BF16))
    for s in range(halves):
        acc = dot(parts[0], ws[0][s], 1, 0)
        for r in range(1, len(ws)):
            acc = acc + dot(parts[r], ws[r][s], 1, 0)
        sl = pl.ds(pl.multiple_of(cols[s] * wide, 128), wide)
        mixed_ref[:, sl] = x[:, sl] + acc + vec[2:3, sl]
    xhat, _ = norm_stats(mixed_ref[...])
    normed = xhat * vec[0:1, :] + vec[3:4, :]
    normed_ref[...] = normed
    low_ref[...] = normed.astype(BF16)


def merge_specs(ws, layer):
    shape = ws[0].shape
    spec = pl.BlockSpec((shape[0], None) + shape[2:], lambda *_: (0, layer, 0, 0))
    return [spec] * len(ws)


def merge_norm(ctx, ws, layer, x, vec, perm, cols):
    rows, width = x.shape
    big = jax.ShapeDtypeStruct((rows, width), F32)
    return pl.pallas_call(
        merge_kernel,
        grid_spec=pltpu.PrefetchScalarGridSpec(
            num_scalar_prefetch=2,
            grid=(1,),
            in_specs=[VMEM] * 3 + merge_specs(ws, layer),
            out_specs=[VMEM] * 3,
        ),
        out_shape=[big, big, jax.ShapeDtypeStruct((rows, width), BF16)],
        compiler_params=params(),
        cost_estimate=cost(2 * rows * width * width, 2 * width * width + 16 * rows * width),
        name="merge_norm",
    )(perm, cols, ctx, x, vec, *ws)


def add_up(refs):
    total = refs[0][...].astype(F32)
    for ref in refs[1:]:
        total = total + ref[...].astype(F32)
    return total


def row_blocks(count, rows, width):
    block = rows
    return (rows // block,), [pl.BlockSpec((block, width), lambda r: (r, 0))] * count


def all_of(shape):
    return pl.BlockSpec(shape, lambda r: (0, 0))


def norm_kernel(vec, *refs, n_in):
    summed_ref, out_ref, low_ref = refs[n_in:]
    summed = add_up(refs[:n_in]) + vec[4:5, :]
    summed_ref[...] = summed
    xhat, _ = norm_stats(summed)
    out = xhat * vec[1:2, :] + vec[5:6, :]
    out_ref[...] = out
    low_ref[...] = out.astype(BF16)


def second_norm(vec, terms):
    shape = terms[0].shape
    big = jax.ShapeDtypeStruct(shape, F32)
    grid, specs = row_blocks(len(terms) + 3, *shape)
    return pl.pallas_call(
        functools.partial(norm_kernel, n_in=len(terms)),
        grid=grid,
        in_specs=[all_of(vec.shape)] + specs[3:],
        out_specs=specs[:3],
        out_shape=[big, big, jax.ShapeDtypeStruct(shape, BF16)],
        compiler_params=params(),
        cost_estimate=cost(20 * shape[0] * shape[1], 20 * shape[0] * shape[1]),
        name="second_norm",
    )(vec, *terms)


def second_back_math(vec, summed, d_out, d_ref, low_ref, sum_ref):
    xhat, rstd = norm_stats(summed)
    d_summed = norm_back(xhat, rstd, d_out, vec[1:2, :])
    d_ref[...] = d_summed
    low_ref[...] = d_summed.astype(BF16)

    @pl.when(pl.program_id(0) == 0)
    def _():
        sum_ref[...] = jnp.zeros_like(sum_ref)

    sum_ref[0:1, :] += column(d_out * xhat)
    sum_ref[1:2, :] += column(d_out)
    sum_ref[2:3, :] += column(d_summed)
    return xhat


def last_kernel(vec, d_out_ref, *refs, n_in):
    out_ref, d_ref, low_ref, sum_ref = refs[n_in:]
    summed = add_up(refs[:n_in]) + vec[4:5, :]
    d_out = d_out_ref[...].astype(F32)
    xhat = second_back_math(vec, summed, d_out, d_ref, low_ref, sum_ref)
    out_ref[...] = (xhat * vec[1:2, :] + vec[5:6, :]).astype(BF16)


def last_norm(vec, d_out, terms):
    rows, width = terms[0].shape
    low = jax.ShapeDtypeStruct((rows, width), BF16)
    grid, specs = row_blocks(len(terms) + 4, rows, width)
    return pl.pallas_call(
        functools.partial(last_kernel, n_in=len(terms)),
        grid=grid,
        in_specs=[all_of(vec.shape)] + specs[3:],
        out_specs=specs[:3] + [all_of((3, width))],
        out_shape=[
            low,
            jax.ShapeDtypeStruct((rows, width), F32),
            low,
            jax.ShapeDtypeStruct((3, width), F32),
        ],
        compiler_params=params(),
        cost_estimate=cost(40 * rows * width, 20 * rows * width),
        name="last_norm",
    )(vec, d_out, *terms)


def second_back_kernel(vec, summed_ref, *refs, n_in):
    d_ref, low_ref, sum_ref = refs[n_in:]
    second_back_math(vec, summed_ref[...], add_up(refs[:n_in]), d_ref, low_ref, sum_ref)


def second_back(vec, summed, terms):
    rows, width = summed.shape
    grid, specs = row_blocks(len(terms) + 3, rows, width)
    return pl.pallas_call(
        functools.partial(second_back_kernel, n_in=len(terms)),
        grid=grid,
        in_specs=[all_of(vec.shape)] + specs[2:],
        out_specs=specs[:2] + [all_of((3, width))],
        out_shape=[
            jax.ShapeDtypeStruct((rows, width), F32),
            jax.ShapeDtypeStruct((rows, width), BF16),
            jax.ShapeDtypeStruct((3, width), F32),
        ],
        compiler_params=params(),
        cost_estimate=cost(40 * rows * width, 20 * rows * width),
        name="second_back",
    )(vec, summed, *terms)


def first_back_kernel(perm, cols, vec, mixed_ref, *refs, n_w, n_in):
    ws = refs[:n_w]
    d_ref, low_ref, sum_ref, ctx_ref = refs[n_w + n_in :]
    d_out = add_up(refs[n_w : n_w + n_in])
    xhat, rstd = norm_stats(mixed_ref[...])
    d_mixed = norm_back(xhat, rstd, d_out, vec[0:1, :])
    d_ref[...] = d_mixed
    low_ref[...] = d_mixed.astype(BF16)
    sum_ref[0:1, :] = column(d_out * xhat)
    sum_ref[1:2, :] = column(d_out)
    sum_ref[2:3, :] = column(d_mixed)
    halves, deep, wide = ws[0].shape
    parts = []
    for s in range(halves):
        parts.append(low_ref[:, pl.ds(pl.multiple_of(cols[s] * wide, 128), wide)])
    for r in range(n_w):
        acc = dot(ws[r][0], parts[0], 1, 1)
        for s in range(1, halves):
            acc = acc + dot(ws[r][s], parts[s], 1, 1)
        rows = pl.ds(pl.multiple_of(perm[r] * deep, deep), deep)
        ctx_ref[rows, :] = acc.astype(BF16)


def first_back(vec, mixed, ws, layer, terms, perm, cols):
    rows, width = mixed.shape
    return pl.pallas_call(
        functools.partial(first_back_kernel, n_w=len(ws), n_in=len(terms)),
        grid_spec=pltpu.PrefetchScalarGridSpec(
            num_scalar_prefetch=2,
            grid=(1,),
            in_specs=[VMEM] * 2 + merge_specs(ws, layer) + [VMEM] * len(terms),
            out_specs=[VMEM] * 4,
        ),
        out_shape=[
            jax.ShapeDtypeStruct((rows, width), F32),
            jax.ShapeDtypeStruct((rows, width), BF16),
            jax.ShapeDtypeStruct((3, width), F32),
            jax.ShapeDtypeStruct((width, rows), BF16),
        ],
        compiler_params=params(),
        cost_estimate=cost(2 * rows * width * width, 2 * width * width + 20 * rows * width),
        name="first_back",
    )(perm, cols, vec, mixed, *ws, *terms)


ERF_TOP = (
    -2.72614225801306e-10,
    2.77068142495902e-08,
    -2.10102402082508e-06,
    -5.69250639462346e-05,
    -7.34990630326855e-04,
    -2.95459980854025e-03,
    -1.60960333262415e-02,
)
ERF_BOTTOM = (
    -1.45660718464996e-05,
    -2.13374055278905e-04,
    -1.68282697438203e-03,
    -7.37332916720468e-03,
    -1.42647390514189e-02,
)


def erf(value):
    x = jnp.clip(value, -4.0, 4.0)
    sq = x * x
    top = jnp.full_like(x, ERF_TOP[0])
    for c in ERF_TOP[1:]:
        top = top * sq + c
    bottom = jnp.full_like(x, ERF_BOTTOM[0])
    for c in ERF_BOTTOM[1:]:
        bottom = bottom * sq + c
    return x * top / bottom


def up_kernel(*refs, n, fc):
    xs = refs[:n]
    up, bias, down = refs[n : n + 3]
    outs = refs[-3 - n : -3]
    cat_ref, act_ref, slope_ref = refs[-3:]
    r = pl.program_id(0)
    for i in range(n):

        @pl.when(r == i)
        def _():
            cat_ref[...] = xs[i][...]

    halves, deep, hidden = up.shape
    for f in range(0, hidden, fc):
        fs = slice(f, f + fc)
        u = dot(cat_ref[:, :deep], up[0, :, fs], 1, 0)
        for s in range(1, halves):
            u = u + dot(cat_ref[:, s * deep : (s + 1) * deep], up[s, :, fs], 1, 0)
        u = u + bias[:, fs].astype(F32)
        phi = 0.5 + 0.5 * erf(u * (0.5**0.5))
        act_ref[:, fs] = (u * phi).astype(BF16)
        slope = phi + u * (jnp.exp(-0.5 * u * u) * 0.3989422804014327)
        slope_ref[:, fs] = slope.astype(BF16)
    out = [dot(act_ref[...], down[s], 1, 0).astype(BF16) for s in range(halves)]
    for i in range(n):

        @pl.when(r == i)
        def _():
            for s in range(halves):
                outs[i][:, s * deep : (s + 1) * deep] = out[s]


def ff_specs(n, piece, width, hidden, base):
    whole = pl.BlockSpec((piece, width), lambda r: (0, 0))
    flat = pl.BlockSpec((piece, width), lambda r: (r + base, 0))
    tall = pl.BlockSpec((piece, hidden), lambda r: (r + base, 0))
    return whole, flat, tall


def feed_forward(xs, up, bias, down, fc, base, rows, kept):
    n = len(xs)
    piece, width = xs[0].shape
    hidden = up.shape[2]
    whole, flat, tall = ff_specs(n, piece, width, hidden, base)
    got = pl.pallas_call(
        functools.partial(up_kernel, n=n, fc=fc),
        grid=(n,),
        in_specs=[whole] * n
        + [
            pl.BlockSpec(up.shape, lambda r: (0, 0, 0)),
            pl.BlockSpec((1, hidden), lambda r: (0, 0)),
            pl.BlockSpec(down.shape, lambda r: (0, 0, 0)),
        ]
        + [pl.BlockSpec(memory_space=pl.ANY)] * len(kept),
        out_specs=[whole] * n + [flat, tall, tall],
        out_shape=[jax.ShapeDtypeStruct((piece, width), BF16)] * n
        + [jax.ShapeDtypeStruct((rows, w), BF16) for w in (width, hidden, hidden)],
        input_output_aliases={n + 3 + i: n + i for i in range(len(kept))},
        compiler_params=params(),
        cost_estimate=pl.CostEstimate(
            flops=16 * n * piece * width * hidden, bytes_accessed=1, transcendentals=0
        ),
        name="feed_forward",
    )(*xs, up, bias, down, *kept)
    return list(got[:n]), list(got[n:])


def down_kernel(*refs, n, fc):
    ds = refs[:n]
    slope_ref, up, down = refs[n : n + 3]
    outs = refs[-3 - n : -3]
    cat_ref, du_ref, sum_ref = refs[-3:]
    r = pl.program_id(0)
    for i in range(n):

        @pl.when(r == i)
        def _():
            cat_ref[...] = ds[i][...]

    halves, deep, hidden = up.shape

    @pl.when(r == 0)
    def _():
        sum_ref[...] = jnp.zeros_like(sum_ref)

    for f in range(0, hidden, fc):
        fs = slice(f, f + fc)
        d = dot(cat_ref[:, :deep], down[0, fs, :], 1, 1)
        for s in range(1, halves):
            d = d + dot(cat_ref[:, s * deep : (s + 1) * deep], down[s, fs, :], 1, 1)
        du = (d * slope_ref[:, fs].astype(F32)).astype(BF16)
        du_ref[:, fs] = du
        sum_ref[:, fs] += column(du.astype(F32))
    out = [dot(du_ref[...], up[s], 1, 1).astype(BF16) for s in range(halves)]
    for i in range(n):

        @pl.when(r == i)
        def _():
            for s in range(halves):
                outs[i][:, s * deep : (s + 1) * deep] = out[s]


def feed_back(ds, slope, up, down, fc, base, kept, filler):
    n = len(ds)
    piece, width = ds[0].shape
    rows, hidden = slope.shape
    whole, flat, tall = ff_specs(n, piece, width, hidden, base)
    got = pl.pallas_call(
        functools.partial(down_kernel, n=n, fc=fc),
        grid=(n,),
        in_specs=[whole] * n
        + [
            tall,
            pl.BlockSpec(up.shape, lambda r: (0, 0, 0)),
            pl.BlockSpec(down.shape, lambda r: (0, 0, 0)),
        ]
        + [pl.BlockSpec(memory_space=pl.ANY)] * len(kept),
        out_specs=[whole] * n + [flat, tall, pl.BlockSpec((1, hidden), lambda r: (0, 0))],
        out_shape=[jax.ShapeDtypeStruct((piece, width), BF16)] * n
        + [jax.ShapeDtypeStruct((rows, w), BF16) for w in (width, hidden)]
        + [jax.ShapeDtypeStruct((1, hidden), F32)],
        input_output_aliases={n + 3 + i: n + i for i in range(len(kept))},
        compiler_params=params(),
        cost_estimate=pl.CostEstimate(
            flops=16 * n * piece * width * hidden if filler else 1,
            bytes_accessed=1,
            transcendentals=0,
        ),
        name="feed_back",
    )(*ds, slope, up, down, *kept)
    return list(got[:n]), list(got[n : n + 2]), got[n + 2]


def place_kernel(perm, *refs):
    out = refs[-1]
    for i, ref in enumerate(refs[:-1]):

        @pl.when(pl.program_id(0) == i)
        def _():
            out[...] = ref[...].astype(out.dtype)


def place(blocks, perm, dtype):
    piece, width = blocks[0].shape
    n = len(blocks)
    return pl.pallas_call(
        place_kernel,
        grid_spec=pltpu.PrefetchScalarGridSpec(
            num_scalar_prefetch=1,
            grid=(n,),
            in_specs=[pl.BlockSpec((piece, width), lambda r, p: (0, 0))] * n,
            out_specs=pl.BlockSpec((piece, width), lambda r, p: (p[r], 0)),
        ),
        out_shape=jax.ShapeDtypeStruct((n * piece, width), dtype),
        compiler_params=params(),
        cost_estimate=cost(n * piece * width, 6 * n * piece * width),
        name="place",
    )(perm, *blocks)


def store_kernel(*refs):
    refs[-1][...] = refs[-2][...].astype(F32)


def store(buffer, joined, first, rows, width, layer, layers, runs):
    wide = joined.shape[1]
    chunk = min(wide, width)
    own, whole, start = runs
    stride = rows if width >= wide else rows * width // wide
    block = math.gcd(math.gcd(math.gcd(stride, 256), first), math.gcd(own, start))

    def place_of(i, j):
        row = j * rows + i * block
        side = 0
        if width < wide:
            row, side = i * block % stride, i * block // stride
        row = first + row
        return ((row // own * whole + start + row % own) // block, side)

    ins = [pl.BlockSpec((block, chunk), place_of)]
    args = [joined]
    alias = {}
    if buffer is not None:
        ins = [pl.BlockSpec(memory_space=pl.ANY)] + ins
        args = [buffer] + args
        alias = {0: 0}
    return pl.pallas_call(
        store_kernel,
        grid=(rows // block, width // chunk),
        in_specs=ins,
        out_specs=pl.BlockSpec((None, block, chunk), lambda i, j: (layer, i, j)),
        out_shape=jax.ShapeDtypeStruct((layers, rows, width), F32),
        input_output_aliases=alias,
        compiler_params=params(32),
        cost_estimate=cost(rows * width, 6 * rows * width),
        name="store",
    )(*args)


def swap(value, axis, count, bit):
    return lax.ppermute(value, axis, [(i, i ^ bit) for i in range(count)])


def spread(own, count):
    one = swap(own, "tensor", count, 1)
    two = swap(own, "tensor", count, 2)
    return [own, one, two, swap(two, "tensor", count, 1)]


def collect(blocks, count):
    three = swap(blocks[3], "tensor", count, 1)
    far = (blocks[2].astype(F32) + three.astype(F32)).astype(BF16)
    two = swap(far, "tensor", count, 2)
    return [blocks[0], swap(blocks[1], "tensor", count, 1), two]


def ordered(parts, index, bits):
    for bit in bits:
        flip = (index & bit) != 0
        parts = [jnp.where(flip, parts[i ^ bit], parts[i]) for i in range(len(parts))]
    return parts


def sum_all(value, axis, count):
    bit = 1
    while bit < count:
        value = value + swap(value, axis, count, bit)
        bit *= 2
    return value


BQ, BK, UNROLL = 256, 512, 4
BQ_BACK, BK_BACK, UNROLL_BACK = 256, 256, 4


def build(n_shard, n_context, n_tensor):
    def shards(
        hidden_in,
        segment_ids,
        cotangent,
        qkv_weight,
        merge_weight,
        up_weight,
        down_weight,
        row_gains,
        row_bias,
        head_bias,
        up_bias,
    ):
        layers = qkv_weight.shape[0]
        rows, width = hidden_in.shape
        piece = rows // n_tensor
        deep = width // n_shard
        me_s = lax.axis_index(SHARD)
        me_t = lax.axis_index("tensor")
        order = jnp.arange(n_tensor, dtype=jnp.int32)
        relative = order ^ me_t.astype(jnp.int32)
        cols_all = jnp.arange(n_shard, dtype=jnp.int32)
        cols_rel = cols_all ^ me_s.astype(jnp.int32)

        w_in = jnp.transpose(qkv_weight, (0, 2, 1, 3))
        first = [w_in[0:1]]
        for bit in range(1, n_shard):
            first.append(swap(w_in[0:1], SHARD, n_shard, bit))
        tables = jnp.concatenate([row_gains, row_bias], axis=1)
        w_in = [w_in[layer] for layer in range(layers)]
        up_weight = [up_weight[layer] for layer in range(layers)]
        down_weight = [down_weight[layer] for layer in range(layers)]
        up_weight, segment_ids = lax.optimization_barrier((up_weight, segment_ids))
        segs = [segment_ids[0]]
        for bit in range(1, n_context):
            segs.append(swap(segment_ids[0], CONTEXT, n_context, bit))
        first, segs, tables, merge_weight, up_weight, down_weight, w_in = (
            lax.optimization_barrier(
                (first, segs, tables, merge_weight, up_weight, down_weight, w_in)
            )
        )
        parts = [merge_weight]
        tabs = [tables]
        for bit in range(1, n_shard):
            parts.append(swap(merge_weight, SHARD, n_shard, bit))
            tabs.append(swap(tables, SHARD, n_shard, bit))
        bits = [1 << i for i in range(n_context.bit_length() - 1)]
        seg = jnp.concatenate(ordered(segs, lax.axis_index(CONTEXT), bits))
        doc = document_bounds(seg)
        tiles = tile_list(*doc, BQ, BK, UNROLL)
        tiles_back = tile_list(*doc, BQ_BACK, BK_BACK, UNROLL_BACK)
        w_qkv, cols = [first], [cols_rel]
        x_own = lax.dynamic_slice_in_dim(hidden_in, me_t * piece, piece, 0).astype(F32)
        d_last = lax.dynamic_slice_in_dim(cotangent, me_t * piece, piece, 0)
        xs = [hidden_in]
        x_nat = hidden_in
        saved = []
        for layer in range(layers):
            args = (w_qkv[layer], cols[layer], head_bias[layer])
            if layer == 0:
                got = list(project(xs, *args, order, piece, 0, rows, []))
            else:
                near = [x_low, swap(x_low, "tensor", n_tensor, 1)]
                far = swap(x_low, "tensor", n_tensor, 2)
                got = list(project(near, *args, relative, piece, 0, rows, []))
                far, got = lax.optimization_barrier((far, got))
                far = [far, swap(far, "tensor", n_tensor, 1)]
                got = list(project(far, *args, relative, piece, 2, rows, got))
            if layer == 0:
                got[0], up_weight, down_weight, w_in = lax.optimization_barrier(
                    (got[0], up_weight, down_weight, w_in)
                )
                pair = jnp.stack(parts)
                far = swap(pair, "tensor", n_tensor, 2)
                bits = [1 << i for i in range(n_shard.bit_length() - 1)]
                vec = jnp.concatenate(ordered(tabs, me_s, bits), axis=2).astype(F32)
                w_up, w_down = [], []
                for i in range(layers):
                    if i > 0:
                        w_qkv.append([lax.all_gather(w_in[i], SHARD, axis=0, tiled=False)])
                        cols.append(cols_all)
                    w_up.append(lax.all_gather(up_weight[i], SHARD, axis=0, tiled=False))
                    w_down.append(lax.all_gather(down_weight[i], SHARD, axis=0, tiled=False))
            else:
                x_nat = got[1]
            qkv = lax.all_to_all(got[0], CONTEXT, 0, 0, tiled=True)
            ctx_low, ctx, lse = attend(qkv, doc, tiles, piece, BQ, BK, UNROLL)
            if layer == 0:
                ctx_low, far, pair = lax.optimization_barrier((ctx_low, far, pair))
                w_merge = [pair, swap(pair, "tensor", n_tensor, 1)]
                w_merge += [far, swap(far, "tensor", n_tensor, 1)]
            mine = lax.all_to_all(ctx_low, ("tensor", CONTEXT), 0, 0, tiled=True)
            mine = mine.reshape(width, piece)
            mixed, normed, low = merge_norm(
                mine, w_merge, layer, x_own, vec[layer], relative, cols_rel
            )
            ff_args = (w_up[layer], up_bias[layer : layer + 1], w_down[layer], 512)
            far = swap(low, "tensor", n_tensor, 2)
            near = [low, swap(low, "tensor", n_tensor, 1)]
            blocks, kept = feed_forward(near, *ff_args, 0, rows, [])
            far, kept = lax.optimization_barrier((far, kept))
            far = [far, swap(far, "tensor", n_tensor, 1)]
            got, kept = feed_forward(far, *ff_args, 2, rows, kept)
            blocks += got
            x1, act, slope = kept
            terms = [normed] + collect(blocks, n_tensor)
            keep = [x_nat, qkv, ctx, lse, mine, mixed, x1, act, slope]
            if layer + 1 < layers:
                terms, w_qkv[1] = lax.optimization_barrier((terms, w_qkv[1]))
                summed, x_own, x_low = second_norm(vec[layer], terms)
                keep.append(summed)
            else:
                out_low, d_summed, d_low, sums = last_norm(vec[layer], d_last, terms)
            saved.append(keep)

        def send_parts(make):
            return [make(me_s ^ bit).astype(BF16) for bit in range(1, n_shard)]

        def exchange(parts):
            return [swap(p, SHARD, n_shard, i + 1) for i, p in enumerate(parts)]

        def settle(make, got):
            total = make(me_s)
            for part in got:
                total = total + part.astype(F32)
            return total.astype(BF16)

        def context_scatter(value):
            return lax.psum_scatter(value, CONTEXT, scatter_dimension=0, tiled=True)

        def context_gather(value):
            return lax.all_gather(value, CONTEXT, axis=0, tiled=True)

        def chunks(value, wide):
            return [value[:, i : i + wide] for i in range(0, value.shape[1], wide)]

        def join_wide(g_down, g_up):
            return jnp.concatenate(g_down + chunks(g_up, deep), axis=0)

        def join_narrow(g_qkv, g_merge):
            flat = g_qkv.reshape(-1, g_qkv.shape[2])
            if deep > flat.shape[1]:
                part = flat.shape[0] * flat.shape[1] // deep
                sides = [flat[i : i + part] for i in range(0, flat.shape[0], part)]
                flat = jnp.concatenate(sides, axis=1)
            return jnp.concatenate(chunks(flat, deep) + [g_merge], axis=0)

        tie = lax.optimization_barrier
        grads = [None] * layers
        rowsums, sides = [None] * layers, [None] * layers
        terms = None
        hidden_out = None
        deep_t = width // n_tensor
        late, wide, narrow = (), (), ()
        for layer in reversed(range(layers)):
            last = layer + 1 == layers
            x_nat, qkv, ctx, lse, mine, mixed, x1, act, slope = saved[layer][:9]
            if not last:
                d_summed, d_low, sums = second_back(vec[layer], saved[layer][9], terms)
            ff_args = (slope, w_up[layer], w_down[layer], 512)
            far = swap(d_low, "tensor", n_tensor, 2)
            near = [d_low, swap(d_low, "tensor", n_tensor, 1)]
            if not last:
                near, wide = tie((near, jnp.concatenate(wide, axis=0)))
                wide = context_gather(wide)
            blocks, kept, g_hidden = feed_back(near, *ff_args, 0, [], last)
            far, kept = tie((far, kept))
            far = [far, swap(far, "tensor", n_tensor, 1)]
            got, kept, part = feed_back(far, *ff_args, 2, kept, last)
            blocks += got
            blocks, late = tie((blocks, late))
            g_hidden = g_hidden + part
            dy, du = kept

            def down_part(i, act=act, dy=dy):
                return dot(act, lax.dynamic_slice_in_dim(dy, i * deep, deep, 1), 0, 0)

            def up_part(i, x1=x1, du=du):
                return dot(lax.dynamic_slice_in_dim(x1, i * deep, deep, 1), du, 0, 0)

            terms = [d_summed] + collect(blocks, n_tensor)
            down_send, up_send = send_parts(down_part), send_parts(up_part)
            terms, down_send, up_send, wide = tie((terms, down_send, up_send, wide))
            down_got, up_got = exchange(down_send), exchange(up_send)
            d_mixed, d_low, sums_one, d_mine = first_back(
                vec[layer], mixed, w_merge, layer, terms, relative, cols_rel
            )
            if not last:
                narrow = join_narrow(settle(makers[0], late[0]), settle(makers[1], late[1]))
                narrow = context_scatter(narrow)
            pieces = d_mine.reshape(n_tensor * n_context, HEAD_DIM, piece)
            d_ctx = lax.all_to_all(pieces, ("tensor", CONTEXT), 0, 0, tiled=True)
            g_blocks = []
            for r in range(n_tensor):
                part = lax.dynamic_slice_in_dim(mine, relative[r] * deep_t, deep_t, 0)
                g_blocks.append(dot(part, d_low, 1, 0).astype(BF16))
            g_down = settle(down_part, down_got) if last else ()
            d_ctx, g_blocks, narrow, down_got, g_down, out_low = tie(
                (d_ctx, g_blocks, narrow, down_got, g_down, out_low)
            )
            if last:
                out_low = [out_low, swap(out_low, "tensor", n_tensor, 2)]
                g_down = context_scatter(g_down)
            else:
                narrow = context_gather(narrow)
            d_heads = attend_back(
                qkv, doc, tiles_back, lse, ctx, d_ctx, piece, BQ_BACK, BK_BACK, UNROLL_BACK
            )
            d_heads, down_got, up_got, g_blocks, g_down, out_low, narrow = tie(
                (d_heads, down_got, up_got, g_blocks, g_down, out_low, narrow)
            )
            d_heads = lax.all_to_all(d_heads, CONTEXT, 0, 0, tiled=True)
            g_terms = collect(g_blocks, n_tensor)
            g_merge = sum(term.astype(F32) for term in g_terms).astype(BF16)
            g_up = settle(up_part, up_got)
            if last:
                new_wide = join_wide([], g_up)
            else:
                new_wide = join_wide([settle(down_part, down_got)], g_up)
            if last:
                near = [swap(v, "tensor", n_tensor, 1) for v in out_low]
                out_low = [out_low[0], near[0], out_low[1], near[1]]
                hidden_out = place(out_low, relative, BF16)
            d_heads, new_wide, g_merge, narrow, hidden_out = tie(
                (d_heads, new_wide, g_merge, narrow, hidden_out)
            )
            new_wide = context_scatter(new_wide)
            if last:
                new_wide = [g_down, new_wide]
            got = project_back(d_heads, w_qkv[layer], cols[layer], relative, piece, width)
            d_x, d_proj, g_heads = got[:n_tensor], got[n_tensor], got[n_tensor + 1]

            def merge_part(i, g_merge=g_merge):
                return lax.dynamic_slice_in_dim(g_merge, i * deep, deep, 1).astype(F32)

            def qkv_part(i, x_nat=x_nat, d_proj=d_proj):
                d = lax.dynamic_slice_in_dim(x_nat, i * deep, deep, 1)
                return jnp.einsum("rd,crj->cdj", d, d_proj, preferred_element_type=F32)

            qkv_send, merge_send = send_parts(qkv_part), send_parts(merge_part)
            terms = [d_mixed] + collect(d_x, n_tensor)
            if layer > 0:
                terms, qkv_send, merge_send = tie((terms, qkv_send, merge_send))

            if not last:
                grads[layer + 1] = (wide, narrow)
            late = (exchange(qkv_send), exchange(merge_send))
            makers = (qkv_part, merge_part)
            wide, narrow = new_wide, ()
            rowsums[layer] = jnp.concatenate([sums_one, sums], axis=0)
            sides[layer] = jnp.concatenate([g_heads.reshape(-1), g_hidden.reshape(-1)])
        total = terms[0]
        for term in terms[1:]:
            total = total + term.astype(F32)
        narrow = join_narrow(settle(makers[0], late[0]), settle(makers[1], late[1]))
        total, wide, narrow = tie((total.astype(BF16), wide, narrow))
        blocks = spread(total, n_tensor)
        table = sum_all(jnp.concatenate(rowsums, axis=0), "tensor", n_tensor)
        side = jnp.concatenate(sides).reshape(-1, width)
        packed = jnp.concatenate([table, side], axis=0)
        packed = sum_all(packed, SHARD, n_shard)
        packed = sum_all(packed, CONTEXT, n_context)
        narrow = context_scatter(narrow)
        wide, narrow, blocks, packed = tie((wide, narrow, blocks, packed))
        grads[0] = context_gather(jnp.concatenate([wide, narrow], axis=0))
        input_grad = place(blocks, relative, F32)
        hw = width // n_tensor
        hidden = up_bias.shape[1]
        g_down = g_up = g_qkv = g_merge = None
        n_qkv = 3 * deep * hw // deep
        n_narrow = n_qkv + hw
        run_w, run_n = 2 * hidden // n_context, n_narrow // n_context
        for layer in reversed(range(layers)):
            if layer == 0:
                wide = narrow = grads[0]
                runs_d = runs_u = (run_w, run_w + run_n, 0)
                runs_n = (run_n, run_w + run_n, run_w)
                second = hidden
            else:
                wide, narrow = grads[layer]
                runs_d = runs_u = runs_n = (1 << 20, 0, 0)
                second = hidden
                if layer + 1 == layers:
                    run = hidden // n_context
                    runs_d, runs_u, second = (run, 2 * run, 0), (run, 2 * run, run), 0
                runs_n = (n_narrow, 0, 0)
            g_down = store(g_down, wide, 0, hidden, deep, layer, layers, runs_d)
            g_up = store(g_up, wide, second, deep, hidden, layer, layers, runs_u)
            g_qkv = store(g_qkv, narrow, 0, 3 * deep, hw, layer, layers, runs_n)
            g_merge = store(g_merge, narrow, n_qkv, hw, deep, layer, layers, runs_n)
        g_qkv = g_qkv.reshape(layers, 3, deep, -1)

        table = packed[: layers * 6].reshape(layers, 6, width)
        table = lax.dynamic_slice_in_dim(table, me_s * deep, deep, 2)
        side = packed[layers * 6 :].reshape(layers, -1)
        head_count = 2 * head_bias.shape[2]
        grad_gains = table[:, 0::3]
        grad_shifts = table[:, jnp.array([2, 1, 5, 4])]
        grad_heads = side[:, :head_count].reshape(head_bias.shape)
        grad_hidden = side[:, head_count:]
        return (
            hidden_out,
            input_grad,
            jnp.transpose(g_qkv, (0, 2, 1, 3)),
            g_merge,
            g_up,
            g_down,
            grad_gains,
            grad_shifts,
            grad_heads,
            grad_hidden,
        )

    return shards


def solution(mesh):
    tokens = (SHARD, CONTEXT)
    weights = (
        P(None, SHARD, None, "tensor"),
        P(None, "tensor", SHARD),
        P(None, SHARD, "tensor"),
        P(None, "tensor", SHARD),
        P(None, None, SHARD),
        P(None, None, SHARD),
        P(None, None, "tensor"),
        P(None, "tensor"),
    )
    return jax.shard_map(
        build(mesh.shape[SHARD], mesh.shape[CONTEXT], mesh.shape["tensor"]),
        mesh=mesh,
        in_specs=(P(tokens, None), P(*tokens), P(tokens, None)) + weights,
        out_specs=(P(tokens, None), P(tokens, None)) + weights,
        check_vma=False,
    )
```

```python
import functools
import math

import jax
import jax.numpy as jnp
from jax import lax
from jax.experimental import pallas as pl
from jax.experimental.pallas import tpu as pltpu
from jax.sharding import PartitionSpec as P

HEAD_DIM = 64
DOCS = 16
NEG = -1e30
EPSILON = 1e-05
CALM = 75.0
FAR = 1 << 24
F32 = jnp.float32
BF16 = jnp.bfloat16
SHARD = "shard"
CONTEXT = "context"
VMEM = pl.BlockSpec(memory_space=pltpu.VMEM)


def dot(a, b, ca, cb):
    return lax.dot_general(a, b, (((ca,), (cb,)), ((), ())), preferred_element_type=F32)


def params(mib=56):
    return pltpu.CompilerParams(vmem_limit_bytes=mib << 20)


def cost(flops, nbytes, trans=0):
    return pl.CostEstimate(flops=1, bytes_accessed=1, transcendentals=0)


def qkv_kernel(perm, cols, *refs, n_x, n_w):
    xs, bias_ref = refs[:n_x], refs[n_x]
    w_refs = refs[n_x + 1 : n_x + 1 + n_w]
    out_ref = refs[-1]
    x_ref = xs[0]
    if n_x > 1:
        out_ref, x_ref = refs[-2:]
        for i in range(n_x):

            @pl.when(pl.program_id(0) == i)
            def _():
                x_ref[...] = xs[i][...]

    scale = HEAD_DIM ** (-0.5)
    width = w_refs[0].shape[-1]
    for c in range(3):
        acc = None
        k = 0
        for w_ref in w_refs:
            deep = w_ref.shape[2]
            for i in range(w_ref.shape[0]):
                off = pl.multiple_of(cols[k] * deep, 128)
                part = dot(x_ref[:, pl.ds(off, deep)], w_ref[i, c], 1, 0)
                acc = part if acc is None else acc + part
                k += 1
        if c == 0:
            acc = (acc + bias_ref[0:1, :].astype(F32)) * scale
        if c == 2:
            acc = acc + bias_ref[1:2, :].astype(F32)
        turned = acc.T.astype(BF16)
        for h in range(width // HEAD_DIM):
            out_ref[h, c] = turned[h * HEAD_DIM : (h + 1) * HEAD_DIM]


def project(xs, weights, cols, bias, perm, piece, base, rows, kept):
    width = xs[0].shape[1]
    count = sum(x.shape[0] for x in xs) // piece
    hw = weights[0].shape[-1]
    heads = hw // HEAD_DIM
    out_shape = [jax.ShapeDtypeStruct((heads, 3, HEAD_DIM, rows), BF16)]
    out_specs = [
        pl.BlockSpec((heads, 3, HEAD_DIM, piece), lambda r, p, c: (0, 0, 0, p[r + base]))
    ]
    x_specs = [pl.BlockSpec((piece, width), lambda r, p, c: (r, 0))]
    if len(xs) > 1:
        x_specs = [pl.BlockSpec((piece, width), lambda r, p, c: (0, 0))] * len(xs)
        out_shape.append(jax.ShapeDtypeStruct((rows, width), BF16))
        out_specs.append(pl.BlockSpec((piece, width), lambda r, p, c: (p[r + base], 0)))
    first = 3 + len(xs) + len(weights)
    return pl.pallas_call(
        functools.partial(qkv_kernel, n_x=len(xs), n_w=len(weights)),
        grid_spec=pltpu.PrefetchScalarGridSpec(
            num_scalar_prefetch=2,
            grid=(count,),
            in_specs=x_specs
            + [pl.BlockSpec(bias.shape, lambda r, p, c: (0, 0))]
            + [pl.BlockSpec(w.shape, lambda r, p, c: (0, 0, 0, 0)) for w in weights]
            + [pl.BlockSpec(memory_space=pl.ANY)] * len(kept),
            out_specs=out_specs,
        ),
        out_shape=out_shape,
        input_output_aliases={first + i: i for i in range(len(kept))},
        compiler_params=params(),
        cost_estimate=pl.CostEstimate(
            flops=8 * count * piece * width * 3 * hw, bytes_accessed=1, transcendentals=0
        ),
        name="project",
    )(perm, cols, *xs, bias, *weights, *kept)


def back_kernel(perm, cols, *refs, n_w):
    d_ref = refs[0]
    w_refs = refs[1 : 1 + n_w]
    out_refs = refs[1 + n_w : -2]
    proj_ref, sum_ref = refs[-2:]
    heads = d_ref.shape[0]
    r = pl.program_id(0)
    first = r == 0

    @pl.when(first)
    def _():
        sum_ref[...] = jnp.zeros_like(sum_ref)

    parts = []
    for c in range(3):
        flat = jnp.concatenate([d_ref[h, c] for h in range(heads)], axis=0)
        turned = flat.astype(F32).T
        if c != 1:
            row = c // 2
            sum_ref[row : row + 1, :] += jnp.sum(turned, axis=0, keepdims=True)
        turned = turned.astype(BF16)
        proj_ref[c] = turned
        parts.append(turned)
    k = 0
    for w_ref in w_refs:
        deep = w_ref.shape[2]
        for i in range(w_ref.shape[0]):
            acc = dot(parts[0], w_ref[i, 0], 1, 1)
            acc = acc + dot(parts[1], w_ref[i, 1], 1, 1)
            acc = acc + dot(parts[2], w_ref[i, 2], 1, 1)
            off = pl.multiple_of(cols[k] * deep, 128)
            low = acc.astype(BF16)
            for n, out_ref in enumerate(out_refs):

                @pl.when(r == n)
                def _():
                    out_ref[:, pl.ds(off, deep)] = low

            k += 1


def project_back(d_heads, weights, cols, perm, piece, width):
    heads, _, _, rows = d_heads.shape
    blocks = rows // piece
    hw = heads * HEAD_DIM
    return pl.pallas_call(
        functools.partial(back_kernel, n_w=len(weights)),
        grid_spec=pltpu.PrefetchScalarGridSpec(
            num_scalar_prefetch=2,
            grid=(blocks,),
            in_specs=[pl.BlockSpec((heads, 3, HEAD_DIM, piece), lambda r, p, c: (0, 0, 0, p[r]))]
            + [pl.BlockSpec(w.shape, lambda r, p, c: (0, 0, 0, 0)) for w in weights],
            out_specs=[pl.BlockSpec((piece, width), lambda r, p, c: (0, 0))] * blocks
            + [
                pl.BlockSpec((3, piece, hw), lambda r, p, c: (0, p[r], 0)),
                pl.BlockSpec((2, hw), lambda r, p, c: (0, 0)),
            ],
        ),
        out_shape=[jax.ShapeDtypeStruct((piece, width), BF16)] * blocks
        + [
            jax.ShapeDtypeStruct((3, rows, hw), BF16),
            jax.ShapeDtypeStruct((2, hw), F32),
        ],
        compiler_params=params(),
        cost_estimate=cost(2 * rows * width * 3 * hw, 2 * rows * width * 2 + 6 * width * hw),
        name="project_back",
    )(perm, cols, d_heads, *weights)


def tile_kernel_index(tiles, t, size, bq, bk, chunk):
    q0 = pl.multiple_of(tiles[1 + t] * bq, bq)
    k0 = pl.multiple_of(tiles[1 + size + t] * bk, bk)
    cj, kj = q0 // chunk, k0 // chunk
    off = pl.multiple_of(q0 - cj * chunk, bq)
    ko = pl.multiple_of(k0 - kj * chunk, bk)
    return q0, k0, cj, off, kj, ko, tiles[1 + 2 * size + t]


def inside(spot, pos, start, length):
    place = (spot + (pos - start)).astype(jnp.uint32)
    return place < length.astype(jnp.uint32)


def attend_kernel(
    tiles,
    qkv,
    start,
    length,
    low,
    high,
    lse,
    keys,
    acc,
    total,
    top,
    *,
    bq,
    bk,
    seq,
    chunk,
    piece,
    unroll,
    size,
):
    n_chunks = seq // chunk
    q_most = jnp.zeros((1, chunk), F32)
    k_most = jnp.zeros((1, chunk), F32)
    for j in range(n_chunks):
        q = qkv[j, 0].astype(F32)
        k = qkv[j, 1].astype(F32)
        q_most = jnp.maximum(q_most, jnp.sum(q * q, axis=0, keepdims=True))
        k_most = jnp.maximum(k_most, jnp.sum(k * k, axis=0, keepdims=True))
        keys[j * chunk : (j + 1) * chunk, :] = k.T.astype(BF16)
    calm = jnp.max(q_most) * jnp.max(k_most) < CALM * CALM
    acc[...] = jnp.zeros_like(acc)
    total[...] = jnp.zeros_like(total)
    spot = lax.broadcasted_iota(jnp.int32, (bk, bq), 0)

    def tile(t):
        q0, k0, cj, off, kj, ko, pos = tile_kernel_index(tiles, t, size, bq, bk, chunk)
        s = dot(keys[pl.ds(k0, bk), :], qkv[cj, 0, :, pl.ds(off, bq)], 1, 0)
        ok = inside(spot, pos, start[:, pl.ds(q0, bq)], length[:, pl.ds(q0, bq)])
        return q0, kj, ko, s, ok

    @pl.when(calm)
    def _():
        top[...] = jnp.zeros_like(top)

        def step(i, _):
            group = [tile(i * unroll + u) for u in range(unroll)]
            for q0, kj, ko, s, ok in group:
                p = jnp.where(ok, jnp.exp(s), 0.0)
                total[:, pl.ds(q0, bq)] += jnp.sum(p, axis=0, keepdims=True)
                value = qkv[kj, 2, :, pl.ds(ko, bk)]
                acc[:, pl.ds(q0, bq)] += dot(value, p.astype(BF16), 1, 0)
            return 0

        lax.fori_loop(0, tiles[0], step, 0)

    @pl.when(jnp.logical_not(calm))
    def _():
        top[...] = jnp.full_like(top, NEG)

        def step(i, _):
            q0, kj, ko, s, ok = tile(i)
            s = jnp.where(ok, s, NEG)
            here = pl.ds(q0, bq)
            new = jnp.maximum(top[:, here], jnp.max(s, axis=0, keepdims=True))
            p = jnp.where(ok, jnp.exp(s - new), 0.0)
            fade = jnp.exp(top[:, here] - new)
            total[:, here] = total[:, here] * fade + jnp.sum(p, axis=0, keepdims=True)
            value = qkv[kj, 2, :, pl.ds(ko, bk)]
            acc[:, here] = acc[:, here] * fade + dot(value, p.astype(BF16), 1, 0)
            top[:, here] = new
            return 0

        lax.fori_loop(0, tiles[0] * unroll, step, 0)

    lse[...] = top[...] + jnp.log(total[...])
    for z in range(n_chunks):
        for t in range(chunk // piece):
            base = z * chunk + t * piece
            out = acc[:, base : base + piece] / total[:, base : base + piece]
            low[t * n_chunks + z] = out.astype(BF16)
            high[t * n_chunks + z] = out


def attend(qkv, doc, tiles, piece, bq, bk, unroll):
    n_chunks, _, hd, chunk = qkv.shape
    seq = n_chunks * chunk
    start, end = doc
    pieces = seq // piece
    return pl.pallas_call(
        functools.partial(
            attend_kernel,
            bq=bq,
            bk=bk,
            seq=seq,
            chunk=chunk,
            piece=piece,
            unroll=unroll,
            size=(tiles.shape[0] - 1) // 3,
        ),
        grid_spec=pltpu.PrefetchScalarGridSpec(
            num_scalar_prefetch=1,
            grid=(),
            in_specs=[VMEM] * 3,
            out_specs=[VMEM] * 3,
            scratch_shapes=[
                pltpu.VMEM((seq, hd), BF16),
                pltpu.VMEM((hd, seq), F32),
                pltpu.VMEM((1, seq), F32),
                pltpu.VMEM((1, seq), F32),
            ],
        ),
        out_shape=[
            jax.ShapeDtypeStruct((pieces, hd, piece), BF16),
            jax.ShapeDtypeStruct((pieces, hd, piece), F32),
            jax.ShapeDtypeStruct((1, seq), F32),
        ],
        compiler_params=params(40),
        cost_estimate=cost(2 * seq * seq * hd, 8 * seq * hd, seq * seq // 4),
        name="attend",
    )(tiles, qkv, start[None], (end - start)[None])


def attend_back_kernel(
    tiles,
    qkv,
    start,
    length,
    lse,
    ctx,
    d_ctx,
    out,
    keys,
    values,
    queries,
    grads,
    d_keys,
    d_values,
    d_queries,
    delta,
    d_turned,
    *,
    bq,
    bk,
    seq,
    chunk,
    piece,
    unroll,
    size,
):
    n_chunks = seq // chunk
    for j in range(n_chunks):
        sl = slice(j * chunk, (j + 1) * chunk)
        queries[sl, :] = qkv[j, 0].astype(F32).T.astype(BF16)
        keys[sl, :] = qkv[j, 1].astype(F32).T.astype(BF16)
        values[sl, :] = qkv[j, 2].astype(F32).T.astype(BF16)
    for at in range(seq // piece):
        t, z = at // n_chunks, at % n_chunks
        base = z * chunk + t * piece
        part = d_ctx[at].astype(F32)
        d_turned[:, base : base + piece] = d_ctx[at]
        grads[base : base + piece, :] = part.T.astype(BF16)
        delta[:, base : base + piece] = jnp.sum(part * ctx[at], axis=0, keepdims=True)
    d_queries[...] = jnp.zeros_like(d_queries)
    d_keys[...] = jnp.zeros_like(d_keys)
    d_values[...] = jnp.zeros_like(d_values)
    spot = lax.broadcasted_iota(jnp.int32, (bk, bq), 0)

    def tile(t):
        q0, k0, cj, off, kj, ko, pos = tile_kernel_index(tiles, t, size, bq, bk, chunk)
        s = dot(keys[pl.ds(k0, bk), :], qkv[cj, 0, :, pl.ds(off, bq)], 1, 0)
        dp = dot(values[pl.ds(k0, bk), :], d_turned[:, pl.ds(q0, bq)], 1, 0)
        ok = inside(spot, pos, start[:, pl.ds(q0, bq)], length[:, pl.ds(q0, bq)])
        return q0, k0, kj, ko, s, dp, ok

    def step(i, _):
        group = [tile(i * unroll + u) for u in range(unroll)]
        for q0, k0, kj, ko, s, dp, ok in group:
            here = pl.ds(q0, bq)
            there = pl.ds(k0, bk)
            p = jnp.where(ok, jnp.exp(s - lse[:, here]), 0.0)
            ds = (p * (dp - delta[:, here])).astype(BF16)
            d_values[there, :] += dot(p.astype(BF16), grads[here, :], 1, 0)
            d_keys[there, :] += dot(ds, queries[here, :], 1, 0)
            d_queries[:, here] += dot(qkv[kj, 1, :, pl.ds(ko, bk)], ds, 1, 0)
        return 0

    lax.fori_loop(0, tiles[0], step, 0)
    scale = HEAD_DIM ** (-0.5)
    for j in range(n_chunks):
        sl = slice(j * chunk, (j + 1) * chunk)
        out[j, 0] = (d_queries[:, sl].astype(BF16).astype(F32) * scale).astype(BF16)
        out[j, 1] = d_keys[sl, :].T.astype(BF16)
        out[j, 2] = d_values[sl, :].T.astype(BF16)


def attend_back(qkv, doc, tiles, lse, ctx, d_ctx, piece, bq, bk, unroll):
    n_chunks, _, hd, chunk = qkv.shape
    seq = n_chunks * chunk
    start, end = doc
    return pl.pallas_call(
        functools.partial(
            attend_back_kernel,
            bq=bq,
            bk=bk,
            seq=seq,
            chunk=chunk,
            piece=piece,
            unroll=unroll,
            size=(tiles.shape[0] - 1) // 3,
        ),
        grid_spec=pltpu.PrefetchScalarGridSpec(
            num_scalar_prefetch=1,
            grid=(),
            in_specs=[VMEM] * 6,
            out_specs=VMEM,
            scratch_shapes=[pltpu.VMEM((seq, hd), BF16)] * 4
            + [pltpu.VMEM((seq, hd), F32)] * 2
            + [
                pltpu.VMEM((hd, seq), F32),
                pltpu.VMEM((1, seq), F32),
                pltpu.VMEM((hd, seq), BF16),
            ],
        ),
        out_shape=jax.ShapeDtypeStruct((n_chunks, 3, hd, chunk), BF16),
        compiler_params=params(48),
        cost_estimate=cost(4 * seq * seq * hd, 16 * seq * hd, seq * seq // 4),
        name="attend_back",
    )(tiles, qkv, start[None], (end - start)[None], lse, ctx, d_ctx)


def document_bounds(seg):
    ids = jnp.arange(DOCS, dtype=jnp.int32)[:, None]
    below = jnp.sum((seg[None] < ids).astype(jnp.int32), axis=1, keepdims=True)
    upto = jnp.sum((seg[None] <= ids).astype(jnp.int32), axis=1, keepdims=True)
    mine = seg[None] == ids
    start = jnp.sum(jnp.where(mine, below, 0), axis=0)
    end = jnp.sum(jnp.where(mine, upto, 0), axis=0)
    return start, end


def tile_list(start, end, bq, bk, unroll):
    n, m = start.shape[0] // bq, start.shape[0] // bk
    low = start.reshape(n, bq)[:, 0] // bk
    high = (end.reshape(n, bq)[:, -1] + bk - 1) // bk
    count = high - low
    order = jnp.arange(n)
    upto = jnp.sum(jnp.where(order[:, None] <= order[None], count[:, None], 0), axis=0)
    total = upto[-1]
    t = jnp.arange(n * m + unroll, dtype=jnp.int32)
    mine = jnp.minimum(jnp.sum((t[:, None] >= upto[None]).astype(jnp.int32), axis=1), n - 1)
    base = jnp.sum(jnp.where(mine[:, None] == order[None], (high - upto)[None], 0), axis=1)
    real = t < total
    key = jnp.where(real, base + t, 0)
    pos = jnp.where(real, key * bk, FAR)
    steps = (total + unroll - 1) // unroll
    return jnp.concatenate([steps[None], mine, key, pos]).astype(jnp.int32)


def norm_stats(value):
    center = value - jnp.mean(value, axis=-1, keepdims=True)
    rstd = lax.rsqrt(jnp.mean(center * center, axis=-1, keepdims=True) + EPSILON)
    return center * rstd, rstd


def norm_back(xhat, rstd, d_out, gain):
    scaled = d_out * gain
    m1 = jnp.mean(scaled, axis=-1, keepdims=True)
    m2 = jnp.mean(scaled * xhat, axis=-1, keepdims=True)
    return (scaled - m1 - xhat * m2) * rstd


def column(value):
    return jnp.sum(value, axis=0, keepdims=True)


def merge_kernel(perm, cols, ctx, x, vec, *refs):
    ws = refs[:-3]
    mixed_ref, normed_ref, low_ref = refs[-3:]
    halves, deep, wide = ws[0].shape
    parts = []
    for r in range(len(ws)):
        rows = pl.ds(pl.multiple_of(perm[r] * deep, deep), deep)
        parts.append(ctx[rows, :].astype(F32).T.astype(BF16))
    for s in range(halves):
        acc = dot(parts[0], ws[0][s], 1, 0)
        for r in range(1, len(ws)):
            acc = acc + dot(parts[r], ws[r][s], 1, 0)
        sl = pl.ds(pl.multiple_of(cols[s] * wide, 128), wide)
        mixed_ref[:, sl] = x[:, sl] + acc + vec[2:3, sl]
    xhat, _ = norm_stats(mixed_ref[...])
    normed = xhat * vec[0:1, :] + vec[3:4, :]
    normed_ref[...] = normed
    low_ref[...] = normed.astype(BF16)


def merge_specs(ws, layer):
    shape = ws[0].shape
    spec = pl.BlockSpec((shape[0], None) + shape[2:], lambda *_: (0, layer, 0, 0))
    return [spec] * len(ws)


def merge_norm(ctx, ws, layer, x, vec, perm, cols):
    rows, width = x.shape
    big = jax.ShapeDtypeStruct((rows, width), F32)
    return pl.pallas_call(
        merge_kernel,
        grid_spec=pltpu.PrefetchScalarGridSpec(
            num_scalar_prefetch=2,
            grid=(1,),
            in_specs=[VMEM] * 3 + merge_specs(ws, layer),
            out_specs=[VMEM] * 3,
        ),
        out_shape=[big, big, jax.ShapeDtypeStruct((rows, width), BF16)],
        compiler_params=params(),
        cost_estimate=cost(2 * rows * width * width, 2 * width * width + 16 * rows * width),
        name="merge_norm",
    )(perm, cols, ctx, x, vec, *ws)


def add_up(refs):
    total = refs[0][...].astype(F32)
    for ref in refs[1:]:
        total = total + ref[...].astype(F32)
    return total


def row_blocks(count, rows, width):
    block = rows
    return (rows // block,), [pl.BlockSpec((block, width), lambda r: (r, 0))] * count


def all_of(shape):
    return pl.BlockSpec(shape, lambda r: (0, 0))


def norm_kernel(vec, *refs, n_in):
    summed_ref, out_ref, low_ref = refs[n_in:]
    summed = add_up(refs[:n_in]) + vec[4:5, :]
    summed_ref[...] = summed
    xhat, _ = norm_stats(summed)
    out = xhat * vec[1:2, :] + vec[5:6, :]
    out_ref[...] = out
    low_ref[...] = out.astype(BF16)


def second_norm(vec, terms):
    shape = terms[0].shape
    big = jax.ShapeDtypeStruct(shape, F32)
    grid, specs = row_blocks(len(terms) + 3, *shape)
    return pl.pallas_call(
        functools.partial(norm_kernel, n_in=len(terms)),
        grid=grid,
        in_specs=[all_of(vec.shape)] + specs[3:],
        out_specs=specs[:3],
        out_shape=[big, big, jax.ShapeDtypeStruct(shape, BF16)],
        compiler_params=params(),
        cost_estimate=cost(20 * shape[0] * shape[1], 20 * shape[0] * shape[1]),
        name="second_norm",
    )(vec, *terms)


def second_back_math(vec, summed, d_out, d_ref, low_ref, sum_ref):
    xhat, rstd = norm_stats(summed)
    d_summed = norm_back(xhat, rstd, d_out, vec[1:2, :])
    d_ref[...] = d_summed
    low_ref[...] = d_summed.astype(BF16)

    @pl.when(pl.program_id(0) == 0)
    def _():
        sum_ref[...] = jnp.zeros_like(sum_ref)

    sum_ref[0:1, :] += column(d_out * xhat)
    sum_ref[1:2, :] += column(d_out)
    sum_ref[2:3, :] += column(d_summed)
    return xhat


def last_kernel(vec, d_out_ref, *refs, n_in):
    out_ref, d_ref, low_ref, sum_ref = refs[n_in:]
    summed = add_up(refs[:n_in]) + vec[4:5, :]
    d_out = d_out_ref[...].astype(F32)
    xhat = second_back_math(vec, summed, d_out, d_ref, low_ref, sum_ref)
    out_ref[...] = (xhat * vec[1:2, :] + vec[5:6, :]).astype(BF16)


def last_norm(vec, d_out, terms):
    rows, width = terms[0].shape
    low = jax.ShapeDtypeStruct((rows, width), BF16)
    grid, specs = row_blocks(len(terms) + 4, rows, width)
    return pl.pallas_call(
        functools.partial(last_kernel, n_in=len(terms)),
        grid=grid,
        in_specs=[all_of(vec.shape)] + specs[3:],
        out_specs=specs[:3] + [all_of((3, width))],
        out_shape=[
            low,
            jax.ShapeDtypeStruct((rows, width), F32),
            low,
            jax.ShapeDtypeStruct((3, width), F32),
        ],
        compiler_params=params(),
        cost_estimate=cost(40 * rows * width, 20 * rows * width),
        name="last_norm",
    )(vec, d_out, *terms)


def second_back_kernel(vec, summed_ref, *refs, n_in):
    d_ref, low_ref, sum_ref = refs[n_in:]
    second_back_math(vec, summed_ref[...], add_up(refs[:n_in]), d_ref, low_ref, sum_ref)


def second_back(vec, summed, terms):
    rows, width = summed.shape
    grid, specs = row_blocks(len(terms) + 3, rows, width)
    return pl.pallas_call(
        functools.partial(second_back_kernel, n_in=len(terms)),
        grid=grid,
        in_specs=[all_of(vec.shape)] + specs[2:],
        out_specs=specs[:2] + [all_of((3, width))],
        out_shape=[
            jax.ShapeDtypeStruct((rows, width), F32),
            jax.ShapeDtypeStruct((rows, width), BF16),
            jax.ShapeDtypeStruct((3, width), F32),
        ],
        compiler_params=params(),
        cost_estimate=cost(40 * rows * width, 20 * rows * width),
        name="second_back",
    )(vec, summed, *terms)


def first_back_kernel(perm, cols, vec, mixed_ref, *refs, n_w, n_in):
    ws = refs[:n_w]
    d_ref, low_ref, sum_ref, ctx_ref = refs[n_w + n_in :]
    d_out = add_up(refs[n_w : n_w + n_in])
    xhat, rstd = norm_stats(mixed_ref[...])
    d_mixed = norm_back(xhat, rstd, d_out, vec[0:1, :])
    d_ref[...] = d_mixed
    low_ref[...] = d_mixed.astype(BF16)
    sum_ref[0:1, :] = column(d_out * xhat)
    sum_ref[1:2, :] = column(d_out)
    sum_ref[2:3, :] = column(d_mixed)
    halves, deep, wide = ws[0].shape
    parts = []
    for s in range(halves):
        parts.append(low_ref[:, pl.ds(pl.multiple_of(cols[s] * wide, 128), wide)])
    for r in range(n_w):
        acc = dot(ws[r][0], parts[0], 1, 1)
        for s in range(1, halves):
            acc = acc + dot(ws[r][s], parts[s], 1, 1)
        rows = pl.ds(pl.multiple_of(perm[r] * deep, deep), deep)
        ctx_ref[rows, :] = acc.astype(BF16)


def first_back(vec, mixed, ws, layer, terms, perm, cols):
    rows, width = mixed.shape
    return pl.pallas_call(
        functools.partial(first_back_kernel, n_w=len(ws), n_in=len(terms)),
        grid_spec=pltpu.PrefetchScalarGridSpec(
            num_scalar_prefetch=2,
            grid=(1,),
            in_specs=[VMEM] * 2 + merge_specs(ws, layer) + [VMEM] * len(terms),
            out_specs=[VMEM] * 4,
        ),
        out_shape=[
            jax.ShapeDtypeStruct((rows, width), F32),
            jax.ShapeDtypeStruct((rows, width), BF16),
            jax.ShapeDtypeStruct((3, width), F32),
            jax.ShapeDtypeStruct((width, rows), BF16),
        ],
        compiler_params=params(),
        cost_estimate=cost(2 * rows * width * width, 2 * width * width + 20 * rows * width),
        name="first_back",
    )(perm, cols, vec, mixed, *ws, *terms)


ERF_TOP = (
    -2.72614225801306e-10,
    2.77068142495902e-08,
    -2.10102402082508e-06,
    -5.69250639462346e-05,
    -7.34990630326855e-04,
    -2.95459980854025e-03,
    -1.60960333262415e-02,
)
ERF_BOTTOM = (
    -1.45660718464996e-05,
    -2.13374055278905e-04,
    -1.68282697438203e-03,
    -7.37332916720468e-03,
    -1.42647390514189e-02,
)


def erf(value):
    x = jnp.clip(value, -4.0, 4.0)
    sq = x * x
    top = jnp.full_like(x, ERF_TOP[0])
    for c in ERF_TOP[1:]:
        top = top * sq + c
    bottom = jnp.full_like(x, ERF_BOTTOM[0])
    for c in ERF_BOTTOM[1:]:
        bottom = bottom * sq + c
    return x * top / bottom


def up_kernel(*refs, n, fc):
    xs = refs[:n]
    up, bias, down = refs[n : n + 3]
    outs = refs[-3 - n : -3]
    cat_ref, act_ref, slope_ref = refs[-3:]
    piece = xs[0].shape[0]
    for i in range(n):
        cat_ref[i * piece : (i + 1) * piece, :] = xs[i][...]

    halves, deep, hidden = up.shape
    for f in range(0, hidden, fc):
        fs = slice(f, f + fc)
        u = dot(cat_ref[:, :deep], up[0, :, fs], 1, 0)
        for s in range(1, halves):
            u = u + dot(cat_ref[:, s * deep : (s + 1) * deep], up[s, :, fs], 1, 0)
        u = u + bias[:, fs].astype(F32)
        phi = 0.5 + 0.5 * erf(u * (0.5**0.5))
        act_ref[:, fs] = (u * phi).astype(BF16)
        slope = phi + u * (jnp.exp(-0.5 * u * u) * 0.3989422804014327)
        slope_ref[:, fs] = slope.astype(BF16)
    for s in range(halves):
        out = dot(act_ref[...], down[s], 1, 0).astype(BF16)
        for i in range(n):
            outs[i][:, s * deep : (s + 1) * deep] = out[i * piece : (i + 1) * piece]


def ff_specs(n, piece, width, hidden, base):
    whole = pl.BlockSpec((piece, width), lambda r: (0, 0))
    flat = pl.BlockSpec((n * piece, width), lambda r: (base // n, 0))
    tall = pl.BlockSpec((n * piece, hidden), lambda r: (base // n, 0))
    return whole, flat, tall


def feed_forward(xs, up, bias, down, fc, base, rows, kept):
    n = len(xs)
    piece, width = xs[0].shape
    hidden = up.shape[2]
    whole, flat, tall = ff_specs(n, piece, width, hidden, base)
    got = pl.pallas_call(
        functools.partial(up_kernel, n=n, fc=fc),
        grid=(1,),
        in_specs=[whole] * n
        + [
            pl.BlockSpec(up.shape, lambda r: (0, 0, 0)),
            pl.BlockSpec((1, hidden), lambda r: (0, 0)),
            pl.BlockSpec(down.shape, lambda r: (0, 0, 0)),
        ]
        + [pl.BlockSpec(memory_space=pl.ANY)] * len(kept),
        out_specs=[whole] * n + [flat, tall, tall],
        out_shape=[jax.ShapeDtypeStruct((piece, width), BF16)] * n
        + [jax.ShapeDtypeStruct((rows, w), BF16) for w in (width, hidden, hidden)],
        input_output_aliases={n + 3 + i: n + i for i in range(len(kept))},
        compiler_params=params(),
        cost_estimate=pl.CostEstimate(
            flops=16 * n * piece * width * hidden, bytes_accessed=1, transcendentals=0
        ),
        name="feed_forward",
    )(*xs, up, bias, down, *kept)
    return list(got[:n]), list(got[n:])


def down_kernel(*refs, n, fc):
    ds = refs[:n]
    slope_ref, up, down = refs[n : n + 3]
    outs = refs[-3 - n : -3]
    cat_ref, du_ref, sum_ref = refs[-3:]
    piece = ds[0].shape[0]
    for i in range(n):
        cat_ref[i * piece : (i + 1) * piece, :] = ds[i][...]
    halves, deep, hidden = up.shape
    for f in range(0, hidden, fc):
        fs = slice(f, f + fc)
        d = dot(cat_ref[:, :deep], down[0, fs, :], 1, 1)
        for s in range(1, halves):
            d = d + dot(cat_ref[:, s * deep : (s + 1) * deep], down[s, fs, :], 1, 1)
        du = (d * slope_ref[:, fs].astype(F32)).astype(BF16)
        du_ref[:, fs] = du
        sum_ref[:, fs] = column(du.astype(F32))
    for s in range(halves):
        out = dot(du_ref[...], up[s], 1, 1).astype(BF16)
        for i in range(n):
            outs[i][:, s * deep : (s + 1) * deep] = out[i * piece : (i + 1) * piece]


def feed_back(ds, slope, up, down, fc, base, kept, filler):
    n = len(ds)
    piece, width = ds[0].shape
    rows, hidden = slope.shape
    whole, flat, tall = ff_specs(n, piece, width, hidden, base)
    got = pl.pallas_call(
        functools.partial(down_kernel, n=n, fc=fc),
        grid=(1,),
        in_specs=[whole] * n
        + [
            tall,
            pl.BlockSpec(up.shape, lambda r: (0, 0, 0)),
            pl.BlockSpec(down.shape, lambda r: (0, 0, 0)),
        ]
        + [pl.BlockSpec(memory_space=pl.ANY)] * len(kept),
        out_specs=[whole] * n + [flat, tall, pl.BlockSpec((1, hidden), lambda r: (0, 0))],
        out_shape=[jax.ShapeDtypeStruct((piece, width), BF16)] * n
        + [jax.ShapeDtypeStruct((rows, w), BF16) for w in (width, hidden)]
        + [jax.ShapeDtypeStruct((1, hidden), F32)],
        input_output_aliases={n + 3 + i: n + i for i in range(len(kept))},
        compiler_params=params(),
        cost_estimate=pl.CostEstimate(
            flops=16 * n * piece * width * hidden if filler else 1,
            bytes_accessed=1,
            transcendentals=0,
        ),
        name="feed_back",
    )(*ds, slope, up, down, *kept)
    return list(got[:n]), list(got[n : n + 2]), got[n + 2]


def place_kernel(perm, *refs):
    out = refs[-1]
    for i, ref in enumerate(refs[:-1]):

        @pl.when(pl.program_id(0) == i)
        def _():
            out[...] = ref[...].astype(out.dtype)


def place(blocks, perm, dtype):
    piece, width = blocks[0].shape
    n = len(blocks)
    return pl.pallas_call(
        place_kernel,
        grid_spec=pltpu.PrefetchScalarGridSpec(
            num_scalar_prefetch=1,
            grid=(n,),
            in_specs=[pl.BlockSpec((piece, width), lambda r, p: (0, 0))] * n,
            out_specs=pl.BlockSpec((piece, width), lambda r, p: (p[r], 0)),
        ),
        out_shape=jax.ShapeDtypeStruct((n * piece, width), dtype),
        compiler_params=params(),
        cost_estimate=cost(n * piece * width, 6 * n * piece * width),
        name="place",
    )(perm, *blocks)


def store_kernel(*refs, n):
    for source, target in zip(refs[-2 * n : -n], refs[-n:]):
        target[...] = source[...].astype(F32)


def part_specs(joined, first, rows, width, runs, layer):
    wide = joined.shape[1]
    chunk = min(wide, width)
    own, whole, start = runs
    stride = rows if width >= wide else rows * width // wide
    block = math.gcd(math.gcd(math.gcd(stride, 256), first), math.gcd(own, start))
    down = rows // block
    steps = down * (width // chunk)

    def spot(t):
        t = jnp.minimum(t, steps - 1)
        return t % down, t // down

    def source(t):
        i, j = spot(t)
        row = j * rows + i * block
        side = 0
        if width < wide:
            row, side = i * block % stride, i * block // stride
        row = first + row
        return ((row // own * whole + start + row % own) // block, side)

    def target(t):
        i, j = spot(t)
        return (layer, i, j)

    return (
        steps,
        pl.BlockSpec((block, chunk), source),
        pl.BlockSpec((None, block, chunk), target),
    )


def store(buffers, items, layer, layers):
    n = len(items)
    parts = [part_specs(*item, layer) for item in items]
    return pl.pallas_call(
        functools.partial(store_kernel, n=n),
        grid=(max(part[0] for part in parts),),
        in_specs=[pl.BlockSpec(memory_space=pl.ANY)] * len(buffers) + [p[1] for p in parts],
        out_specs=[p[2] for p in parts],
        out_shape=[jax.ShapeDtypeStruct((layers, item[2], item[3]), F32) for item in items],
        input_output_aliases={i: i for i in range(len(buffers))},
        compiler_params=params(32),
        cost_estimate=cost(1, 1),
        name="store",
    )(*buffers, *[item[0] for item in items])


def swap(value, axis, count, bit):
    return lax.ppermute(value, axis, [(i, i ^ bit) for i in range(count)])


def spread(own, count):
    one = swap(own, "tensor", count, 1)
    two = swap(own, "tensor", count, 2)
    return [own, one, two, swap(two, "tensor", count, 1)]


def collect(blocks, count):
    three = swap(blocks[3], "tensor", count, 1)
    far = (blocks[2].astype(F32) + three.astype(F32)).astype(BF16)
    two = swap(far, "tensor", count, 2)
    return [blocks[0], swap(blocks[1], "tensor", count, 1), two]


def ordered(parts, index, bits):
    for bit in bits:
        flip = (index & bit) != 0
        parts = [jnp.where(flip, parts[i ^ bit], parts[i]) for i in range(len(parts))]
    return parts


def sum_all(value, axis, count):
    bit = 1
    while bit < count:
        value = value + swap(value, axis, count, bit)
        bit *= 2
    return value


BQ, BK, UNROLL = 256, 512, 4
BQ_BACK, BK_BACK, UNROLL_BACK = 256, 256, 4


def build(n_shard, n_context, n_tensor):
    def shards(
        hidden_in,
        segment_ids,
        cotangent,
        qkv_weight,
        merge_weight,
        up_weight,
        down_weight,
        row_gains,
        row_bias,
        head_bias,
        up_bias,
    ):
        layers = qkv_weight.shape[0]
        rows, width = hidden_in.shape
        piece = rows // n_tensor
        deep = width // n_shard
        me_s = lax.axis_index(SHARD)
        me_t = lax.axis_index("tensor")
        order = jnp.arange(n_tensor, dtype=jnp.int32)
        relative = order ^ me_t.astype(jnp.int32)
        cols_all = jnp.arange(n_shard, dtype=jnp.int32)
        cols_rel = cols_all ^ me_s.astype(jnp.int32)

        w_in = jnp.transpose(qkv_weight, (0, 2, 1, 3))
        first = [w_in[0:1]]
        for bit in range(1, n_shard):
            first.append(swap(w_in[0:1], SHARD, n_shard, bit))
        tables = jnp.concatenate([row_gains, row_bias], axis=1)
        w_in = [w_in[layer] for layer in range(layers)]
        up_weight = [up_weight[layer] for layer in range(layers)]
        down_weight = [down_weight[layer] for layer in range(layers)]
        up_weight, segment_ids = lax.optimization_barrier((up_weight, segment_ids))
        segs = [segment_ids[0]]
        for bit in range(1, n_context):
            segs.append(swap(segment_ids[0], CONTEXT, n_context, bit))
        first, segs, tables, merge_weight, up_weight, down_weight, w_in = (
            lax.optimization_barrier(
                (first, segs, tables, merge_weight, up_weight, down_weight, w_in)
            )
        )
        parts = [merge_weight]
        tabs = [tables]
        for bit in range(1, n_shard):
            parts.append(swap(merge_weight, SHARD, n_shard, bit))
            tabs.append(swap(tables, SHARD, n_shard, bit))
        bits = [1 << i for i in range(n_context.bit_length() - 1)]
        seg = jnp.concatenate(ordered(segs, lax.axis_index(CONTEXT), bits))
        doc = document_bounds(seg)
        tiles = tile_list(*doc, BQ, BK, UNROLL)
        tiles_back = tile_list(*doc, BQ_BACK, BK_BACK, UNROLL_BACK)
        w_qkv, cols = [first], [cols_rel]
        x_own = lax.dynamic_slice_in_dim(hidden_in, me_t * piece, piece, 0).astype(F32)
        d_last = lax.dynamic_slice_in_dim(cotangent, me_t * piece, piece, 0)
        xs = [hidden_in]
        x_nat = hidden_in
        saved = []
        for layer in range(layers):
            args = (w_qkv[layer], cols[layer], head_bias[layer])
            if layer == 0:
                got = list(project(xs, *args, order, piece, 0, rows, []))
            else:
                near = [x_low, swap(x_low, "tensor", n_tensor, 1)]
                far = swap(x_low, "tensor", n_tensor, 2)
                got = list(project(near, *args, relative, piece, 0, rows, []))
                far, got = lax.optimization_barrier((far, got))
                far = [far, swap(far, "tensor", n_tensor, 1)]
                got = list(project(far, *args, relative, piece, 2, rows, got))
            if layer == 0:
                got[0], up_weight, down_weight, w_in = lax.optimization_barrier(
                    (got[0], up_weight, down_weight, w_in)
                )
                pair = jnp.stack(parts)
                far = swap(pair, "tensor", n_tensor, 2)
                bits = [1 << i for i in range(n_shard.bit_length() - 1)]
                vec = jnp.concatenate(ordered(tabs, me_s, bits), axis=2).astype(F32)
                w_up, w_down = [], []
                for i in range(layers):
                    if i > 0:
                        w_qkv.append([lax.all_gather(w_in[i], SHARD, axis=0, tiled=False)])
                        cols.append(cols_all)
                    w_up.append(lax.all_gather(up_weight[i], SHARD, axis=0, tiled=False))
                    w_down.append(lax.all_gather(down_weight[i], SHARD, axis=0, tiled=False))
            else:
                x_nat = got[1]
            qkv = lax.all_to_all(got[0], CONTEXT, 0, 0, tiled=True)
            ctx_low, ctx, lse = attend(qkv, doc, tiles, piece, BQ, BK, UNROLL)
            if layer == 0:
                ctx_low, far, pair = lax.optimization_barrier((ctx_low, far, pair))
                w_merge = [pair, swap(pair, "tensor", n_tensor, 1)]
                w_merge += [far, swap(far, "tensor", n_tensor, 1)]
            mine = lax.all_to_all(ctx_low, ("tensor", CONTEXT), 0, 0, tiled=True)
            mine = mine.reshape(width, piece)
            mixed, normed, low = merge_norm(
                mine, w_merge, layer, x_own, vec[layer], relative, cols_rel
            )
            ff_args = (w_up[layer], up_bias[layer : layer + 1], w_down[layer], 512)
            far = swap(low, "tensor", n_tensor, 2)
            near = [low, swap(low, "tensor", n_tensor, 1)]
            blocks, kept = feed_forward(near, *ff_args, 0, rows, [])
            far, kept = lax.optimization_barrier((far, kept))
            far = [far, swap(far, "tensor", n_tensor, 1)]
            got, kept = feed_forward(far, *ff_args, 2, rows, kept)
            blocks += got
            x1, act, slope = kept
            terms = [normed] + collect(blocks, n_tensor)
            keep = [x_nat, qkv, ctx, lse, mine, mixed, x1, act, slope]
            if layer + 1 < layers:
                terms, w_qkv[1] = lax.optimization_barrier((terms, w_qkv[1]))
                summed, x_own, x_low = second_norm(vec[layer], terms)
                keep.append(summed)
            else:
                out_low, d_summed, d_low, sums = last_norm(vec[layer], d_last, terms)
            saved.append(keep)

        def send_parts(make):
            return [make(me_s ^ bit).astype(BF16) for bit in range(1, n_shard)]

        def exchange(parts):
            return [swap(p, SHARD, n_shard, i + 1) for i, p in enumerate(parts)]

        def settle(make, got):
            total = make(me_s)
            for part in got:
                total = total + part.astype(F32)
            return total.astype(BF16)

        def context_scatter(value):
            return lax.psum_scatter(value, CONTEXT, scatter_dimension=0, tiled=True)

        def context_gather(value):
            return lax.all_gather(value, CONTEXT, axis=0, tiled=True)

        def chunks(value, wide):
            return [value[:, i : i + wide] for i in range(0, value.shape[1], wide)]

        def join_wide(g_down, g_up):
            return jnp.concatenate(g_down + chunks(g_up, deep), axis=0)

        def join_narrow(g_qkv, g_merge):
            flat = g_qkv.reshape(-1, g_qkv.shape[2])
            if deep > flat.shape[1]:
                part = flat.shape[0] * flat.shape[1] // deep
                sides = [flat[i : i + part] for i in range(0, flat.shape[0], part)]
                flat = jnp.concatenate(sides, axis=1)
            return jnp.concatenate(chunks(flat, deep) + [g_merge], axis=0)

        tie = lax.optimization_barrier
        grads = [None] * layers
        rowsums, sides = [None] * layers, [None] * layers
        terms = None
        hidden_out = None
        deep_t = width // n_tensor
        late, wide, narrow = (), (), ()
        for layer in reversed(range(layers)):
            last = layer + 1 == layers
            x_nat, qkv, ctx, lse, mine, mixed, x1, act, slope = saved[layer][:9]
            if not last:
                d_summed, d_low, sums = second_back(vec[layer], saved[layer][9], terms)
            ff_args = (slope, w_up[layer], w_down[layer], 512)
            far = swap(d_low, "tensor", n_tensor, 2)
            near = [d_low, swap(d_low, "tensor", n_tensor, 1)]
            if not last:
                near, wide = tie((near, jnp.concatenate(wide, axis=0)))
                wide = context_gather(wide)
            blocks, kept, g_hidden = feed_back(near, *ff_args, 0, [], last)
            far, kept = tie((far, kept))
            far = [far, swap(far, "tensor", n_tensor, 1)]
            got, kept, part = feed_back(far, *ff_args, 2, kept, last)
            blocks += got
            blocks, late = tie((blocks, late))
            g_hidden = g_hidden + part
            dy, du = kept

            def down_part(i, act=act, dy=dy):
                return dot(act, lax.dynamic_slice_in_dim(dy, i * deep, deep, 1), 0, 0)

            def up_part(i, x1=x1, du=du):
                return dot(lax.dynamic_slice_in_dim(x1, i * deep, deep, 1), du, 0, 0)

            terms = [d_summed] + collect(blocks, n_tensor)
            down_send, up_send = send_parts(down_part), send_parts(up_part)
            terms, down_send, up_send, wide = tie((terms, down_send, up_send, wide))
            down_got, up_got = exchange(down_send), exchange(up_send)
            d_mixed, d_low, sums_one, d_mine = first_back(
                vec[layer], mixed, w_merge, layer, terms, relative, cols_rel
            )
            if not last:
                narrow = join_narrow(settle(makers[0], late[0]), settle(makers[1], late[1]))
                narrow = context_scatter(narrow)
            pieces = d_mine.reshape(n_tensor * n_context, HEAD_DIM, piece)
            d_ctx = lax.all_to_all(pieces, ("tensor", CONTEXT), 0, 0, tiled=True)
            g_blocks = []
            for r in range(n_tensor):
                part = lax.dynamic_slice_in_dim(mine, relative[r] * deep_t, deep_t, 0)
                g_blocks.append(dot(part, d_low, 1, 0).astype(BF16))
            g_down = settle(down_part, down_got) if last else ()
            d_ctx, g_blocks, narrow, down_got, g_down, out_low = tie(
                (d_ctx, g_blocks, narrow, down_got, g_down, out_low)
            )
            if last:
                out_low = [out_low, swap(out_low, "tensor", n_tensor, 2)]
                g_down = context_scatter(g_down)
            else:
                narrow = context_gather(narrow)
            d_heads = attend_back(
                qkv, doc, tiles_back, lse, ctx, d_ctx, piece, BQ_BACK, BK_BACK, UNROLL_BACK
            )
            d_heads, down_got, up_got, g_blocks, g_down, out_low, narrow = tie(
                (d_heads, down_got, up_got, g_blocks, g_down, out_low, narrow)
            )
            d_heads = lax.all_to_all(d_heads, CONTEXT, 0, 0, tiled=True)
            g_terms = collect(g_blocks, n_tensor)
            g_merge = sum(term.astype(F32) for term in g_terms).astype(BF16)
            g_up = settle(up_part, up_got)
            if last:
                new_wide = join_wide([], g_up)
            else:
                new_wide = join_wide([settle(down_part, down_got)], g_up)
            if last:
                near = [swap(v, "tensor", n_tensor, 1) for v in out_low]
                out_low = [out_low[0], near[0], out_low[1], near[1]]
                hidden_out = place(out_low, relative, BF16)
            d_heads, new_wide, g_merge, narrow, hidden_out = tie(
                (d_heads, new_wide, g_merge, narrow, hidden_out)
            )
            new_wide = context_scatter(new_wide)
            if last:
                new_wide = [g_down, new_wide]
            got = project_back(d_heads, w_qkv[layer], cols[layer], relative, piece, width)
            d_x, d_proj, g_heads = got[:n_tensor], got[n_tensor], got[n_tensor + 1]

            def merge_part(i, g_merge=g_merge):
                return lax.dynamic_slice_in_dim(g_merge, i * deep, deep, 1).astype(F32)

            def qkv_part(i, x_nat=x_nat, d_proj=d_proj):
                d = lax.dynamic_slice_in_dim(x_nat, i * deep, deep, 1)
                return jnp.einsum("rd,crj->cdj", d, d_proj, preferred_element_type=F32)

            qkv_send, merge_send = send_parts(qkv_part), send_parts(merge_part)
            terms = [d_mixed] + collect(d_x, n_tensor)
            if layer > 0:
                terms, qkv_send, merge_send = tie((terms, qkv_send, merge_send))

            if not last:
                grads[layer + 1] = (wide, narrow)
            late = (exchange(qkv_send), exchange(merge_send))
            makers = (qkv_part, merge_part)
            wide, narrow = new_wide, ()
            rowsums[layer] = jnp.concatenate([sums_one, sums], axis=0)
            sides[layer] = jnp.concatenate([g_heads.reshape(-1), g_hidden.reshape(-1)])
        total = terms[0]
        for term in terms[1:]:
            total = total + term.astype(F32)
        narrow = join_narrow(settle(makers[0], late[0]), settle(makers[1], late[1]))
        total = total.astype(BF16)
        wide, narrow = tie((wide, narrow))
        blocks = spread(total, n_tensor)
        table = sum_all(jnp.concatenate(rowsums, axis=0), "tensor", n_tensor)
        side = jnp.concatenate(sides).reshape(-1, width)
        packed = jnp.concatenate([table, side], axis=0)
        packed = sum_all(packed, SHARD, n_shard)
        packed = sum_all(packed, CONTEXT, n_context)
        narrow = context_scatter(narrow)
        blocks, packed = tie((blocks, packed))
        grads[0] = context_gather(jnp.concatenate([wide, narrow], axis=0))
        input_grad = place(blocks, relative, F32)
        hw = width // n_tensor
        hidden = up_bias.shape[1]
        stored = []
        n_qkv = 3 * deep * hw // deep
        n_narrow = n_qkv + hw
        run_w, run_n = 2 * hidden // n_context, n_narrow // n_context
        for layer in reversed(range(layers)):
            if layer == 0:
                wide = narrow = grads[0]
                runs_d = runs_u = (run_w, run_w + run_n, 0)
                runs_n = (run_n, run_w + run_n, run_w)
                second = hidden
            else:
                wide, narrow = grads[layer]
                runs_d = runs_u = runs_n = (1 << 20, 0, 0)
                second = hidden
                if layer + 1 == layers:
                    run = hidden // n_context
                    runs_d, runs_u, second = (run, 2 * run, 0), (run, 2 * run, run), 0
                runs_n = (n_narrow, 0, 0)
            items = [
                (wide, 0, hidden, deep, runs_d),
                (wide, second, deep, hidden, runs_u),
                (narrow, 0, 3 * deep, hw, runs_n),
                (narrow, n_qkv, hw, deep, runs_n),
            ]
            stored = store(stored, items, layer, layers)
        g_down, g_up, g_qkv, g_merge = stored
        g_qkv = g_qkv.reshape(layers, 3, deep, -1)

        table = packed[: layers * 6].reshape(layers, 6, width)
        table = lax.dynamic_slice_in_dim(table, me_s * deep, deep, 2)
        side = packed[layers * 6 :].reshape(layers, -1)
        head_count = 2 * head_bias.shape[2]
        grad_gains = table[:, 0::3]
        grad_shifts = table[:, jnp.array([2, 1, 5, 4])]
        grad_heads = side[:, :head_count].reshape(head_bias.shape)
        grad_hidden = side[:, head_count:]
        return (
            hidden_out,
            input_grad,
            jnp.transpose(g_qkv, (0, 2, 1, 3)),
            g_merge,
            g_up,
            g_down,
            grad_gains,
            grad_shifts,
            grad_heads,
            grad_hidden,
        )

    return shards


def solution(mesh):
    tokens = (SHARD, CONTEXT)
    weights = (
        P(None, SHARD, None, "tensor"),
        P(None, "tensor", SHARD),
        P(None, SHARD, "tensor"),
        P(None, "tensor", SHARD),
        P(None, None, SHARD),
        P(None, None, SHARD),
        P(None, None, "tensor"),
        P(None, "tensor"),
    )
    return jax.shard_map(
        build(mesh.shape[SHARD], mesh.shape[CONTEXT], mesh.shape["tensor"]),
        mesh=mesh,
        in_specs=(P(tokens, None), P(*tokens), P(tokens, None)) + weights,
        out_specs=(P(tokens, None), P(tokens, None)) + weights,
        check_vma=False,
    )
```

```python
import functools
import math

import jax
import jax.numpy as jnp
from jax import lax
from jax.experimental import pallas as pl
from jax.experimental.pallas import tpu as pltpu
from jax.sharding import PartitionSpec as P

HEAD_DIM = 64
DOCS = 16
NEG = -1e30
EPSILON = 1e-05
CALM = 75.0
FAR = 1 << 24
F32 = jnp.float32
BF16 = jnp.bfloat16
SHARD = "shard"
CONTEXT = "context"
VMEM = pl.BlockSpec(memory_space=pltpu.VMEM)


def dot(a, b, ca, cb):
    return lax.dot_general(a, b, (((ca,), (cb,)), ((), ())), preferred_element_type=F32)


def params(mib=56):
    return pltpu.CompilerParams(vmem_limit_bytes=mib << 20)


def cost(flops, nbytes, trans=0):
    return pl.CostEstimate(flops=1, bytes_accessed=1, transcendentals=0)


def qkv_kernel(perm, cols, *refs, n_x, n_w):
    xs, bias_ref = refs[:n_x], refs[n_x]
    w_refs = refs[n_x + 1 : n_x + 1 + n_w]
    out_ref = refs[-1]
    x_ref = xs[0]
    if n_x > 1:
        out_ref, x_ref = refs[-2:]
        for i in range(n_x):

            @pl.when(pl.program_id(0) == i)
            def _():
                x_ref[...] = xs[i][...]

    scale = HEAD_DIM ** (-0.5)
    width = w_refs[0].shape[-1]
    for c in range(3):
        acc = None
        k = 0
        for w_ref in w_refs:
            deep = w_ref.shape[2]
            for i in range(w_ref.shape[0]):
                off = pl.multiple_of(cols[k] * deep, 128)
                part = dot(x_ref[:, pl.ds(off, deep)], w_ref[i, c], 1, 0)
                acc = part if acc is None else acc + part
                k += 1
        if c == 0:
            acc = (acc + bias_ref[0:1, :].astype(F32)) * scale
        if c == 2:
            acc = acc + bias_ref[1:2, :].astype(F32)
        turned = acc.T.astype(BF16)
        for h in range(width // HEAD_DIM):
            out_ref[h, c] = turned[h * HEAD_DIM : (h + 1) * HEAD_DIM]


def project(xs, weights, cols, bias, perm, piece, base, rows, kept):
    width = xs[0].shape[1]
    count = sum(x.shape[0] for x in xs) // piece
    hw = weights[0].shape[-1]
    heads = hw // HEAD_DIM
    out_shape = [jax.ShapeDtypeStruct((heads, 3, HEAD_DIM, rows), BF16)]
    out_specs = [
        pl.BlockSpec((heads, 3, HEAD_DIM, piece), lambda r, p, c: (0, 0, 0, p[r + base]))
    ]
    x_specs = [pl.BlockSpec((piece, width), lambda r, p, c: (r, 0))]
    if len(xs) > 1:
        x_specs = [pl.BlockSpec((piece, width), lambda r, p, c: (0, 0))] * len(xs)
        out_shape.append(jax.ShapeDtypeStruct((rows, width), BF16))
        out_specs.append(pl.BlockSpec((piece, width), lambda r, p, c: (p[r + base], 0)))
    first = 3 + len(xs) + len(weights)
    return pl.pallas_call(
        functools.partial(qkv_kernel, n_x=len(xs), n_w=len(weights)),
        grid_spec=pltpu.PrefetchScalarGridSpec(
            num_scalar_prefetch=2,
            grid=(count,),
            in_specs=x_specs
            + [pl.BlockSpec(bias.shape, lambda r, p, c: (0, 0))]
            + [pl.BlockSpec(w.shape, lambda r, p, c: (0, 0, 0, 0)) for w in weights]
            + [pl.BlockSpec(memory_space=pl.ANY)] * len(kept),
            out_specs=out_specs,
        ),
        out_shape=out_shape,
        input_output_aliases={first + i: i for i in range(len(kept))},
        compiler_params=params(),
        cost_estimate=pl.CostEstimate(
            flops=8 * count * piece * width * 3 * hw, bytes_accessed=1, transcendentals=0
        ),
        name="project",
    )(perm, cols, *xs, bias, *weights, *kept)


def back_kernel(perm, cols, *refs, n_w):
    d_ref = refs[0]
    w_refs = refs[1 : 1 + n_w]
    out_refs = refs[1 + n_w : -2]
    proj_ref, sum_ref = refs[-2:]
    heads = d_ref.shape[0]
    r = pl.program_id(0)
    first = r == 0

    @pl.when(first)
    def _():
        sum_ref[...] = jnp.zeros_like(sum_ref)

    parts = []
    for c in range(3):
        flat = jnp.concatenate([d_ref[h, c] for h in range(heads)], axis=0)
        turned = flat.astype(F32).T
        if c != 1:
            row = c // 2
            sum_ref[row : row + 1, :] += jnp.sum(turned, axis=0, keepdims=True)
        turned = turned.astype(BF16)
        proj_ref[c] = turned
        parts.append(turned)
    k = 0
    for w_ref in w_refs:
        deep = w_ref.shape[2]
        for i in range(w_ref.shape[0]):
            acc = dot(parts[0], w_ref[i, 0], 1, 1)
            acc = acc + dot(parts[1], w_ref[i, 1], 1, 1)
            acc = acc + dot(parts[2], w_ref[i, 2], 1, 1)
            off = pl.multiple_of(cols[k] * deep, 128)
            low = acc.astype(BF16)
            for n, out_ref in enumerate(out_refs):

                @pl.when(r == n)
                def _():
                    out_ref[:, pl.ds(off, deep)] = low

            k += 1


def project_back(d_heads, weights, cols, perm, piece, width):
    heads, _, _, rows = d_heads.shape
    blocks = rows // piece
    hw = heads * HEAD_DIM
    return pl.pallas_call(
        functools.partial(back_kernel, n_w=len(weights)),
        grid_spec=pltpu.PrefetchScalarGridSpec(
            num_scalar_prefetch=2,
            grid=(blocks,),
            in_specs=[pl.BlockSpec((heads, 3, HEAD_DIM, piece), lambda r, p, c: (0, 0, 0, p[r]))]
            + [pl.BlockSpec(w.shape, lambda r, p, c: (0, 0, 0, 0)) for w in weights],
            out_specs=[pl.BlockSpec((piece, width), lambda r, p, c: (0, 0))] * blocks
            + [
                pl.BlockSpec((3, piece, hw), lambda r, p, c: (0, p[r], 0)),
                pl.BlockSpec((2, hw), lambda r, p, c: (0, 0)),
            ],
        ),
        out_shape=[jax.ShapeDtypeStruct((piece, width), BF16)] * blocks
        + [
            jax.ShapeDtypeStruct((3, rows, hw), BF16),
            jax.ShapeDtypeStruct((2, hw), F32),
        ],
        compiler_params=params(),
        cost_estimate=cost(2 * rows * width * 3 * hw, 2 * rows * width * 2 + 6 * width * hw),
        name="project_back",
    )(perm, cols, d_heads, *weights)


def tile_kernel_index(tiles, t, size, bq, bk, chunk):
    q0 = pl.multiple_of(tiles[1 + t] * bq, bq)
    k0 = pl.multiple_of(tiles[1 + size + t] * bk, bk)
    cj, kj = q0 // chunk, k0 // chunk
    off = pl.multiple_of(q0 - cj * chunk, bq)
    ko = pl.multiple_of(k0 - kj * chunk, bk)
    return q0, k0, cj, off, kj, ko, tiles[1 + 2 * size + t]


def inside(spot, pos, start, length):
    place = (spot + (pos - start)).astype(jnp.uint32)
    return place < length.astype(jnp.uint32)


def attend_kernel(
    tiles,
    qkv,
    start,
    length,
    low,
    high,
    lse,
    keys,
    acc,
    total,
    top,
    *,
    bq,
    bk,
    seq,
    chunk,
    piece,
    unroll,
    size,
):
    n_chunks = seq // chunk
    q_most = jnp.zeros((1, chunk), F32)
    k_most = jnp.zeros((1, chunk), F32)
    for j in range(n_chunks):
        q = qkv[j, 0].astype(F32)
        k = qkv[j, 1].astype(F32)
        q_most = jnp.maximum(q_most, jnp.sum(q * q, axis=0, keepdims=True))
        k_most = jnp.maximum(k_most, jnp.sum(k * k, axis=0, keepdims=True))
        keys[j * chunk : (j + 1) * chunk, :] = k.T.astype(BF16)
    calm = jnp.max(q_most) * jnp.max(k_most) < CALM * CALM
    acc[...] = jnp.zeros_like(acc)
    total[...] = jnp.zeros_like(total)
    spot = lax.broadcasted_iota(jnp.int32, (bk, bq), 0)

    def tile(t):
        q0, k0, cj, off, kj, ko, pos = tile_kernel_index(tiles, t, size, bq, bk, chunk)
        s = dot(keys[pl.ds(k0, bk), :], qkv[cj, 0, :, pl.ds(off, bq)], 1, 0)
        ok = inside(spot, pos, start[:, pl.ds(q0, bq)], length[:, pl.ds(q0, bq)])
        return q0, kj, ko, s, ok

    @pl.when(calm)
    def _():
        top[...] = jnp.zeros_like(top)

        def step(i, _):
            group = [tile(i * unroll + u) for u in range(unroll)]
            for q0, kj, ko, s, ok in group:
                p = jnp.where(ok, jnp.exp(s), 0.0)
                total[:, pl.ds(q0, bq)] += jnp.sum(p, axis=0, keepdims=True)
                value = qkv[kj, 2, :, pl.ds(ko, bk)]
                acc[:, pl.ds(q0, bq)] += dot(value, p.astype(BF16), 1, 0)
            return 0

        lax.fori_loop(0, tiles[0], step, 0)

    @pl.when(jnp.logical_not(calm))
    def _():
        top[...] = jnp.full_like(top, NEG)

        def step(i, _):
            q0, kj, ko, s, ok = tile(i)
            s = jnp.where(ok, s, NEG)
            here = pl.ds(q0, bq)
            new = jnp.maximum(top[:, here], jnp.max(s, axis=0, keepdims=True))
            p = jnp.where(ok, jnp.exp(s - new), 0.0)
            fade = jnp.exp(top[:, here] - new)
            total[:, here] = total[:, here] * fade + jnp.sum(p, axis=0, keepdims=True)
            value = qkv[kj, 2, :, pl.ds(ko, bk)]
            acc[:, here] = acc[:, here] * fade + dot(value, p.astype(BF16), 1, 0)
            top[:, here] = new
            return 0

        lax.fori_loop(0, tiles[0] * unroll, step, 0)

    lse[...] = top[...] + jnp.log(total[...])
    for z in range(n_chunks):
        for t in range(chunk // piece):
            base = z * chunk + t * piece
            out = acc[:, base : base + piece] / total[:, base : base + piece]
            low[t * n_chunks + z] = out.astype(BF16)
            high[t * n_chunks + z] = out


def attend(qkv, doc, tiles, piece, bq, bk, unroll):
    n_chunks, _, hd, chunk = qkv.shape
    seq = n_chunks * chunk
    start, end = doc
    pieces = seq // piece
    return pl.pallas_call(
        functools.partial(
            attend_kernel,
            bq=bq,
            bk=bk,
            seq=seq,
            chunk=chunk,
            piece=piece,
            unroll=unroll,
            size=(tiles.shape[0] - 1) // 3,
        ),
        grid_spec=pltpu.PrefetchScalarGridSpec(
            num_scalar_prefetch=1,
            grid=(),
            in_specs=[VMEM] * 3,
            out_specs=[VMEM] * 3,
            scratch_shapes=[
                pltpu.VMEM((seq, hd), BF16),
                pltpu.VMEM((hd, seq), F32),
                pltpu.VMEM((1, seq), F32),
                pltpu.VMEM((1, seq), F32),
            ],
        ),
        out_shape=[
            jax.ShapeDtypeStruct((pieces, hd, piece), BF16),
            jax.ShapeDtypeStruct((pieces, hd, piece), F32),
            jax.ShapeDtypeStruct((1, seq), F32),
        ],
        compiler_params=params(40),
        cost_estimate=cost(2 * seq * seq * hd, 8 * seq * hd, seq * seq // 4),
        name="attend",
    )(tiles, qkv, start[None], (end - start)[None])


def attend_back_kernel(
    tiles,
    qkv,
    start,
    length,
    lse,
    ctx,
    d_ctx,
    out,
    keys,
    values,
    queries,
    grads,
    d_keys,
    d_values,
    d_queries,
    delta,
    d_turned,
    *,
    bq,
    bk,
    seq,
    chunk,
    piece,
    unroll,
    size,
):
    n_chunks = seq // chunk
    for j in range(n_chunks):
        sl = slice(j * chunk, (j + 1) * chunk)
        queries[sl, :] = qkv[j, 0].astype(F32).T.astype(BF16)
        keys[sl, :] = qkv[j, 1].astype(F32).T.astype(BF16)
        values[sl, :] = qkv[j, 2].astype(F32).T.astype(BF16)
    for at in range(seq // piece):
        t, z = at // n_chunks, at % n_chunks
        base = z * chunk + t * piece
        part = d_ctx[at].astype(F32)
        d_turned[:, base : base + piece] = d_ctx[at]
        grads[base : base + piece, :] = part.T.astype(BF16)
        delta[:, base : base + piece] = jnp.sum(part * ctx[at], axis=0, keepdims=True)
    d_queries[...] = jnp.zeros_like(d_queries)
    d_keys[...] = jnp.zeros_like(d_keys)
    d_values[...] = jnp.zeros_like(d_values)
    spot = lax.broadcasted_iota(jnp.int32, (bk, bq), 0)

    def tile(t):
        q0, k0, cj, off, kj, ko, pos = tile_kernel_index(tiles, t, size, bq, bk, chunk)
        s = dot(keys[pl.ds(k0, bk), :], qkv[cj, 0, :, pl.ds(off, bq)], 1, 0)
        dp = dot(values[pl.ds(k0, bk), :], d_turned[:, pl.ds(q0, bq)], 1, 0)
        ok = inside(spot, pos, start[:, pl.ds(q0, bq)], length[:, pl.ds(q0, bq)])
        return q0, k0, kj, ko, s, dp, ok

    def step(i, _):
        group = [tile(i * unroll + u) for u in range(unroll)]
        for q0, k0, kj, ko, s, dp, ok in group:
            here = pl.ds(q0, bq)
            there = pl.ds(k0, bk)
            p = jnp.where(ok, jnp.exp(s - lse[:, here]), 0.0)
            ds = (p * (dp - delta[:, here])).astype(BF16)
            d_values[there, :] += dot(p.astype(BF16), grads[here, :], 1, 0)
            d_keys[there, :] += dot(ds, queries[here, :], 1, 0)
            d_queries[:, here] += dot(qkv[kj, 1, :, pl.ds(ko, bk)], ds, 1, 0)
        return 0

    lax.fori_loop(0, tiles[0], step, 0)
    scale = HEAD_DIM ** (-0.5)
    for j in range(n_chunks):
        sl = slice(j * chunk, (j + 1) * chunk)
        out[j, 0] = (d_queries[:, sl].astype(BF16).astype(F32) * scale).astype(BF16)
        out[j, 1] = d_keys[sl, :].T.astype(BF16)
        out[j, 2] = d_values[sl, :].T.astype(BF16)


def attend_back(qkv, doc, tiles, lse, ctx, d_ctx, piece, bq, bk, unroll):
    n_chunks, _, hd, chunk = qkv.shape
    seq = n_chunks * chunk
    start, end = doc
    return pl.pallas_call(
        functools.partial(
            attend_back_kernel,
            bq=bq,
            bk=bk,
            seq=seq,
            chunk=chunk,
            piece=piece,
            unroll=unroll,
            size=(tiles.shape[0] - 1) // 3,
        ),
        grid_spec=pltpu.PrefetchScalarGridSpec(
            num_scalar_prefetch=1,
            grid=(),
            in_specs=[VMEM] * 6,
            out_specs=VMEM,
            scratch_shapes=[pltpu.VMEM((seq, hd), BF16)] * 4
            + [pltpu.VMEM((seq, hd), F32)] * 2
            + [
                pltpu.VMEM((hd, seq), F32),
                pltpu.VMEM((1, seq), F32),
                pltpu.VMEM((hd, seq), BF16),
            ],
        ),
        out_shape=jax.ShapeDtypeStruct((n_chunks, 3, hd, chunk), BF16),
        compiler_params=params(48),
        cost_estimate=cost(4 * seq * seq * hd, 16 * seq * hd, seq * seq // 4),
        name="attend_back",
    )(tiles, qkv, start[None], (end - start)[None], lse, ctx, d_ctx)


def document_bounds(seg):
    ids = jnp.arange(DOCS, dtype=jnp.int32)[:, None]
    below = jnp.sum((seg[None] < ids).astype(jnp.int32), axis=1, keepdims=True)
    upto = jnp.sum((seg[None] <= ids).astype(jnp.int32), axis=1, keepdims=True)
    mine = seg[None] == ids
    start = jnp.sum(jnp.where(mine, below, 0), axis=0)
    end = jnp.sum(jnp.where(mine, upto, 0), axis=0)
    return start, end


def tile_list(start, end, bq, bk, unroll):
    n, m = start.shape[0] // bq, start.shape[0] // bk
    low = start.reshape(n, bq)[:, 0] // bk
    high = (end.reshape(n, bq)[:, -1] + bk - 1) // bk
    count = high - low
    order = jnp.arange(n)
    upto = jnp.sum(jnp.where(order[:, None] <= order[None], count[:, None], 0), axis=0)
    total = upto[-1]
    t = jnp.arange(n * m + unroll, dtype=jnp.int32)
    mine = jnp.minimum(jnp.sum((t[:, None] >= upto[None]).astype(jnp.int32), axis=1), n - 1)
    base = jnp.sum(jnp.where(mine[:, None] == order[None], (high - upto)[None], 0), axis=1)
    real = t < total
    key = jnp.where(real, base + t, 0)
    pos = jnp.where(real, key * bk, FAR)
    steps = (total + unroll - 1) // unroll
    return jnp.concatenate([steps[None], mine, key, pos]).astype(jnp.int32)


def norm_stats(value):
    center = value - jnp.mean(value, axis=-1, keepdims=True)
    rstd = lax.rsqrt(jnp.mean(center * center, axis=-1, keepdims=True) + EPSILON)
    return center * rstd, rstd


def norm_back(xhat, rstd, d_out, gain):
    scaled = d_out * gain
    m1 = jnp.mean(scaled, axis=-1, keepdims=True)
    m2 = jnp.mean(scaled * xhat, axis=-1, keepdims=True)
    return (scaled - m1 - xhat * m2) * rstd


def column(value):
    return jnp.sum(value, axis=0, keepdims=True)


def merge_kernel(perm, cols, ctx, x, vec, *refs):
    ws = refs[:-3]
    mixed_ref, normed_ref, low_ref = refs[-3:]
    halves, deep, wide = ws[0].shape
    parts = []
    for r in range(len(ws)):
        rows = pl.ds(pl.multiple_of(perm[r] * deep, deep), deep)
        parts.append(ctx[rows, :].astype(F32).T.astype(BF16))
    for s in range(halves):
        acc = dot(parts[0], ws[0][s], 1, 0)
        for r in range(1, len(ws)):
            acc = acc + dot(parts[r], ws[r][s], 1, 0)
        sl = pl.ds(pl.multiple_of(cols[s] * wide, 128), wide)
        mixed_ref[:, sl] = x[:, sl] + acc + vec[2:3, sl]
    xhat, _ = norm_stats(mixed_ref[...])
    normed = xhat * vec[0:1, :] + vec[3:4, :]
    normed_ref[...] = normed
    low_ref[...] = normed.astype(BF16)


def merge_specs(ws, layer):
    shape = ws[0].shape
    spec = pl.BlockSpec((shape[0], None) + shape[2:], lambda *_: (0, layer, 0, 0))
    return [spec] * len(ws)


def merge_norm(ctx, ws, layer, x, vec, perm, cols):
    rows, width = x.shape
    big = jax.ShapeDtypeStruct((rows, width), F32)
    return pl.pallas_call(
        merge_kernel,
        grid_spec=pltpu.PrefetchScalarGridSpec(
            num_scalar_prefetch=2,
            grid=(1,),
            in_specs=[VMEM] * 3 + merge_specs(ws, layer),
            out_specs=[VMEM] * 3,
        ),
        out_shape=[big, big, jax.ShapeDtypeStruct((rows, width), BF16)],
        compiler_params=params(),
        cost_estimate=cost(2 * rows * width * width, 2 * width * width + 16 * rows * width),
        name="merge_norm",
    )(perm, cols, ctx, x, vec, *ws)


def add_up(refs):
    total = refs[0][...].astype(F32)
    for ref in refs[1:]:
        total = total + ref[...].astype(F32)
    return total


def row_blocks(count, rows, width):
    block = rows
    return (rows // block,), [pl.BlockSpec((block, width), lambda r: (r, 0))] * count


def all_of(shape):
    return pl.BlockSpec(shape, lambda r: (0, 0))


def norm_kernel(vec, *refs, n_in):
    summed_ref, out_ref, low_ref = refs[n_in:]
    summed = add_up(refs[:n_in]) + vec[4:5, :]
    summed_ref[...] = summed
    xhat, _ = norm_stats(summed)
    out = xhat * vec[1:2, :] + vec[5:6, :]
    out_ref[...] = out
    low_ref[...] = out.astype(BF16)


def second_norm(vec, terms):
    shape = terms[0].shape
    big = jax.ShapeDtypeStruct(shape, F32)
    grid, specs = row_blocks(len(terms) + 3, *shape)
    return pl.pallas_call(
        functools.partial(norm_kernel, n_in=len(terms)),
        grid=grid,
        in_specs=[all_of(vec.shape)] + specs[3:],
        out_specs=specs[:3],
        out_shape=[big, big, jax.ShapeDtypeStruct(shape, BF16)],
        compiler_params=params(),
        cost_estimate=cost(20 * shape[0] * shape[1], 20 * shape[0] * shape[1]),
        name="second_norm",
    )(vec, *terms)


def second_back_math(vec, summed, d_out, d_ref, low_ref, sum_ref):
    xhat, rstd = norm_stats(summed)
    d_summed = norm_back(xhat, rstd, d_out, vec[1:2, :])
    d_ref[...] = d_summed
    low_ref[...] = d_summed.astype(BF16)

    @pl.when(pl.program_id(0) == 0)
    def _():
        sum_ref[...] = jnp.zeros_like(sum_ref)

    sum_ref[0:1, :] += column(d_out * xhat)
    sum_ref[1:2, :] += column(d_out)
    sum_ref[2:3, :] += column(d_summed)
    return xhat


def last_kernel(vec, d_out_ref, *refs, n_in):
    out_ref, d_ref, low_ref, sum_ref = refs[n_in:]
    summed = add_up(refs[:n_in]) + vec[4:5, :]
    d_out = d_out_ref[...].astype(F32)
    xhat = second_back_math(vec, summed, d_out, d_ref, low_ref, sum_ref)
    out_ref[...] = (xhat * vec[1:2, :] + vec[5:6, :]).astype(BF16)


def last_norm(vec, d_out, terms):
    rows, width = terms[0].shape
    low = jax.ShapeDtypeStruct((rows, width), BF16)
    grid, specs = row_blocks(len(terms) + 4, rows, width)
    return pl.pallas_call(
        functools.partial(last_kernel, n_in=len(terms)),
        grid=grid,
        in_specs=[all_of(vec.shape)] + specs[3:],
        out_specs=specs[:3] + [all_of((3, width))],
        out_shape=[
            low,
            jax.ShapeDtypeStruct((rows, width), F32),
            low,
            jax.ShapeDtypeStruct((3, width), F32),
        ],
        compiler_params=params(),
        cost_estimate=cost(40 * rows * width, 20 * rows * width),
        name="last_norm",
    )(vec, d_out, *terms)


def second_back_kernel(vec, summed_ref, *refs, n_in):
    d_ref, low_ref, sum_ref = refs[n_in:]
    second_back_math(vec, summed_ref[...], add_up(refs[:n_in]), d_ref, low_ref, sum_ref)


def second_back(vec, summed, terms):
    rows, width = summed.shape
    grid, specs = row_blocks(len(terms) + 3, rows, width)
    return pl.pallas_call(
        functools.partial(second_back_kernel, n_in=len(terms)),
        grid=grid,
        in_specs=[all_of(vec.shape)] + specs[2:],
        out_specs=specs[:2] + [all_of((3, width))],
        out_shape=[
            jax.ShapeDtypeStruct((rows, width), F32),
            jax.ShapeDtypeStruct((rows, width), BF16),
            jax.ShapeDtypeStruct((3, width), F32),
        ],
        compiler_params=params(),
        cost_estimate=cost(40 * rows * width, 20 * rows * width),
        name="second_back",
    )(vec, summed, *terms)


def first_back_kernel(perm, cols, vec, mixed_ref, *refs, n_w, n_in):
    ws = refs[:n_w]
    d_ref, low_ref, sum_ref, ctx_ref = refs[n_w + n_in :]
    d_out = add_up(refs[n_w : n_w + n_in])
    xhat, rstd = norm_stats(mixed_ref[...])
    d_mixed = norm_back(xhat, rstd, d_out, vec[0:1, :])
    d_ref[...] = d_mixed
    low_ref[...] = d_mixed.astype(BF16)
    sum_ref[0:1, :] = column(d_out * xhat)
    sum_ref[1:2, :] = column(d_out)
    sum_ref[2:3, :] = column(d_mixed)
    halves, deep, wide = ws[0].shape
    parts = []
    for s in range(halves):
        parts.append(low_ref[:, pl.ds(pl.multiple_of(cols[s] * wide, 128), wide)])
    for r in range(n_w):
        acc = dot(ws[r][0], parts[0], 1, 1)
        for s in range(1, halves):
            acc = acc + dot(ws[r][s], parts[s], 1, 1)
        rows = pl.ds(pl.multiple_of(perm[r] * deep, deep), deep)
        ctx_ref[rows, :] = acc.astype(BF16)


def first_back(vec, mixed, ws, layer, terms, perm, cols):
    rows, width = mixed.shape
    return pl.pallas_call(
        functools.partial(first_back_kernel, n_w=len(ws), n_in=len(terms)),
        grid_spec=pltpu.PrefetchScalarGridSpec(
            num_scalar_prefetch=2,
            grid=(1,),
            in_specs=[VMEM] * 2 + merge_specs(ws, layer) + [VMEM] * len(terms),
            out_specs=[VMEM] * 4,
        ),
        out_shape=[
            jax.ShapeDtypeStruct((rows, width), F32),
            jax.ShapeDtypeStruct((rows, width), BF16),
            jax.ShapeDtypeStruct((3, width), F32),
            jax.ShapeDtypeStruct((width, rows), BF16),
        ],
        compiler_params=params(),
        cost_estimate=cost(2 * rows * width * width, 2 * width * width + 20 * rows * width),
        name="first_back",
    )(perm, cols, vec, mixed, *ws, *terms)


ERF_TOP = (
    -2.72614225801306e-10,
    2.77068142495902e-08,
    -2.10102402082508e-06,
    -5.69250639462346e-05,
    -7.34990630326855e-04,
    -2.95459980854025e-03,
    -1.60960333262415e-02,
)
ERF_BOTTOM = (
    -1.45660718464996e-05,
    -2.13374055278905e-04,
    -1.68282697438203e-03,
    -7.37332916720468e-03,
    -1.42647390514189e-02,
)


def erf(value):
    x = jnp.clip(value, -4.0, 4.0)
    sq = x * x
    top = jnp.full_like(x, ERF_TOP[0])
    for c in ERF_TOP[1:]:
        top = top * sq + c
    bottom = jnp.full_like(x, ERF_BOTTOM[0])
    for c in ERF_BOTTOM[1:]:
        bottom = bottom * sq + c
    return x * top / bottom


def up_kernel(*refs, n, fc):
    xs = refs[:n]
    up, bias, down = refs[n : n + 3]
    outs = refs[-3 - n : -3]
    cat_ref, act_ref, slope_ref = refs[-3:]
    piece = xs[0].shape[0]
    for i in range(n):
        cat_ref[i * piece : (i + 1) * piece, :] = xs[i][...]

    halves, deep, hidden = up.shape
    for f in range(0, hidden, fc):
        fs = slice(f, f + fc)
        u = dot(cat_ref[:, :deep], up[0, :, fs], 1, 0)
        for s in range(1, halves):
            u = u + dot(cat_ref[:, s * deep : (s + 1) * deep], up[s, :, fs], 1, 0)
        u = u + bias[:, fs].astype(F32)
        phi = 0.5 + 0.5 * erf(u * (0.5**0.5))
        act_ref[:, fs] = (u * phi).astype(BF16)
        slope = phi + u * (jnp.exp(-0.5 * u * u) * 0.3989422804014327)
        slope_ref[:, fs] = slope.astype(BF16)
    for s in range(halves):
        out = dot(act_ref[...], down[s], 1, 0).astype(BF16)
        for i in range(n):
            outs[i][:, s * deep : (s + 1) * deep] = out[i * piece : (i + 1) * piece]


def ff_specs(n, piece, width, hidden, base):
    whole = pl.BlockSpec((piece, width), lambda r: (0, 0))
    flat = pl.BlockSpec((n * piece, width), lambda r: (base // n, 0))
    tall = pl.BlockSpec((n * piece, hidden), lambda r: (base // n, 0))
    return whole, flat, tall


def feed_forward(xs, up, bias, down, fc, base, rows, kept):
    n = len(xs)
    piece, width = xs[0].shape
    hidden = up.shape[2]
    whole, flat, tall = ff_specs(n, piece, width, hidden, base)
    got = pl.pallas_call(
        functools.partial(up_kernel, n=n, fc=fc),
        grid=(1,),
        in_specs=[whole] * n
        + [
            pl.BlockSpec(up.shape, lambda r: (0, 0, 0)),
            pl.BlockSpec((1, hidden), lambda r: (0, 0)),
            pl.BlockSpec(down.shape, lambda r: (0, 0, 0)),
        ]
        + [pl.BlockSpec(memory_space=pl.ANY)] * len(kept),
        out_specs=[whole] * n + [flat, tall, tall],
        out_shape=[jax.ShapeDtypeStruct((piece, width), BF16)] * n
        + [jax.ShapeDtypeStruct((rows, w), BF16) for w in (width, hidden, hidden)],
        input_output_aliases={n + 3 + i: n + i for i in range(len(kept))},
        compiler_params=params(),
        cost_estimate=pl.CostEstimate(
            flops=16 * n * piece * width * hidden, bytes_accessed=1, transcendentals=0
        ),
        name="feed_forward",
    )(*xs, up, bias, down, *kept)
    return list(got[:n]), list(got[n:])


def down_kernel(*refs, n, fc):
    ds = refs[:n]
    slope_ref, up, down = refs[n : n + 3]
    outs = refs[-3 - n : -3]
    cat_ref, du_ref, sum_ref = refs[-3:]
    piece = ds[0].shape[0]
    for i in range(n):
        cat_ref[i * piece : (i + 1) * piece, :] = ds[i][...]
    halves, deep, hidden = up.shape
    for f in range(0, hidden, fc):
        fs = slice(f, f + fc)
        d = dot(cat_ref[:, :deep], down[0, fs, :], 1, 1)
        for s in range(1, halves):
            d = d + dot(cat_ref[:, s * deep : (s + 1) * deep], down[s, fs, :], 1, 1)
        du = (d * slope_ref[:, fs].astype(F32)).astype(BF16)
        du_ref[:, fs] = du
        sum_ref[:, fs] = column(du.astype(F32))
    for s in range(halves):
        out = dot(du_ref[...], up[s], 1, 1).astype(BF16)
        for i in range(n):
            outs[i][:, s * deep : (s + 1) * deep] = out[i * piece : (i + 1) * piece]


def feed_back(ds, slope, up, down, fc, base, kept, filler):
    n = len(ds)
    piece, width = ds[0].shape
    rows, hidden = slope.shape
    whole, flat, tall = ff_specs(n, piece, width, hidden, base)
    got = pl.pallas_call(
        functools.partial(down_kernel, n=n, fc=fc),
        grid=(1,),
        in_specs=[whole] * n
        + [
            tall,
            pl.BlockSpec(up.shape, lambda r: (0, 0, 0)),
            pl.BlockSpec(down.shape, lambda r: (0, 0, 0)),
        ]
        + [pl.BlockSpec(memory_space=pl.ANY)] * len(kept),
        out_specs=[whole] * n + [flat, tall, pl.BlockSpec((1, hidden), lambda r: (0, 0))],
        out_shape=[jax.ShapeDtypeStruct((piece, width), BF16)] * n
        + [jax.ShapeDtypeStruct((rows, w), BF16) for w in (width, hidden)]
        + [jax.ShapeDtypeStruct((1, hidden), F32)],
        input_output_aliases={n + 3 + i: n + i for i in range(len(kept))},
        compiler_params=params(),
        cost_estimate=pl.CostEstimate(
            flops=16 * n * piece * width * hidden if filler else 1,
            bytes_accessed=1,
            transcendentals=0,
        ),
        name="feed_back",
    )(*ds, slope, up, down, *kept)
    return list(got[:n]), list(got[n : n + 2]), got[n + 2]


def place_kernel(perm, *refs):
    out = refs[-1]
    for i, ref in enumerate(refs[:-1]):

        @pl.when(pl.program_id(0) == i)
        def _():
            out[...] = ref[...].astype(out.dtype)


def place(blocks, perm, dtype):
    piece, width = blocks[0].shape
    n = len(blocks)
    return pl.pallas_call(
        place_kernel,
        grid_spec=pltpu.PrefetchScalarGridSpec(
            num_scalar_prefetch=1,
            grid=(n,),
            in_specs=[pl.BlockSpec((piece, width), lambda r, p: (0, 0))] * n,
            out_specs=pl.BlockSpec((piece, width), lambda r, p: (p[r], 0)),
        ),
        out_shape=jax.ShapeDtypeStruct((n * piece, width), dtype),
        compiler_params=params(),
        cost_estimate=cost(n * piece * width, 6 * n * piece * width),
        name="place",
    )(perm, *blocks)


def store_kernel(*refs, n):
    for source, target in zip(refs[-2 * n : -n], refs[-n:]):
        target[...] = source[...].astype(F32)


def part_specs(joined, first, rows, width, runs, layer):
    wide = joined.shape[1]
    chunk = min(wide, width)
    own, whole, start = runs
    stride = rows if width >= wide else rows * width // wide
    block = math.gcd(math.gcd(math.gcd(stride, 256), first), math.gcd(own, start))
    down = rows // block
    steps = down * (width // chunk)

    def spot(t):
        t = jnp.minimum(t, steps - 1)
        return t % down, t // down

    def source(t):
        i, j = spot(t)
        row = j * rows + i * block
        side = 0
        if width < wide:
            row, side = i * block % stride, i * block // stride
        row = first + row
        return ((row // own * whole + start + row % own) // block, side)

    def target(t):
        i, j = spot(t)
        return (layer, i, j)

    return (
        steps,
        pl.BlockSpec((block, chunk), source),
        pl.BlockSpec((None, block, chunk), target),
    )


def store(buffers, items, layer, layers):
    n = len(items)
    parts = [part_specs(*item, layer) for item in items]
    return pl.pallas_call(
        functools.partial(store_kernel, n=n),
        grid=(max(part[0] for part in parts),),
        in_specs=[pl.BlockSpec(memory_space=pl.ANY)] * len(buffers) + [p[1] for p in parts],
        out_specs=[p[2] for p in parts],
        out_shape=[jax.ShapeDtypeStruct((layers, item[2], item[3]), F32) for item in items],
        input_output_aliases={i: i for i in range(len(buffers))},
        compiler_params=params(32),
        cost_estimate=cost(1, 1),
        name="store",
    )(*buffers, *[item[0] for item in items])


def swap(value, axis, count, bit):
    return lax.ppermute(value, axis, [(i, i ^ bit) for i in range(count)])


def spread(own, count):
    one = swap(own, "tensor", count, 1)
    two = swap(own, "tensor", count, 2)
    return [own, one, two, swap(two, "tensor", count, 1)]


def collect(blocks, count):
    three = swap(blocks[3], "tensor", count, 1)
    far = (blocks[2].astype(F32) + three.astype(F32)).astype(BF16)
    two = swap(far, "tensor", count, 2)
    return [blocks[0], swap(blocks[1], "tensor", count, 1), two]


def ordered(parts, index, bits):
    for bit in bits:
        flip = (index & bit) != 0
        parts = [jnp.where(flip, parts[i ^ bit], parts[i]) for i in range(len(parts))]
    return parts


def sum_all(value, axis, count):
    bit = 1
    while bit < count:
        value = value + swap(value, axis, count, bit)
        bit *= 2
    return value


BQ, BK, UNROLL = 256, 512, 6
BQ_BACK, BK_BACK, UNROLL_BACK = 256, 256, 6


def build(n_shard, n_context, n_tensor):
    def shards(
        hidden_in,
        segment_ids,
        cotangent,
        qkv_weight,
        merge_weight,
        up_weight,
        down_weight,
        row_gains,
        row_bias,
        head_bias,
        up_bias,
    ):
        layers = qkv_weight.shape[0]
        rows, width = hidden_in.shape
        piece = rows // n_tensor
        deep = width // n_shard
        me_s = lax.axis_index(SHARD)
        me_t = lax.axis_index("tensor")
        order = jnp.arange(n_tensor, dtype=jnp.int32)
        relative = order ^ me_t.astype(jnp.int32)
        cols_all = jnp.arange(n_shard, dtype=jnp.int32)
        cols_rel = cols_all ^ me_s.astype(jnp.int32)

        w_in = jnp.transpose(qkv_weight, (0, 2, 1, 3))
        first = [w_in[0:1]]
        for bit in range(1, n_shard):
            first.append(swap(w_in[0:1], SHARD, n_shard, bit))
        tables = jnp.concatenate([row_gains, row_bias], axis=1)
        w_in = [w_in[layer] for layer in range(layers)]
        up_weight = [up_weight[layer] for layer in range(layers)]
        down_weight = [down_weight[layer] for layer in range(layers)]
        up_weight, segment_ids = lax.optimization_barrier((up_weight, segment_ids))
        segs = [segment_ids[0]]
        for bit in range(1, n_context):
            segs.append(swap(segment_ids[0], CONTEXT, n_context, bit))
        first, segs, tables, merge_weight, up_weight, down_weight, w_in = (
            lax.optimization_barrier(
                (first, segs, tables, merge_weight, up_weight, down_weight, w_in)
            )
        )
        parts = [merge_weight]
        tabs = [tables]
        for bit in range(1, n_shard):
            parts.append(swap(merge_weight, SHARD, n_shard, bit))
            tabs.append(swap(tables, SHARD, n_shard, bit))
        bits = [1 << i for i in range(n_context.bit_length() - 1)]
        seg = jnp.concatenate(ordered(segs, lax.axis_index(CONTEXT), bits))
        doc = document_bounds(seg)
        tiles = tile_list(*doc, BQ, BK, UNROLL)
        tiles_back = tile_list(*doc, BQ_BACK, BK_BACK, UNROLL_BACK)
        w_qkv, cols = [first], [cols_rel]
        x_own = lax.dynamic_slice_in_dim(hidden_in, me_t * piece, piece, 0).astype(F32)
        d_last = lax.dynamic_slice_in_dim(cotangent, me_t * piece, piece, 0)
        xs = [hidden_in]
        x_nat = hidden_in
        saved = []
        for layer in range(layers):
            args = (w_qkv[layer], cols[layer], head_bias[layer])
            if layer == 0:
                got = list(project(xs, *args, order, piece, 0, rows, []))
            else:
                near = [x_low, swap(x_low, "tensor", n_tensor, 1)]
                far = swap(x_low, "tensor", n_tensor, 2)
                got = list(project(near, *args, relative, piece, 0, rows, []))
                far, got = lax.optimization_barrier((far, got))
                far = [far, swap(far, "tensor", n_tensor, 1)]
                got = list(project(far, *args, relative, piece, 2, rows, got))
            if layer == 0:
                got[0], up_weight, down_weight, w_in = lax.optimization_barrier(
                    (got[0], up_weight, down_weight, w_in)
                )
                pair = jnp.stack(parts)
                far = swap(pair, "tensor", n_tensor, 2)
                bits = [1 << i for i in range(n_shard.bit_length() - 1)]
                vec = jnp.concatenate(ordered(tabs, me_s, bits), axis=2).astype(F32)
                w_up, w_down = [], []
                for i in range(layers):
                    if i > 0:
                        w_qkv.append([lax.all_gather(w_in[i], SHARD, axis=0, tiled=False)])
                        cols.append(cols_all)
                    w_up.append(lax.all_gather(up_weight[i], SHARD, axis=0, tiled=False))
                    w_down.append(lax.all_gather(down_weight[i], SHARD, axis=0, tiled=False))
            else:
                x_nat = got[1]
            qkv = lax.all_to_all(got[0], CONTEXT, 0, 0, tiled=True)
            ctx_low, ctx, lse = attend(qkv, doc, tiles, piece, BQ, BK, UNROLL)
            if layer == 0:
                ctx_low, far, pair = lax.optimization_barrier((ctx_low, far, pair))
                w_merge = [pair, swap(pair, "tensor", n_tensor, 1)]
                w_merge += [far, swap(far, "tensor", n_tensor, 1)]
            mine = lax.all_to_all(ctx_low, ("tensor", CONTEXT), 0, 0, tiled=True)
            mine = mine.reshape(width, piece)
            mixed, normed, low = merge_norm(
                mine, w_merge, layer, x_own, vec[layer], relative, cols_rel
            )
            ff_args = (w_up[layer], up_bias[layer : layer + 1], w_down[layer], 512)
            far = swap(low, "tensor", n_tensor, 2)
            near = [low, swap(low, "tensor", n_tensor, 1)]
            blocks, kept = feed_forward(near, *ff_args, 0, rows, [])
            far, kept = lax.optimization_barrier((far, kept))
            far = [far, swap(far, "tensor", n_tensor, 1)]
            got, kept = feed_forward(far, *ff_args, 2, rows, kept)
            blocks += got
            x1, act, slope = kept
            terms = [normed] + collect(blocks, n_tensor)
            keep = [x_nat, qkv, ctx, lse, mine, mixed, x1, act, slope]
            if layer + 1 < layers:
                terms, w_qkv[1] = lax.optimization_barrier((terms, w_qkv[1]))
                summed, x_own, x_low = second_norm(vec[layer], terms)
                keep.append(summed)
            else:
                out_low, d_summed, d_low, sums = last_norm(vec[layer], d_last, terms)
            saved.append(keep)

        def send_parts(make):
            return [make(me_s ^ bit).astype(BF16) for bit in range(1, n_shard)]

        def exchange(parts):
            return [swap(p, SHARD, n_shard, i + 1) for i, p in enumerate(parts)]

        def settle(make, got):
            total = make(me_s)
            for part in got:
                total = total + part.astype(F32)
            return total.astype(BF16)

        def context_scatter(value):
            return lax.psum_scatter(value, CONTEXT, scatter_dimension=0, tiled=True)

        def context_gather(value):
            return lax.all_gather(value, CONTEXT, axis=0, tiled=True)

        def chunks(value, wide):
            return [value[:, i : i + wide] for i in range(0, value.shape[1], wide)]

        def join_wide(g_down, g_up):
            return jnp.concatenate(g_down + chunks(g_up, deep), axis=0)

        def join_narrow(g_qkv, g_merge):
            flat = g_qkv.reshape(-1, g_qkv.shape[2])
            if deep > flat.shape[1]:
                part = flat.shape[0] * flat.shape[1] // deep
                sides = [flat[i : i + part] for i in range(0, flat.shape[0], part)]
                flat = jnp.concatenate(sides, axis=1)
            return jnp.concatenate(chunks(flat, deep) + [g_merge], axis=0)

        tie = lax.optimization_barrier
        grads = [None] * layers
        rowsums, sides = [None] * layers, [None] * layers
        terms = None
        hidden_out = None
        deep_t = width // n_tensor
        late, wide, narrow = (), (), ()
        for layer in reversed(range(layers)):
            last = layer + 1 == layers
            x_nat, qkv, ctx, lse, mine, mixed, x1, act, slope = saved[layer][:9]
            if not last:
                d_summed, d_low, sums = second_back(vec[layer], saved[layer][9], terms)
            ff_args = (slope, w_up[layer], w_down[layer], 512)
            far = swap(d_low, "tensor", n_tensor, 2)
            near = [d_low, swap(d_low, "tensor", n_tensor, 1)]
            if not last:
                near, wide = tie((near, jnp.concatenate(wide, axis=0)))
                wide = context_gather(wide)
            blocks, kept, g_hidden = feed_back(near, *ff_args, 0, [], last)
            far, kept = tie((far, kept))
            far = [far, swap(far, "tensor", n_tensor, 1)]
            got, kept, part = feed_back(far, *ff_args, 2, kept, last)
            blocks += got
            blocks, late = tie((blocks, late))
            g_hidden = g_hidden + part
            dy, du = kept

            def down_part(i, act=act, dy=dy):
                return dot(act, lax.dynamic_slice_in_dim(dy, i * deep, deep, 1), 0, 0)

            def up_part(i, x1=x1, du=du):
                return dot(lax.dynamic_slice_in_dim(x1, i * deep, deep, 1), du, 0, 0)

            terms = [d_summed] + collect(blocks, n_tensor)
            down_send, up_send = send_parts(down_part), send_parts(up_part)
            terms, down_send, up_send, wide = tie((terms, down_send, up_send, wide))
            down_got, up_got = exchange(down_send), exchange(up_send)
            d_mixed, d_low, sums_one, d_mine = first_back(
                vec[layer], mixed, w_merge, layer, terms, relative, cols_rel
            )
            if not last:
                narrow = join_narrow(settle(makers[0], late[0]), settle(makers[1], late[1]))
                narrow = context_scatter(narrow)
            pieces = d_mine.reshape(n_tensor * n_context, HEAD_DIM, piece)
            d_ctx = lax.all_to_all(pieces, ("tensor", CONTEXT), 0, 0, tiled=True)
            g_blocks = []
            for r in range(n_tensor):
                part = lax.dynamic_slice_in_dim(mine, relative[r] * deep_t, deep_t, 0)
                g_blocks.append(dot(part, d_low, 1, 0).astype(BF16))
            g_down = settle(down_part, down_got) if last else ()
            d_ctx, g_blocks, narrow, down_got, g_down, out_low = tie(
                (d_ctx, g_blocks, narrow, down_got, g_down, out_low)
            )
            if last:
                out_low = [out_low, swap(out_low, "tensor", n_tensor, 2)]
                g_down = context_scatter(g_down)
            else:
                narrow = context_gather(narrow)
            d_heads = attend_back(
                qkv, doc, tiles_back, lse, ctx, d_ctx, piece, BQ_BACK, BK_BACK, UNROLL_BACK
            )
            d_heads, down_got, up_got, g_blocks, g_down, out_low, narrow = tie(
                (d_heads, down_got, up_got, g_blocks, g_down, out_low, narrow)
            )
            d_heads = lax.all_to_all(d_heads, CONTEXT, 0, 0, tiled=True)
            g_terms = collect(g_blocks, n_tensor)
            g_merge = sum(term.astype(F32) for term in g_terms).astype(BF16)
            g_up = settle(up_part, up_got)
            if last:
                new_wide = join_wide([], g_up)
            else:
                new_wide = join_wide([settle(down_part, down_got)], g_up)
            if last:
                near = [swap(v, "tensor", n_tensor, 1) for v in out_low]
                out_low = [out_low[0], near[0], out_low[1], near[1]]
                hidden_out = place(out_low, relative, BF16)
            d_heads, new_wide, g_merge, narrow, hidden_out = tie(
                (d_heads, new_wide, g_merge, narrow, hidden_out)
            )
            new_wide = context_scatter(new_wide)
            if last:
                new_wide = [g_down, new_wide]
            got = project_back(d_heads, w_qkv[layer], cols[layer], relative, piece, width)
            d_x, d_proj, g_heads = got[:n_tensor], got[n_tensor], got[n_tensor + 1]

            def merge_part(i, g_merge=g_merge):
                return lax.dynamic_slice_in_dim(g_merge, i * deep, deep, 1).astype(F32)

            def qkv_part(i, x_nat=x_nat, d_proj=d_proj):
                d = lax.dynamic_slice_in_dim(x_nat, i * deep, deep, 1)
                return jnp.einsum("rd,crj->cdj", d, d_proj, preferred_element_type=F32)

            qkv_send, merge_send = send_parts(qkv_part), send_parts(merge_part)
            terms = [d_mixed] + collect(d_x, n_tensor)
            if layer > 0:
                terms, qkv_send, merge_send = tie((terms, qkv_send, merge_send))

            if not last:
                grads[layer + 1] = (wide, narrow)
            late = (exchange(qkv_send), exchange(merge_send))
            makers = (qkv_part, merge_part)
            wide, narrow = new_wide, ()
            rowsums[layer] = jnp.concatenate([sums_one, sums], axis=0)
            sides[layer] = jnp.concatenate([g_heads.reshape(-1), g_hidden.reshape(-1)])
        total = terms[0]
        for term in terms[1:]:
            total = total + term.astype(F32)
        narrow = join_narrow(settle(makers[0], late[0]), settle(makers[1], late[1]))
        total = total.astype(BF16)
        wide, narrow = tie((wide, narrow))
        blocks = spread(total, n_tensor)
        table = sum_all(jnp.concatenate(rowsums, axis=0), "tensor", n_tensor)
        side = jnp.concatenate(sides).reshape(-1, width)
        packed = jnp.concatenate([table, side], axis=0)
        packed = sum_all(packed, SHARD, n_shard)
        packed = sum_all(packed, CONTEXT, n_context)
        narrow = context_scatter(narrow)
        blocks, packed = tie((blocks, packed))
        grads[0] = context_gather(jnp.concatenate([wide, narrow], axis=0))
        input_grad = place(blocks, relative, F32)
        hw = width // n_tensor
        hidden = up_bias.shape[1]
        stored = []
        n_qkv = 3 * deep * hw // deep
        n_narrow = n_qkv + hw
        run_w, run_n = 2 * hidden // n_context, n_narrow // n_context
        for layer in reversed(range(layers)):
            if layer == 0:
                wide = narrow = grads[0]
                runs_d = runs_u = (run_w, run_w + run_n, 0)
                runs_n = (run_n, run_w + run_n, run_w)
                second = hidden
            else:
                wide, narrow = grads[layer]
                runs_d = runs_u = runs_n = (1 << 20, 0, 0)
                second = hidden
                if layer + 1 == layers:
                    run = hidden // n_context
                    runs_d, runs_u, second = (run, 2 * run, 0), (run, 2 * run, run), 0
                runs_n = (n_narrow, 0, 0)
            items = [
                (wide, 0, hidden, deep, runs_d),
                (wide, second, deep, hidden, runs_u),
                (narrow, 0, 3 * deep, hw, runs_n),
                (narrow, n_qkv, hw, deep, runs_n),
            ]
            stored = store(stored, items, layer, layers)
        g_down, g_up, g_qkv, g_merge = stored
        g_qkv = g_qkv.reshape(layers, 3, deep, -1)

        table = packed[: layers * 6].reshape(layers, 6, width)
        table = lax.dynamic_slice_in_dim(table, me_s * deep, deep, 2)
        side = packed[layers * 6 :].reshape(layers, -1)
        head_count = 2 * head_bias.shape[2]
        grad_gains = table[:, 0::3]
        grad_shifts = table[:, jnp.array([2, 1, 5, 4])]
        grad_heads = side[:, :head_count].reshape(head_bias.shape)
        grad_hidden = side[:, head_count:]
        return (
            hidden_out,
            input_grad,
            jnp.transpose(g_qkv, (0, 2, 1, 3)),
            g_merge,
            g_up,
            g_down,
            grad_gains,
            grad_shifts,
            grad_heads,
            grad_hidden,
        )

    return shards


def solution(mesh):
    tokens = (SHARD, CONTEXT)
    weights = (
        P(None, SHARD, None, "tensor"),
        P(None, "tensor", SHARD),
        P(None, SHARD, "tensor"),
        P(None, "tensor", SHARD),
        P(None, None, SHARD),
        P(None, None, SHARD),
        P(None, None, "tensor"),
        P(None, "tensor"),
    )
    return jax.shard_map(
        build(mesh.shape[SHARD], mesh.shape[CONTEXT], mesh.shape["tensor"]),
        mesh=mesh,
        in_specs=(P(tokens, None), P(*tokens), P(tokens, None)) + weights,
        out_specs=(P(tokens, None), P(tokens, None)) + weights,
        check_vma=False,
    )
```
